128 devices in a mesh: req: 8 (over z, core), wide: 16 (over x, y).
Axes of the slice: x: 4, y: 4, z: 4, core: 2. Of those that a mesh axis runs over, the one named last changes fastest.
Arguments:
- queries: bfloat16 [16384, 3072], P(('req', 'wide'))
- suffix_latent: bfloat16 [16384, 512], P(('req', 'wide')), may hold values from -6 to 6
- suffix_rope: bfloat16 [64, 16384], P(None, ('req', 'wide')), may hold values from -6 to 6
- residual: bfloat16 [16384, 2048], P(('req', 'wide')), may hold values from -3 to 3
- prefix_latent: bfloat16 [8, 2, 2048, 512], P('req', None, 'wide'), may hold values from -6 to 6
- prefix_rope: bfloat16 [8, 2, 64, 2048], P('req', None, None, 'wide')
- suffix_lengths: int32 [128, 4], P(('req', 'wide')), may hold values from 1 to 64, 128 in all within a row
- prefix_ids: int32 [128, 4], P(('req', 'wide')), may hold values from 0 to 1
- w_ukv: bfloat16 [512, 4096], replicated, may hold values from -0.25 to 0.25
- w_out: bfloat16 [2048, 2048], replicated, may hold values from -0.5 to 0.5
- norm_gain: bfloat16 [2048], replicated, may hold values from 0.099609375 to 1.8984375
- expert_ids: int32 [16384, 6], P(('req', 'wide')), may hold values from 0 to 63, all different within a row; in each aligned block of 128 rows (0 to 127, 128 to 255, ...) at most 13 rows name the same one
- gate_values: float32 [16384, 6], P(('req', 'wide')), may hold values from 0.05 to 0.45
- expert_gate_up: bfloat16 [128, 2048, 1408], P(('req', 'wide')), may hold values from -0.125 to 0.125
- expert_down: bfloat16 [128, 704, 2048], P(('req', 'wide')), may hold values from -0.15625 to 0.15625
Outputs:
- layer_out: bfloat16 [16384, 2048], P(('req', 'wide'))
The draws below stay inside these ranges and needn't reach their ends.
Inputs may be any that keep to these rules, and one draw needn't show every extreme that they name: `suffix_lengths`: row b gives, in order, the lengths of the 4 requests that make up tokens b * 128 to (b + 1) * 128 - 1; each row sums to 128 and its largest entry is 64. `expert_ids`: a token's 6 experts differ; among the 128 tokens of one device no expert is named more than 13 times, and in some device one expert is named exactly 13 times.
All inputs are finite; a program needn't handle non-finite values.
Results may differ from the reference program's by a relative error of at most 0.012.
Values may be sent and summed in bfloat16 or wider, within the bound.
No kernel may reach another device: no remote copies, remote signals or barrier semaphores. Data moves between devices by JAX's collectives and lax.ppermute only.
A program may use at most 192 MiB of HBM per device.

```python
import math
import jax
import jax.numpy as jnp
import numpy as np
from jax import lax

D = 2048
HEADS = 16
NOPE = 128
ROPE = 64
LAT = 512
FF_E = 1408
TOP = 6
PREF = 2
REQ_DEV = 4
TOK_DEV = 128
PLEN_DEV = 128
GROUPS = 8
EXPERTS = 64
TOKENS = 16384
PLEN = 2048
CAP = 13
N_WIDE = 16
DEVICES = 128


def draw_queries(key, part):
    row_width = HEADS * (NOPE + ROPE)
    return (2.0 * jax.random.truncated_normal(jax.random.fold_in(key, 1), -6.0, 6.0, (TOKENS, row_width), jnp.float32)).astype(jnp.bfloat16)


def draw_prefix_rope(key, part):
    array_shape = (GROUPS, PREF, ROPE, PLEN)
    return jax.random.truncated_normal(jax.random.fold_in(key, 2), -6.0, 6.0, array_shape, jnp.float32).astype(jnp.bfloat16)


def touch_ends(result, stream_key, least, high):
    place = [jax.random.randint(jax.random.fold_in(stream_key, axis), (), 0, length) for axis, length in enumerate(result.shape)]
    main_axis = result.shape.index(max(result.shape))
    neighbour = place[:main_axis] + [(place[main_axis] + 1) % result.shape[main_axis]] + place[main_axis + 1:]
    return result.at[tuple(place)].set(least).at[tuple(neighbour)].set(high)


def level_of(own_key, extent, pieces, least, high):
    def one(dim, shards_of):
        draws = jax.random.uniform(jax.random.fold_in(jax.random.fold_in(own_key, 6), dim), (shards_of,), jnp.float32, least / len(pieces), high / len(pieces))
        return jnp.repeat(jnp.exp(draws), extent[dim] // shards_of).reshape((-1,) + (1,) * (len(extent) - dim - 1))

    factor_of = one(*pieces[0])
    for cut in pieces[1:]:
        factor_of = factor_of * one(*cut)
    return factor_of


def length_profile(number_of, total, most, slope):
    loads = [(1 << 20) // math.isqrt(standing ** slope) + 1 for standing in range(2, number_of + 1)]
    rest, given = total - most - (number_of - 1), [1] * (number_of - 1)
    while rest > 0:
        free = [i for i in range(number_of - 1) if given[i] < most]
        pool, budget = sum([loads[i] for i in free]), rest
        for i in free:
            extra = min(most - given[i], max(1, budget * loads[i] // pool), rest)
            given[i] = given[i] + extra
            rest = rest - extra
    return np.array([most] + given)


def ragged(rng, number_of, total, reach, lean):
    if number_of == 2:
        one = jax.random.randint(rng, (), max(1, total - reach), min(reach, total - 1) + 1)
        return jnp.stack([one, total - one])
    tallies = jnp.asarray(length_profile(number_of, total, reach, lean), jnp.int32)
    couples = (number_of - 1) // 2
    giver, sink = tallies[1:1 + 2 * couples:2], tallies[2:2 + 2 * couples:2]
    room = jnp.minimum(giver - 1, reach - sink)
    moved = jax.random.randint(jax.random.fold_in(rng, 1), (couples,), 0, 1 << 20) % (room + 1)
    tallies = tallies.at[1:1 + 2 * couples:2].set(giver - moved).at[2:2 + 2 * couples:2].set(sink + moved)
    return tallies[jax.random.permutation(jax.random.fold_in(rng, 2), number_of)]


def assign_block(key, own, number, rows, count, top, bound, lean):
    order = jax.random.permutation(key, count)
    packed, common = shares(count, rows * top, bound, lean, True), shares(count, rows * top, bound, lean, False)
    places = jnp.arange(count)

    def named(sizes, rotation):
        used = int((sizes > 0).sum())
        fixed = max(1, used // 4)
        shifted = fixed + (places - fixed + rotation * (used - fixed)) % max(1, count - fixed)
        return jnp.zeros((count,), jnp.int32).at[order[jnp.where(places < fixed, places, shifted)]].set(jnp.asarray(sizes, jnp.int32))

    sizes = jnp.where(number % 4 == 0, named(packed, number // 4), named(common, number - number // 4 - 1))
    mixed = jax.random.permutation(jax.random.fold_in(own, 3), count)
    donor, receiver = mixed[0:count // 2 * 2:2], mixed[1:count // 2 * 2:2]
    margin = jnp.minimum(sizes[donor] - 1, bound - sizes[receiver]) // 2
    margin = jnp.where((donor == order[0]) | (receiver == order[0]) | (sizes[receiver] == 0), 0, jnp.maximum(margin, 0))
    shifted = jax.random.randint(jax.random.fold_in(own, 4), (count // 2,), 0, 1 << 20) % (margin + 1)
    sizes = sizes.at[donor].add(-shifted).at[receiver].add(shifted)
    members = jnp.searchsorted(jnp.cumsum(sizes), jnp.arange(rows * top), side="right").astype(jnp.int32)
    grid = members.reshape(top, rows).T
    grid = grid[jax.random.permutation(jax.random.fold_in(own, 1), rows)]
    rotation = jax.random.randint(jax.random.fold_in(own, 2), (rows, 1), 0, top)
    return jnp.take_along_axis(grid, (jnp.arange(top)[None, :] + rotation) % top, axis=1)


def shares(number_of, total, limit, slope, full):
    weights = [(1 << 20) // math.isqrt(grade ** slope) + 1 for grade in range(1, number_of + 1)]
    largest = limit if full else min(limit, max(-(-total // number_of), total * weights[0] // sum(weights)))
    least = 1 if total - largest >= number_of - 1 else 0
    given, rest = [largest] + [least] * (number_of - 1), total - largest - least * (number_of - 1)
    while rest > 0:
        candidates = [i for i in range(1, number_of) if given[i] < largest] or [i for i in range(1, number_of) if given[i] < limit]
        whole, budget = sum([weights[i] for i in candidates]), rest
        for i in candidates:
            extra = min(limit - given[i], max(1, budget * weights[i] // whole), rest)
            given[i] = given[i] + extra
            rest = rest - extra
    return np.array(given)


def bell_draw(stream_key, dims, scale, reach, pieces=(), kind=jnp.bfloat16):
    entries = scale * jax.random.normal(stream_key, dims, jnp.float32)
    if pieces:
        entries = entries * level_of(stream_key, dims, pieces, -0.22, 0.18)
    return jnp.clip(entries, -reach, reach).astype(kind)


def setup_inputs(seed: int = 0) -> dict:
    splits = jax.random.split(jax.random.key(seed), 16)
    queries = draw_queries(jax.random.fold_in(splits[15], 71), 0)
    suffix_latent = bell_draw(splits[1], (TOKENS, LAT), 1.0, 6.0, ((0, 128),))
    suffix_rope = bell_draw(splits[2], (ROPE, TOKENS), 1.0, 6.0, ((1, 128),))
    residual = bell_draw(splits[3], (TOKENS, D), 0.5, 3.0, ((0, 128),))
    prefix_latent = bell_draw(splits[4], (GROUPS, PREF, PLEN, LAT), 1.0, 6.0, ((0, 8), (2, 16)))
    prefix_rope = draw_prefix_rope(jax.random.fold_in(splits[15], 71), 0)
    suffix_lengths = jax.vmap(lambda own: ragged(own, REQ_DEV, TOK_DEV, TOK_DEV // 2, 2))(jax.random.split(splits[6], DEVICES)).reshape((DEVICES, REQ_DEV)).astype(jnp.int32)
    prefix_ids = touch_ends(jax.random.randint(splits[7], (DEVICES, REQ_DEV), 0, PREF), jax.random.fold_in(splits[7], 1), 0, PREF - 1).astype(jnp.int32)
    w_ukv = bell_draw(splits[8], (LAT, HEADS * 2 * NOPE), LAT ** -0.5, 0.25)
    w_out = bell_draw(splits[9], (HEADS * NOPE, D), (HEADS * NOPE // 16) ** -0.5, 0.5)
    norm_gain = jnp.clip(1.0 + 0.18 * jax.random.normal(splits[10], (D,), jnp.float32), 0.099609375, 1.8984375).astype(jnp.bfloat16)
    expert_ids_keys = jax.random.split(jax.random.fold_in(splits[11], 1), TOKENS // TOK_DEV)
    expert_ids_turns = jax.random.permutation(jax.random.fold_in(splits[11], 3), TOKENS // TOK_DEV)
    expert_ids = jax.vmap(lambda own, number: assign_block(jax.random.fold_in(splits[11], 2), own, number, TOK_DEV, EXPERTS, TOP, CAP, 1))(expert_ids_keys, expert_ids_turns).reshape((TOKENS, TOP))
    gate_values = jnp.clip(0.05 + 0.39999999 * jax.random.uniform(splits[12], (TOKENS, TOP), jnp.float32) ** level_of(splits[12], (TOKENS, TOP), ((0, 128),), -0.2, 0.2), 0.05, 0.45)
    expert_gate_up = bell_draw(splits[13], (2 * EXPERTS, D, FF_E), D ** -0.5, 0.125, ((0, 128),))
    expert_down = bell_draw(splits[14], (2 * EXPERTS, FF_E // 2, D), FF_E ** -0.5, 0.15625, ((0, 128),))
    return dict(queries=queries, suffix_latent=suffix_latent, suffix_rope=suffix_rope, residual=residual, prefix_latent=prefix_latent, prefix_rope=prefix_rope, suffix_lengths=suffix_lengths, prefix_ids=prefix_ids, w_ukv=w_ukv, w_out=w_out, norm_gain=norm_gain, expert_ids=expert_ids, gate_values=gate_values, expert_gate_up=expert_gate_up, expert_down=expert_down)


epsilon = 1e-06

def round_trip(values):
    return lax.optimization_barrier(values.astype(jnp.bfloat16)).astype(jnp.float32)

def request_tables(lengths, request_ids):
    request_end = jnp.cumsum(lengths).astype(jnp.int32)
    positions = jnp.arange(TOK_DEV, dtype=jnp.int32)
    segment = lax.optimization_barrier(jnp.sum((positions[:, None] >= request_end[None, :]).astype(jnp.int32), axis=1)).astype(jnp.int32)
    matches = segment[:, None] == jnp.arange(REQ_DEV, dtype=jnp.int32)[None, :]
    prefix = lax.optimization_barrier(jnp.sum(jnp.where(matches, request_ids[None, :], 0), axis=1)).astype(jnp.int32)
    return (segment, prefix)

def project_latent(latent, w_ukv):
    row_count = latent.shape[0]
    joined = jnp.dot(latent, w_ukv, preferred_element_type=jnp.float32).astype(jnp.bfloat16)
    joined = joined.reshape(row_count, HEADS, 2 * NOPE)
    return (joined[:, :, :NOPE], joined[:, :, NOPE:])

def reference(queries, suffix_latent, suffix_rope, residual, prefix_latent, prefix_rope, suffix_lengths, prefix_ids, w_ukv, w_out, norm_gain, expert_ids, gate_values, expert_gate_up, expert_down):
    scaling = 1.0 / (NOPE + ROPE) ** 0.5
    highest = lax.Precision.HIGHEST
    query_all = queries.reshape(GROUPS, N_WIDE, TOK_DEV, HEADS * (NOPE + ROPE))
    latent_all = suffix_latent.reshape(GROUPS, N_WIDE, TOK_DEV, LAT)
    turn_all = suffix_rope.reshape(ROPE, GROUPS, N_WIDE, TOK_DEV).transpose(1, 2, 0, 3)
    residual_all = residual.reshape(GROUPS, N_WIDE, TOK_DEV, D)
    length_all = suffix_lengths.reshape(GROUPS, N_WIDE, REQ_DEV)
    ident_all = prefix_ids.reshape(GROUPS, N_WIDE, REQ_DEV)
    out_heads = w_out.reshape(HEADS, NOPE, D).astype(jnp.float32)
    gain_f32 = norm_gain.astype(jnp.float32)

    def one_group(group_operands):
        query_g, latent_g, turn_g, residual_g, length_g, ident_g, cached_latent, cached_turn = group_operands
        prefix_keys, prefix_values = project_latent(cached_latent.reshape(PREF * PLEN, LAT), w_ukv)
        prefix_keys = prefix_keys.astype(jnp.float32).reshape(PREF, PLEN, HEADS, NOPE)
        prefix_values = prefix_values.astype(jnp.float32).reshape(PREF, N_WIDE, PLEN_DEV, HEADS, NOPE)
        prefix_turn = cached_turn.astype(jnp.float32)

        def one_block(block_operands):
            query_rows, latent_rows, suffix_turn, residual_rows, lengths, request_ids = block_operands
            segment, prefix = request_tables(lengths, request_ids)
            query_f32 = query_rows.astype(jnp.float32)
            query_nope = query_f32[:, :HEADS * NOPE].reshape(TOK_DEV, HEADS, NOPE)
            query_rope = query_f32[:, HEADS * NOPE:].reshape(TOK_DEV, HEADS, ROPE)
            scores = jnp.einsum('thn,pkhn->thpk', query_nope, prefix_keys, precision=highest)
            scores = scores + jnp.einsum('thr,prk->thpk', query_rope, prefix_turn, precision=highest)
            scores = (scores * scaling).reshape(TOK_DEV, HEADS, PREF, N_WIDE, PLEN_DEV)
            own_rows = (prefix[:, None] == jnp.arange(PREF, dtype=jnp.int32)[None, :])[:, None, :, None, None]
            scores = jnp.where(own_rows, scores, -jnp.inf)
            block_max = round_trip(lax.optimization_barrier(jnp.max(scores, axis=(2, 4))))
            block_weight = jnp.where(own_rows, jnp.exp(scores - block_max[:, :, None, :, None]), 0.0)
            block_sum = round_trip(lax.optimization_barrier(jnp.sum(block_weight, axis=(2, 4))))
            block_out = round_trip(jnp.einsum('thpwk,pwkhn->thwn', round_trip(block_weight), prefix_values, precision=highest))
            suffix_keys, suffix_values = project_latent(latent_rows, w_ukv)
            local = jnp.einsum('thn,khn->thk', query_nope, suffix_keys.astype(jnp.float32), precision=highest)
            local = local + jnp.einsum('thr,rk->thk', query_rope, suffix_turn.astype(jnp.float32), precision=highest)
            local = local * scaling
            positions = jnp.arange(TOK_DEV, dtype=jnp.int32)
            allowed = (segment[:, None] == segment[None, :]) & (positions[None, :] <= positions[:, None])
            local = jnp.where(allowed[:, None, :], local, -jnp.inf)
            local_max = lax.optimization_barrier(jnp.max(local, axis=2))
            local_weight = jnp.where(allowed[:, None, :], jnp.exp(local - local_max[:, :, None]), 0.0)
            local_sum = lax.optimization_barrier(jnp.sum(local_weight, axis=2))
            local_out = jnp.einsum('thk,khn->thn', round_trip(local_weight), suffix_values.astype(jnp.float32), precision=highest)
            largest = jnp.maximum(local_max, lax.optimization_barrier(jnp.max(block_max, axis=2)))
            far_weight = jnp.exp(block_max - largest[:, :, None])
            near_weight = jnp.exp(local_max - largest)
            numerator = near_weight[:, :, None] * local_out + lax.optimization_barrier(jnp.sum(far_weight[:, :, :, None] * block_out, axis=2))
            denominator = near_weight * local_sum + lax.optimization_barrier(jnp.sum(far_weight * block_sum, axis=2))
            head_out = round_trip(numerator / denominator[:, :, None])
            attention = jnp.einsum('thn,hnd->td', head_out, out_heads, precision=highest)
            hidden = lax.optimization_barrier((residual_rows.astype(jnp.float32) + attention).astype(jnp.bfloat16))
            hidden_f32 = hidden.astype(jnp.float32)
            inverse = lax.rsqrt(lax.optimization_barrier(jnp.mean(hidden_f32 * hidden_f32, axis=1, keepdims=True)) + epsilon)
            normed = (hidden_f32 * inverse * gain_f32[None, :]).astype(jnp.bfloat16)
            return (hidden, normed)
        return lax.map(one_block, (query_g, latent_g, turn_g, residual_g, length_g, ident_g))
    hidden, normed = lax.map(one_group, (query_all, latent_all, turn_all, residual_all, length_all, ident_all, prefix_latent, prefix_rope))
    hidden = hidden.reshape(TOKENS, D)
    normed = normed.reshape(DEVICES, TOK_DEV, D)
    ids_dev = expert_ids.reshape(DEVICES, TOK_DEV, TOP)
    gates_dev = gate_values.reshape(DEVICES, TOK_DEV, TOP).astype(jnp.float32)
    device_rows = jnp.arange(DEVICES, dtype=jnp.int32)[:, None]

    def one_expert(running, expert):
        named = ids_dev == expert
        chosen = jnp.any(named, axis=2)
        weight = lax.optimization_barrier(jnp.sum(jnp.where(named, gates_dev, 0.0), axis=2))
        ranking = jnp.argsort(jnp.where(chosen, 0, 1).astype(jnp.int32), axis=1, stable=True)[:, :CAP].astype(jnp.int32)
        gathered = jnp.take_along_axis(normed, ranking[:, :, None], axis=1).reshape(DEVICES * CAP, D)
        picked = jnp.take_along_axis(weight, ranking, axis=1)
        output = jnp.zeros((DEVICES * CAP, D), jnp.float32)
        for half_index in range(2):
            gate_up = jnp.dot(gathered, expert_gate_up[2 * expert + half_index], preferred_element_type=jnp.float32)
            activated = (jax.nn.silu(gate_up[:, :FF_E // 2]) * gate_up[:, FF_E // 2:]).astype(jnp.bfloat16)
            output = output + round_trip(jnp.dot(activated, expert_down[2 * expert + half_index], preferred_element_type=jnp.float32))
        contribution = output.reshape(DEVICES, CAP, D) * picked[:, :, None]
        running = running.at[device_rows, ranking].add(contribution)
        return (running, None)
    mixture, unused = lax.scan(one_expert, jnp.zeros((DEVICES, TOK_DEV, D), jnp.float32), jnp.arange(EXPERTS, dtype=jnp.int32))
    return (hidden.astype(jnp.float32) + mixture.reshape(TOKENS, D)).astype(jnp.bfloat16)
```

```python
import jax
import jax.numpy as jnp
from jax import lax
from jax.experimental import pallas as pl
from jax.experimental.pallas import tpu as pltpu
from jax.sharding import PartitionSpec as P

D = 2048
HEADS = 16
NOPE = 128
ROPE = 64
LAT = 512
TOP = 6
PREF = 2
EXPERTS = 64
TOK = 128
REQS = 4
TILE = 16
SLOTS = 16
BLK = 144
EPS = 1e-06
SCALE = 1.0 / (NOPE + ROPE) ** 0.5
LOG2E = 1.4426950408889634
NEG = -1e30
bf16 = jnp.bfloat16
f32 = jnp.float32


def request_scalars(sc_ref):
    lens = [sc_ref[r] for r in range(REQS)]
    own = [sc_ref[REQS + r] for r in range(REQS)]
    starts, total = [], 0
    for r in range(REQS):
        starts.append(total)
        total = total + lens[r]
    zero_count = sum(jnp.where(own[r] == 0, lens[r], 0) for r in range(REQS))
    bases, next0, next1 = [], 0, zero_count
    for r in range(REQS):
        is0 = own[r] == 0
        bases.append(jnp.where(is0, next0, next1))
        next0 = next0 + jnp.where(is0, lens[r], 0)
        next1 = next1 + jnp.where(is0, 0, lens[r])
    return lens, starts, bases, zero_count


def place_of(tokens, starts, bases):
    place = tokens - starts[0] + bases[0]
    for r in range(1, REQS):
        place = jnp.where(tokens >= starts[r], tokens - starts[r] + bases[r], place)
    return place


def sort_matrix(sc_ref, transposed):
    lens, starts, bases, _ = request_scalars(sc_ref)
    token_dim = 0 if transposed else 1
    tokens = lax.broadcasted_iota(jnp.int32, (TOK, TOK), token_dim)
    slots = lax.broadcasted_iota(jnp.int32, (TOK, TOK), 1 - token_dim)
    return jnp.where(place_of(tokens, starts, bases) == slots, 1.0, 0.0).astype(bf16)


def mm(a, b):
    return jnp.dot(a, b, preferred_element_type=f32)


def mm_nt(a, b):
    return lax.dot_general(a, b, (((1,), (1,)), ((), ())), preferred_element_type=f32)


def mm_tn(a, b):
    return lax.dot_general(a, b, (((0,), (0,)), ((), ())), preferred_element_type=f32)


HG = 4


def query_kernel(sc_ref, q_ref, qr_ref, w_ref, qa_ref, qo_ref):
    order = sort_matrix(sc_ref, False)
    nope = mm(order, q_ref[...]).astype(bf16)
    rope = mm(order, qr_ref[...]).astype(bf16)
    for h in range(HG):
        keys = w_ref[:, h * 256 : h * 256 + 128]
        qa_ref[h] = mm_nt(nope[:, h * 128 : (h + 1) * 128], keys).astype(bf16)
        qo_ref[h] = rope[:, h * ROPE : (h + 1) * ROPE]


def prepare_queries(scalars, queries, w_ukv):
    return pl.pallas_call(
        query_kernel,
        out_shape=(
            jax.ShapeDtypeStruct((HEADS, TOK, LAT), bf16),
            jax.ShapeDtypeStruct((HEADS, TOK, ROPE), bf16),
        ),
        grid_spec=pltpu.PrefetchScalarGridSpec(
            num_scalar_prefetch=1,
            grid=(HEADS // HG,),
            in_specs=[
                pl.BlockSpec((TOK, HG * NOPE), lambda i, s: (0, i)),
                pl.BlockSpec((TOK, HG * ROPE), lambda i, s: (0, HEADS * NOPE // (HG * ROPE) + i)),
                pl.BlockSpec((LAT, HG * 2 * NOPE), lambda i, s: (0, i)),
            ],
            out_specs=[
                pl.BlockSpec((HG, TOK, LAT), lambda i, s: (i, 0, 0)),
                pl.BlockSpec((HG, TOK, ROPE), lambda i, s: (i, 0, 0)),
            ],
        ),
        name="query_prep",
    )(scalars, queries, queries, w_ukv)


ROWS = HEADS * TILE


def block_views(refs):
    views = []
    for ref in refs:
        for b in range(ref.shape[0] // BLK):
            views.append((ref, b * BLK))
    return views


def attention_kernel(n_pieces, sc_ref, qa_ref, qr_ref, ll_ref, lr_ref, *rest):
    pieces = (rest[:n_pieces], rest[n_pieces : 2 * n_pieces])
    o_ref, s_scr, m_scr, l_scr, acc_scr = rest[2 * n_pieces :]
    lens, starts, bases, zero_count = request_scalars(sc_ref)
    first = pl.program_id(0) * TILE
    c = SCALE * LOG2E
    q = qa_ref[...].reshape(ROWS, LAT)
    qr = qr_ref[...].reshape(ROWS, ROPE)

    places = first + lax.broadcasted_iota(jnp.int32, (TILE, TOK), 0)
    keys_at = lax.broadcasted_iota(jnp.int32, (TILE, TOK), 1)
    bias = jnp.full((TILE, TOK), NEG, f32)
    for r in range(REQS):
        mine = (places >= bases[r]) & (places < bases[r] + lens[r])
        tok = places - bases[r] + starts[r]
        ok = mine & (keys_at >= starts[r]) & (keys_at <= tok)
        bias = jnp.where(ok, 0.0, bias)
    local_lat = ll_ref[...]
    s = mm_nt(q, local_lat) + mm(qr, lr_ref[...])
    s = (s.reshape(HEADS, TILE, TOK) + bias[None]).reshape(ROWS, TOK)
    m = jnp.max(s, axis=1, keepdims=True)
    p = jnp.exp2((s - m) * c)
    m_scr[...] = jnp.broadcast_to(m, (ROWS, 128))
    l_scr[...] = jnp.broadcast_to(jnp.sum(p, axis=1, keepdims=True), (ROWS, 128))
    acc_scr[...] = mm(p.astype(bf16), local_lat)

    for pre in range(PREF):
        needed = (first < zero_count) if pre == 0 else (first + TILE > zero_count)

        @pl.when(needed)
        def _(pre=pre):
            views = block_views(pieces[pre])
            place = first + lax.broadcasted_iota(jnp.int32, (ROWS, 1), 0) % TILE
            mine = (place < zero_count) if pre == 0 else (place >= zero_count)
            row_bias = jnp.where(mine, 0.0, NEG)
            per = 4
            chunks = [views[k : k + per] for k in range(0, len(views), per)]
            m_old = m_scr[:, :1]
            m_new = m_old
            for k, chunk in enumerate(chunks):
                lat = jnp.concatenate([ref[at : at + 128, :] for ref, at in chunk], axis=0)
                rope = jnp.concatenate(
                    [
                        jnp.concatenate(
                            [ref[at + 128 : at + 144, j * 128 : (j + 1) * 128] for j in range(4)],
                            axis=0,
                        )
                        for ref, at in chunk
                    ],
                    axis=1,
                )
                s = mm_nt(q, lat) + mm(qr, rope) + row_bias
                s_scr[k] = s
                m_new = jnp.maximum(m_new, jnp.max(s, axis=1, keepdims=True))
            scale_old = jnp.exp2((m_old - m_new) * c)
            total = l_scr[:, :1] * scale_old
            acc = acc_scr[...] * scale_old
            for k, chunk in enumerate(chunks):
                lat = jnp.concatenate([ref[at : at + 128, :] for ref, at in chunk], axis=0)
                p = jnp.exp2((s_scr[k] - m_new) * c)
                total = total + jnp.sum(p, axis=1, keepdims=True)
                acc = acc + mm(p.astype(bf16), lat)
            m_scr[...] = jnp.broadcast_to(m_new, (ROWS, 128))
            l_scr[...] = jnp.broadcast_to(total, (ROWS, 128))
            acc_scr[...] = acc

    out = acc_scr[...] / l_scr[:, :1]
    o_ref[...] = out.astype(bf16).reshape(HEADS, TILE, LAT)


def attend(scalars, qa, qr, local_lat, local_rope, pieces0, pieces1):
    n_pieces = len(pieces0)
    whole = lambda a: pl.BlockSpec(a.shape, lambda i, s: (0,) * a.ndim)
    pieces = [*pieces0, *pieces1]
    return pl.pallas_call(
        lambda *refs: attention_kernel(n_pieces, *refs),
        out_shape=jax.ShapeDtypeStruct((HEADS, TOK, LAT), bf16),
        grid_spec=pltpu.PrefetchScalarGridSpec(
            num_scalar_prefetch=1,
            grid=(TOK // TILE,),
            in_specs=[
                pl.BlockSpec((HEADS, TILE, LAT), lambda i, s: (0, i, 0)),
                pl.BlockSpec((HEADS, TILE, ROPE), lambda i, s: (0, i, 0)),
                whole(local_lat),
                whole(local_rope),
                *[whole(a) for a in pieces],
            ],
            out_specs=pl.BlockSpec((HEADS, TILE, LAT), lambda i, s: (0, i, 0)),
            scratch_shapes=[
                pltpu.VMEM((4, ROWS, 512), f32),
                pltpu.VMEM((ROWS, 128), f32),
                pltpu.VMEM((ROWS, 128), f32),
                pltpu.VMEM((ROWS, LAT), f32),
            ],
        ),
        name="attention",
    )(scalars, qa, qr, local_lat, local_rope, *pieces)


def project_kernel(sc_ref, o_ref, w_ref, wo_ref, res_ref, gain_ref, hid_ref, norm_ref, acc_ref):
    step = pl.program_id(0)

    @pl.when(step == 0)
    def _():
        acc_ref[...] = res_ref[...].astype(f32)

    back = sort_matrix(sc_ref, True)
    heads = [mm(o_ref[h], w_ref[:, h * 256 + 128 : h * 256 + 256]).astype(bf16) for h in range(HG)]
    head_out = mm(back, jnp.concatenate(heads, axis=1)).astype(bf16)
    acc_ref[...] += mm(head_out, wo_ref[...])

    @pl.when(step == HEADS // HG - 1)
    def _():
        hidden = acc_ref[...].astype(bf16)
        hid_ref[...] = hidden
        h32 = hidden.astype(f32)
        inverse = lax.rsqrt(jnp.mean(h32 * h32, axis=1, keepdims=True) + EPS)
        norm_ref[...] = (h32 * inverse * gain_ref[...].astype(f32)).astype(bf16)


def project(scalars, o_lat, w_ukv, w_out, residual, gain):
    return pl.pallas_call(
        project_kernel,
        out_shape=(
            jax.ShapeDtypeStruct((TOK, D), bf16),
            jax.ShapeDtypeStruct((TOK, D), bf16),
        ),
        grid_spec=pltpu.PrefetchScalarGridSpec(
            num_scalar_prefetch=1,
            grid=(HEADS // HG,),
            in_specs=[
                pl.BlockSpec((HG, TOK, LAT), lambda i, s: (i, 0, 0)),
                pl.BlockSpec((LAT, HG * 2 * NOPE), lambda i, s: (0, i)),
                pl.BlockSpec((HG * NOPE, D), lambda i, s: (i, 0)),
                pl.BlockSpec((TOK, D), lambda i, s: (0, 0)),
                pl.BlockSpec((1, D), lambda i, s: (0, 0)),
            ],
            out_specs=[
                pl.BlockSpec((TOK, D), lambda i, s: (0, 0)),
                pl.BlockSpec((TOK, D), lambda i, s: (0, 0)),
            ],
            scratch_shapes=[pltpu.VMEM((TOK, D), f32)],
        ),
        name="project",
    )(scalars, o_lat, w_ukv, w_out, residual, gain)


EG = 8


def rank_table(ids_ref):
    expert = lax.broadcasted_iota(jnp.int32, (EXPERTS, TOK), 0)
    named = ids_ref[0:1, :] == expert
    for k in range(1, TOP):
        named = named | (ids_ref[k : k + 1, :] == expert)
    earlier = lax.broadcasted_iota(jnp.int32, (TOK, TOK), 0) < lax.broadcasted_iota(
        jnp.int32, (TOK, TOK), 1
    )
    rank = mm(jnp.where(named, 1.0, 0.0).astype(bf16), jnp.where(earlier, 1.0, 0.0).astype(bf16))
    return jnp.where(named, rank, -1.0)


def gate_table(ids_ref, gates_ref):
    expert = lax.broadcasted_iota(jnp.int32, (EXPERTS, TOK), 0)
    gates = jnp.zeros((EXPERTS, TOK), f32)
    for k in range(TOP):
        gates = gates + jnp.where(ids_ref[k : k + 1, :] == expert, gates_ref[k : k + 1, :], 0.0)
    return gates


def dispatch_kernel(ids_ref, norm_ref, out_ref, rank_scr):
    step = pl.program_id(0)

    @pl.when(step == 0)
    def _():
        rank_scr[...] = rank_table(ids_ref)

    ranks = rank_scr[pl.ds(step * EG, EG), :]
    slot = lax.broadcasted_iota(jnp.int32, (SLOTS, TOK), 0).astype(f32)
    rows = [jnp.where(ranks[e : e + 1, :] == slot, 1.0, 0.0).astype(bf16) for e in range(EG)]
    sent = mm(jnp.concatenate(rows, axis=0), norm_ref[...]).astype(bf16)
    for e in range(EG):
        part = sent[e * SLOTS : (e + 1) * SLOTS]
        out_ref[2 * e] = part
        out_ref[2 * e + 1] = part


def dispatch(ids_t, normed):
    return pl.pallas_call(
        dispatch_kernel,
        out_shape=jax.ShapeDtypeStruct((2 * EXPERTS, SLOTS, D), bf16),
        grid=(EXPERTS // EG,),
        in_specs=[
            pl.BlockSpec((TOP, TOK), lambda i: (0, 0)),
            pl.BlockSpec((TOK, D), lambda i: (0, 0)),
        ],
        out_specs=pl.BlockSpec((2 * EG, SLOTS, D), lambda i: (i, 0, 0)),
        scratch_shapes=[pltpu.VMEM((EXPERTS, TOK), f32)],
        name="dispatch",
    )(ids_t, normed)


FM = 256


def expert_kernel(x_ref, wg_ref, wd_ref, out_ref):
    x = x_ref[...].reshape(FM, D)
    gate_up = mm(x, wg_ref[0])
    half = gate_up.shape[1] // 2
    gate, up = gate_up[:, :half], gate_up[:, half:]
    act = (gate / (1.0 + jnp.exp(-gate)) * up).astype(bf16)
    out_ref[...] = mm(act, wd_ref[0]).astype(bf16).reshape(out_ref.shape)


def run_expert(rows, w_gate_up, w_down):
    n, slots, _ = rows.shape
    per = FM // slots
    return pl.pallas_call(
        expert_kernel,
        out_shape=jax.ShapeDtypeStruct(rows.shape, bf16),
        grid=(n // per,),
        in_specs=[
            pl.BlockSpec((per, slots, D), lambda i: (i, 0, 0)),
            pl.BlockSpec(w_gate_up.shape, lambda i: (0, 0, 0), pipeline_mode=pl.Buffered(1)),
            pl.BlockSpec(w_down.shape, lambda i: (0, 0, 0), pipeline_mode=pl.Buffered(1)),
        ],
        out_specs=pl.BlockSpec((per, slots, D), lambda i: (i, 0, 0)),
        name="expert",
    )(rows, w_gate_up, w_down)


def combine_kernel(ids_ref, gates_ref, hid_ref, back_ref, out_ref, rank_scr, gate_scr, acc_ref):
    step = pl.program_id(0)

    @pl.when(step == 0)
    def _():
        rank_scr[...] = rank_table(ids_ref)
        gate_scr[...] = gate_table(ids_ref, gates_ref)
        acc_ref[...] = hid_ref[...].astype(f32)

    ranks = rank_scr[pl.ds(step * EG, EG), :]
    gates = gate_scr[pl.ds(step * EG, EG), :]
    slot = lax.broadcasted_iota(jnp.int32, (SLOTS, TOK), 0).astype(f32)
    rows = []
    for e in range(EG):
        row = jnp.where(ranks[e : e + 1, :] == slot, gates[e : e + 1, :], 0.0)
        rows += [row, row]
    weight = jnp.concatenate(rows, axis=0)
    high = weight.astype(bf16)
    low = (weight - high.astype(f32)).astype(bf16)
    back = back_ref[...].reshape(2 * EG * SLOTS, D)
    acc_ref[...] += mm_tn(high, back) + mm_tn(low, back)

    @pl.when(step == EXPERTS // EG - 1)
    def _():
        out_ref[...] = acc_ref[...].astype(bf16)


def combine(ids_t, gates_t, hidden, back):
    return pl.pallas_call(
        combine_kernel,
        out_shape=jax.ShapeDtypeStruct((TOK, D), bf16),
        grid=(EXPERTS // EG,),
        in_specs=[
            pl.BlockSpec((TOP, TOK), lambda i: (0, 0)),
            pl.BlockSpec((TOP, TOK), lambda i: (0, 0)),
            pl.BlockSpec((TOK, D), lambda i: (0, 0)),
            pl.BlockSpec((2 * EG, SLOTS, D), lambda i: (i, 0, 0)),
        ],
        out_specs=pl.BlockSpec((TOK, D), lambda i: (0, 0)),
        scratch_shapes=[
            pltpu.VMEM((EXPERTS, TOK), f32),
            pltpu.VMEM((EXPERTS, TOK), f32),
            pltpu.VMEM((TOK, D), f32),
        ],
        name="combine",
    )(ids_t, gates_t, hidden, back)


def shift(axis, k):
    pairs = []
    for x in range(4):
        for y in range(4):
            tx, ty = ((x + k) % 4, y) if axis == "x" else (x, (y + k) % 4)
            pairs.append((x * 4 + y, tx * 4 + ty))
    return pairs


def hop(a, axis, k):
    return lax.ppermute(a, "wide", shift(axis, k))


def gather_blocks(own, first, second):
    row = jnp.concatenate([own, hop(own, first, 1), hop(own, first, -1), hop(own, first, 2)], axis=0)
    ahead, behind = hop(row, second, 1), hop(row, second, -1)
    half = row.shape[0] // 2
    far0, far1 = hop(ahead[:half], second, 1), hop(behind[half:], second, -1)
    return [row, ahead, behind, far0, far1]


def pack_prefix(latent, rope):
    packed = rope.reshape(4, 16, TOK).transpose(1, 0, 2).reshape(16, 4 * TOK)
    return jnp.concatenate([latent, packed], axis=0)


def body(
    queries,
    suffix_latent,
    suffix_rope,
    residual,
    prefix_latent,
    prefix_rope,
    suffix_lengths,
    prefix_ids,
    w_ukv,
    w_out,
    norm_gain,
    expert_ids,
    gate_values,
    expert_gate_up,
    expert_down,
):
    scalars = jnp.concatenate([suffix_lengths[0], prefix_ids[0]])
    pieces0 = gather_blocks(pack_prefix(prefix_latent[0, 0], prefix_rope[0, 0]), "x", "y")
    pieces1 = gather_blocks(pack_prefix(prefix_latent[0, 1], prefix_rope[0, 1]), "y", "x")
    qa, qr = prepare_queries(scalars, queries, w_ukv)
    o_lat = attend(scalars, qa, qr, suffix_latent, suffix_rope, pieces0, pieces1)
    hidden, normed = project(scalars, o_lat, w_ukv, w_out, residual, norm_gain.reshape(1, D))
    ids_t = expert_ids.T
    gates_t = gate_values.T
    sent = dispatch(ids_t, normed)
    rows = lax.all_to_all(sent, ("req", "wide"), split_axis=0, concat_axis=0, tiled=True)
    made = run_expert(rows, expert_gate_up, expert_down)
    back = lax.all_to_all(made, ("req", "wide"), split_axis=0, concat_axis=0, tiled=True)
    return combine(ids_t, gates_t, hidden, back)


def solution(mesh):
    return jax.shard_map(
        body,
        mesh=mesh,
        in_specs=(
            P(("req", "wide"), None),
            P(("req", "wide"), None),
            P(None, ("req", "wide")),
            P(("req", "wide"), None),
            P("req", None, "wide", None),
            P("req", None, None, "wide"),
            P(("req", "wide"), None),
            P(("req", "wide"), None),
            P(),
            P(),
            P(),
            P(("req", "wide"), None),
            P(("req", "wide"), None),
            P(("req", "wide"), None, None),
            P(("req", "wide"), None, None),
        ),
        out_specs=P(("req", "wide"), None),
        check_vma=False,
    )
```

```python
import jax
import jax.numpy as jnp
from jax import lax
from jax.experimental import pallas as pl
from jax.experimental.pallas import tpu as pltpu
from jax.sharding import PartitionSpec as P

D = 2048
HEADS = 16
NOPE = 128
ROPE = 64
LAT = 512
TOP = 6
PREF = 2
EXPERTS = 64
TOK = 128
REQS = 4
TILE = 16
CAP = 13
SLOTS_A = 8
HALF = D // 2
PIECE = D // 8
WIDTH_B = HALF + PIECE
BLK = 144
EPS = 1e-06
SCALE = 1.0 / (NOPE + ROPE) ** 0.5
LOG2E = 1.4426950408889634
NEG = -1e30
bf16 = jnp.bfloat16
f32 = jnp.float32


def request_scalars(sc_ref):
    lens = [sc_ref[r] for r in range(REQS)]
    own = [sc_ref[REQS + r] for r in range(REQS)]
    starts, total = [], 0
    for r in range(REQS):
        starts.append(total)
        total = total + lens[r]
    zero_count = sum(jnp.where(own[r] == 0, lens[r], 0) for r in range(REQS))
    bases, next0, next1 = [], 0, zero_count
    for r in range(REQS):
        is0 = own[r] == 0
        bases.append(jnp.where(is0, next0, next1))
        next0 = next0 + jnp.where(is0, lens[r], 0)
        next1 = next1 + jnp.where(is0, 0, lens[r])
    return lens, starts, bases, zero_count


def place_of(tokens, starts, bases):
    place = tokens - starts[0] + bases[0]
    for r in range(1, REQS):
        place = jnp.where(tokens >= starts[r], tokens - starts[r] + bases[r], place)
    return place


def sort_matrix(sc_ref, transposed):
    lens, starts, bases, _ = request_scalars(sc_ref)
    token_dim = 0 if transposed else 1
    tokens = lax.broadcasted_iota(jnp.int32, (TOK, TOK), token_dim)
    slots = lax.broadcasted_iota(jnp.int32, (TOK, TOK), 1 - token_dim)
    return jnp.where(place_of(tokens, starts, bases) == slots, 1.0, 0.0).astype(bf16)


def mm(a, b):
    return jnp.dot(a, b, preferred_element_type=f32)


def mm_nt(a, b):
    return lax.dot_general(a, b, (((1,), (1,)), ((), ())), preferred_element_type=f32)


def mm_tn(a, b):
    return lax.dot_general(a, b, (((0,), (0,)), ((), ())), preferred_element_type=f32)


HG = 4


def query_kernel(sc_ref, q_ref, qr_ref, w_ref, qa_ref, qo_ref):
    order = sort_matrix(sc_ref, False)
    nope = mm(order, q_ref[...]).astype(bf16)
    rope = mm(order, qr_ref[...]).astype(bf16)
    for h in range(HG):
        keys = w_ref[:, h * 256 : h * 256 + 128]
        qa_ref[h] = mm_nt(nope[:, h * 128 : (h + 1) * 128], keys).astype(bf16)
        qo_ref[h] = rope[:, h * ROPE : (h + 1) * ROPE]


def prepare_queries(scalars, queries, w_ukv):
    return pl.pallas_call(
        query_kernel,
        out_shape=(
            jax.ShapeDtypeStruct((HEADS, TOK, LAT), bf16),
            jax.ShapeDtypeStruct((HEADS, TOK, ROPE), bf16),
        ),
        grid_spec=pltpu.PrefetchScalarGridSpec(
            num_scalar_prefetch=1,
            grid=(HEADS // HG,),
            in_specs=[
                pl.BlockSpec((TOK, HG * NOPE), lambda i, s: (0, i)),
                pl.BlockSpec((TOK, HG * ROPE), lambda i, s: (0, HEADS * NOPE // (HG * ROPE) + i)),
                pl.BlockSpec((LAT, HG * 2 * NOPE), lambda i, s: (0, i)),
            ],
            out_specs=[
                pl.BlockSpec((HG, TOK, LAT), lambda i, s: (i, 0, 0)),
                pl.BlockSpec((HG, TOK, ROPE), lambda i, s: (i, 0, 0)),
            ],
        ),
        name="query_prep",
    )(scalars, queries, queries, w_ukv)


ROWS = HEADS * TILE


def block_views(refs):
    views = []
    for ref in refs:
        for b in range(ref.shape[0] // BLK):
            views.append((ref, b * BLK))
    return views


def attention_kernel(n_pieces, sc_ref, qa_ref, qr_ref, ll_ref, lr_ref, *rest):
    pieces = (rest[:n_pieces], rest[n_pieces : 2 * n_pieces])
    o_ref, s_scr, m_scr, l_scr, acc_scr = rest[2 * n_pieces :]
    lens, starts, bases, zero_count = request_scalars(sc_ref)
    first = pl.program_id(0) * TILE
    c = SCALE * LOG2E
    q = qa_ref[...].reshape(ROWS, LAT)
    qr = qr_ref[...].reshape(ROWS, ROPE)

    places = first + lax.broadcasted_iota(jnp.int32, (TILE, TOK), 0)
    keys_at = lax.broadcasted_iota(jnp.int32, (TILE, TOK), 1)
    bias = jnp.full((TILE, TOK), NEG, f32)
    for r in range(REQS):
        mine = (places >= bases[r]) & (places < bases[r] + lens[r])
        tok = places - bases[r] + starts[r]
        ok = mine & (keys_at >= starts[r]) & (keys_at <= tok)
        bias = jnp.where(ok, 0.0, bias)
    local_lat = ll_ref[...]
    s = mm_nt(q, local_lat) + mm(qr, lr_ref[...])
    s = (s.reshape(HEADS, TILE, TOK) + bias[None]).reshape(ROWS, TOK)
    m = jnp.max(s, axis=1, keepdims=True)
    p = jnp.exp2((s - m) * c)
    m_scr[...] = jnp.broadcast_to(m, (ROWS, 128))
    l_scr[...] = jnp.broadcast_to(jnp.sum(p, axis=1, keepdims=True), (ROWS, 128))
    acc_scr[...] = mm(p.astype(bf16), local_lat)

    for pre in range(PREF):
        needed = (first < zero_count) if pre == 0 else (first + TILE > zero_count)

        @pl.when(needed)
        def _(pre=pre):
            views = block_views(pieces[pre])
            place = first + lax.broadcasted_iota(jnp.int32, (ROWS, 1), 0) % TILE
            mine = (place < zero_count) if pre == 0 else (place >= zero_count)
            row_bias = jnp.where(mine, 0.0, NEG)
            per = 4
            chunks = [views[k : k + per] for k in range(0, len(views), per)]
            m_old = m_scr[:, :1]
            m_new = m_old
            for k, chunk in enumerate(chunks):
                lat = jnp.concatenate([ref[at : at + 128, :] for ref, at in chunk], axis=0)
                rope = jnp.concatenate(
                    [
                        jnp.concatenate(
                            [ref[at + 128 : at + 144, j * 128 : (j + 1) * 128] for j in range(4)],
                            axis=0,
                        )
                        for ref, at in chunk
                    ],
                    axis=1,
                )
                s = mm_nt(q, lat) + mm(qr, rope) + row_bias
                s_scr[k] = s
                m_new = jnp.maximum(m_new, jnp.max(s, axis=1, keepdims=True))
            scale_old = jnp.exp2((m_old - m_new) * c)
            total = l_scr[:, :1] * scale_old
            acc = acc_scr[...] * scale_old
            for k, chunk in enumerate(chunks):
                lat = jnp.concatenate([ref[at : at + 128, :] for ref, at in chunk], axis=0)
                p = jnp.exp2((s_scr[k] - m_new) * c)
                total = total + jnp.sum(p, axis=1, keepdims=True)
                acc = acc + mm(p.astype(bf16), lat)
            m_scr[...] = jnp.broadcast_to(m_new, (ROWS, 128))
            l_scr[...] = jnp.broadcast_to(total, (ROWS, 128))
            acc_scr[...] = acc

    out = acc_scr[...] / l_scr[:, :1]
    o_ref[...] = out.astype(bf16).reshape(HEADS, TILE, LAT)


def attend(scalars, qa, qr, local_lat, local_rope, pieces0, pieces1):
    n_pieces = len(pieces0)
    whole = lambda a: pl.BlockSpec(a.shape, lambda i, s: (0,) * a.ndim)
    pieces = [*pieces0, *pieces1]
    return pl.pallas_call(
        lambda *refs: attention_kernel(n_pieces, *refs),
        out_shape=jax.ShapeDtypeStruct((HEADS, TOK, LAT), bf16),
        grid_spec=pltpu.PrefetchScalarGridSpec(
            num_scalar_prefetch=1,
            grid=(TOK // TILE,),
            in_specs=[
                pl.BlockSpec((HEADS, TILE, LAT), lambda i, s: (0, i, 0)),
                pl.BlockSpec((HEADS, TILE, ROPE), lambda i, s: (0, i, 0)),
                whole(local_lat),
                whole(local_rope),
                *[whole(a) for a in pieces],
            ],
            out_specs=pl.BlockSpec((HEADS, TILE, LAT), lambda i, s: (0, i, 0)),
            scratch_shapes=[
                pltpu.VMEM((4, ROWS, 512), f32),
                pltpu.VMEM((ROWS, 128), f32),
                pltpu.VMEM((ROWS, 128), f32),
                pltpu.VMEM((ROWS, LAT), f32),
            ],
        ),
        name="attention",
    )(scalars, qa, qr, local_lat, local_rope, *pieces)


def project_kernel(sc_ref, o_ref, w_ref, wo_ref, res_ref, gain_ref, hid_ref, norm_ref, acc_ref):
    step = pl.program_id(0)

    @pl.when(step == 0)
    def _():
        acc_ref[...] = res_ref[...].astype(f32)

    back = sort_matrix(sc_ref, True)
    heads = [mm(o_ref[h], w_ref[:, h * 256 + 128 : h * 256 + 256]).astype(bf16) for h in range(HG)]
    head_out = mm(back, jnp.concatenate(heads, axis=1)).astype(bf16)
    acc_ref[...] += mm(head_out, wo_ref[...])

    @pl.when(step == HEADS // HG - 1)
    def _():
        hidden = acc_ref[...].astype(bf16)
        hid_ref[...] = hidden
        h32 = hidden.astype(f32)
        inverse = lax.rsqrt(jnp.mean(h32 * h32, axis=1, keepdims=True) + EPS)
        norm_ref[...] = (h32 * inverse * gain_ref[...].astype(f32)).astype(bf16)


def project(scalars, o_lat, w_ukv, w_out, residual, gain):
    return pl.pallas_call(
        project_kernel,
        out_shape=(
            jax.ShapeDtypeStruct((TOK, D), bf16),
            jax.ShapeDtypeStruct((TOK, D), bf16),
        ),
        grid_spec=pltpu.PrefetchScalarGridSpec(
            num_scalar_prefetch=1,
            grid=(HEADS // HG,),
            in_specs=[
                pl.BlockSpec((HG, TOK, LAT), lambda i, s: (i, 0, 0)),
                pl.BlockSpec((LAT, HG * 2 * NOPE), lambda i, s: (0, i)),
                pl.BlockSpec((HG * NOPE, D), lambda i, s: (i, 0)),
                pl.BlockSpec((TOK, D), lambda i, s: (0, 0)),
                pl.BlockSpec((1, D), lambda i, s: (0, 0)),
            ],
            out_specs=[
                pl.BlockSpec((TOK, D), lambda i, s: (0, 0)),
                pl.BlockSpec((TOK, D), lambda i, s: (0, 0)),
            ],
            scratch_shapes=[pltpu.VMEM((TOK, D), f32)],
        ),
        name="project",
    )(scalars, o_lat, w_ukv, w_out, residual, gain)


def rank_table(ids_ref):
    expert = lax.broadcasted_iota(jnp.int32, (EXPERTS, TOK), 0)
    named = ids_ref[0:1, :] == expert
    for k in range(1, TOP):
        named = named | (ids_ref[k : k + 1, :] == expert)
    earlier = lax.broadcasted_iota(jnp.int32, (TOK, TOK), 0) < lax.broadcasted_iota(
        jnp.int32, (TOK, TOK), 1
    )
    rank = mm(jnp.where(named, 1.0, 0.0).astype(bf16), jnp.where(earlier, 1.0, 0.0).astype(bf16))
    return jnp.where(named, rank, -1.0)


def gate_table(ids_ref, gates_ref):
    expert = lax.broadcasted_iota(jnp.int32, (EXPERTS, TOK), 0)
    gates = jnp.zeros((EXPERTS, TOK), f32)
    for k in range(TOP):
        gates = gates + jnp.where(ids_ref[k : k + 1, :] == expert, gates_ref[k : k + 1, :], 0.0)
    return gates


def whole_rows(ranks, experts, copies, values=None):
    slot = lax.broadcasted_iota(jnp.int32, (SLOTS_A, TOK), 0).astype(f32)
    rows = []
    for e in range(experts):
        on = 1.0 if values is None else values[e : e + 1, :]
        rows += [jnp.where(ranks[e : e + 1, :] == slot, on, 0.0)] * copies
    return jnp.concatenate(rows, axis=0)


def packed_rows(ranks, experts, copies, values=None):
    row = lax.broadcasted_iota(jnp.int32, (8, TOK), 0)
    slot = (SLOTS_A + row // 2).astype(f32)
    even = row % 2 == 0
    lower, upper, last = [], [], []
    for e in range(experts):
        rank = ranks[e : e + 1, :]
        on = 1.0 if values is None else values[e : e + 1, :]
        hit = jnp.where(rank == slot, on, 0.0)
        lower += [jnp.where(even, hit, 0.0)] * copies
        upper += [jnp.where(even, 0.0, hit)] * copies
        last += [jnp.where(jnp.broadcast_to(rank, (8, TOK)) == CAP - 1.0, on, 0.0)] * copies
    return [jnp.concatenate(part, axis=0) for part in (lower, upper, last)]


def pieces_of(last):
    row = lax.broadcasted_iota(jnp.int32, last.shape, 0) % 8
    return [jnp.where(row == q, last, 0.0) for q in range(8)]


EG = 16


def dispatch_kernel(ids_ref, norm_ref, out_ref, rank_scr):
    step = pl.program_id(0)

    @pl.when(step == 0)
    def _():
        rank_scr[...] = rank_table(ids_ref)

    ranks = rank_scr[pl.ds(step * EG, EG), :]
    sent = mm(whole_rows(ranks, EG, 1).astype(bf16), norm_ref[...]).astype(bf16)
    for e in range(EG):
        part = sent[e * SLOTS_A : (e + 1) * SLOTS_A]
        out_ref[2 * e] = part
        out_ref[2 * e + 1] = part


def dispatch_packed_kernel(ids_ref, norm_ref, out_ref, rank_scr):
    step = pl.program_id(0)

    @pl.when(step == 0)
    def _():
        rank_scr[...] = rank_table(ids_ref)

    ranks = rank_scr[pl.ds(step * EG, EG), :]
    lower, upper, last = packed_rows(ranks, EG, 1)
    sent = (
        mm(lower.astype(bf16), norm_ref[:, :HALF]) + mm(upper.astype(bf16), norm_ref[:, HALF:])
    ).astype(bf16)
    tail = jnp.zeros((EG * 8, PIECE), f32)
    for q, piece in enumerate(pieces_of(last)):
        tail = tail + mm(piece.astype(bf16), norm_ref[:, q * PIECE : (q + 1) * PIECE])
    tail = tail.astype(bf16)
    for e in range(EG):
        for copy in range(2):
            out_ref[2 * e + copy, :, :HALF] = sent[e * 8 : (e + 1) * 8]
            out_ref[2 * e + copy, :, HALF:] = tail[e * 8 : (e + 1) * 8]


def dispatch(kernel, width, ids_t, normed, name):
    return pl.pallas_call(
        kernel,
        out_shape=jax.ShapeDtypeStruct((2 * EXPERTS, 8, width), bf16),
        grid=(EXPERTS // EG,),
        in_specs=[
            pl.BlockSpec((TOP, TOK), lambda i: (0, 0)),
            pl.BlockSpec((TOK, D), lambda i: (0, 0)),
        ],
        out_specs=pl.BlockSpec((2 * EG, 8, width), lambda i: (i, 0, 0)),
        scratch_shapes=[pltpu.VMEM((EXPERTS, TOK), f32)],
        name=name,
    )(ids_t, normed)


def expert_rows(x, wg_ref, wd_ref):
    gate_up = mm(x, wg_ref[0])
    half = gate_up.shape[1] // 2
    gate, up = gate_up[:, :half], gate_up[:, half:]
    act = (gate / (1.0 + jnp.exp(-gate)) * up).astype(bf16)
    return mm(act, wd_ref[0]).astype(bf16)


def expert_kernel(x_ref, wg_ref, wd_ref, out_ref):
    x = x_ref[...].reshape(-1, D)
    out_ref[...] = expert_rows(x, wg_ref, wd_ref).reshape(out_ref.shape)


def select(rows, columns, stride, offset):
    r = lax.broadcasted_iota(jnp.int32, (rows, columns), 0)
    c = lax.broadcasted_iota(jnp.int32, (rows, columns), 1)
    return jnp.where(c == r * stride + offset, 1.0, 0.0).astype(bf16)


def expert_packed_kernel(x_ref, wg_ref, wd_ref, out_ref):
    n = x_ref.shape[0]
    x = x_ref[...].reshape(8 * n, WIDTH_B)
    even, odd = select(4 * n, 8 * n, 2, 0), select(4 * n, 8 * n, 2, 1)
    each = [select(n, 8 * n, 8, q) for q in range(8)]
    main = jnp.concatenate([mm(even, x[:, :HALF]), mm(odd, x[:, :HALF])], axis=1)
    last = jnp.concatenate([mm(pick, x[:, HALF:]) for pick in each], axis=1)
    y = expert_rows(jnp.concatenate([main, last], axis=0).astype(bf16), wg_ref, wd_ref)
    main, last = y[: 4 * n], y[4 * n :]
    out = mm_tn(even, main[:, :HALF]) + mm_tn(odd, main[:, HALF:])
    tail = jnp.zeros((8 * n, PIECE), f32)
    for q, pick in enumerate(each):
        tail = tail + mm_tn(pick, last[:, q * PIECE : (q + 1) * PIECE])
    out_ref[:, :, :HALF] = out.astype(bf16).reshape(n, 8, HALF)
    out_ref[:, :, HALF:] = tail.astype(bf16).reshape(n, 8, PIECE)


def run_expert(kernel, rows, w_gate_up, w_down, name):
    width = rows.shape[2]
    per = 32
    return pl.pallas_call(
        kernel,
        out_shape=jax.ShapeDtypeStruct(rows.shape, bf16),
        grid=(rows.shape[0] // per,),
        in_specs=[
            pl.BlockSpec((per, 8, width), lambda i: (i, 0, 0)),
            pl.BlockSpec(w_gate_up.shape, lambda i: (0, 0, 0), pipeline_mode=pl.Buffered(1)),
            pl.BlockSpec(w_down.shape, lambda i: (0, 0, 0), pipeline_mode=pl.Buffered(1)),
        ],
        out_specs=pl.BlockSpec((per, 8, width), lambda i: (i, 0, 0)),
        name=name,
    )(rows, w_gate_up, w_down)


def weighted(weight, back):
    high = weight.astype(bf16)
    low = (weight - high.astype(f32)).astype(bf16)
    both = mm_tn(jnp.concatenate([high, low], axis=1), back)
    return both[:TOK] + both[TOK:]


def combine_kernel(ids_ref, gates_ref, hid_ref, back_ref, out_ref, rank_scr, gate_scr):
    step = pl.program_id(0)

    @pl.when(step == 0)
    def _():
        rank_scr[...] = rank_table(ids_ref)
        gate_scr[...] = gate_table(ids_ref, gates_ref)
        out_ref[...] = hid_ref[...].astype(f32)

    ranks = rank_scr[pl.ds(step * EG, EG), :]
    gates = gate_scr[pl.ds(step * EG, EG), :]
    back = back_ref[...].reshape(2 * EG * SLOTS_A, D)
    out_ref[...] += weighted(whole_rows(ranks, EG, 2, gates), back)


def combine_packed_kernel(
    ids_ref, gates_ref, sum_ref, back_ref, out_ref, rank_scr, gate_scr, acc_ref
):
    step = pl.program_id(0)

    @pl.when(step == 0)
    def _():
        rank_scr[...] = rank_table(ids_ref)
        gate_scr[...] = gate_table(ids_ref, gates_ref)
        acc_ref[...] = sum_ref[...]

    ranks = rank_scr[pl.ds(step * EG, EG), :]
    gates = gate_scr[pl.ds(step * EG, EG), :]
    back = back_ref[...].reshape(2 * EG * 8, WIDTH_B)
    lower, upper, last = packed_rows(ranks, EG, 2, gates)
    acc_ref[:, :HALF] += weighted(lower, back[:, :HALF])
    acc_ref[:, HALF:] += weighted(upper, back[:, :HALF])
    for q, piece in enumerate(pieces_of(last)):
        acc_ref[:, q * PIECE : (q + 1) * PIECE] += weighted(piece, back[:, HALF:])

    @pl.when(step == EXPERTS // EG - 1)
    def _():
        out_ref[...] = acc_ref[...].astype(bf16)


def combine(kernel, ids_t, gates_t, base, back, out_type, name):
    scratch = [pltpu.VMEM((EXPERTS, TOK), f32), pltpu.VMEM((EXPERTS, TOK), f32)]
    if out_type == bf16:
        scratch.append(pltpu.VMEM((TOK, D), f32))
    return pl.pallas_call(
        kernel,
        out_shape=jax.ShapeDtypeStruct((TOK, D), out_type),
        grid=(EXPERTS // EG,),
        in_specs=[
            pl.BlockSpec((TOP, TOK), lambda i: (0, 0)),
            pl.BlockSpec((TOP, TOK), lambda i: (0, 0)),
            pl.BlockSpec((TOK, D), lambda i: (0, 0)),
            pl.BlockSpec((2 * EG, 8, back.shape[2]), lambda i: (i, 0, 0)),
        ],
        out_specs=pl.BlockSpec((TOK, D), lambda i: (0, 0)),
        scratch_shapes=scratch,
        name=name,
    )(ids_t, gates_t, base, back)


def shift(axis, k):
    pairs = []
    for x in range(4):
        for y in range(4):
            tx, ty = ((x + k) % 4, y) if axis == "x" else (x, (y + k) % 4)
            pairs.append((x * 4 + y, tx * 4 + ty))
    return pairs


def hop(a, axis, k):
    return lax.ppermute(a, "wide", shift(axis, k))


def gather_blocks(own, first, second):
    row = jnp.concatenate([own, hop(own, first, 1), hop(own, first, -1), hop(own, first, 2)], axis=0)
    ahead, behind = hop(row, second, 1), hop(row, second, -1)
    half = row.shape[0] // 2
    far0, far1 = hop(ahead[:half], second, 1), hop(behind[half:], second, -1)
    return [row, ahead, behind, far0, far1]


def pack_prefix(latent, rope):
    packed = rope.reshape(4, 16, TOK).transpose(1, 0, 2).reshape(16, 4 * TOK)
    return jnp.concatenate([latent, packed], axis=0)


def exchange(a):
    return lax.all_to_all(a, ("req", "wide"), split_axis=0, concat_axis=0, tiled=True)


def body(
    queries,
    suffix_latent,
    suffix_rope,
    residual,
    prefix_latent,
    prefix_rope,
    suffix_lengths,
    prefix_ids,
    w_ukv,
    w_out,
    norm_gain,
    expert_ids,
    gate_values,
    expert_gate_up,
    expert_down,
):
    scalars = jnp.concatenate([suffix_lengths[0], prefix_ids[0]])
    pieces0 = gather_blocks(pack_prefix(prefix_latent[0, 0], prefix_rope[0, 0]), "x", "y")
    pieces1 = gather_blocks(pack_prefix(prefix_latent[0, 1], prefix_rope[0, 1]), "y", "x")
    qa, qr = prepare_queries(scalars, queries, w_ukv)
    o_lat = attend(scalars, qa, qr, suffix_latent, suffix_rope, pieces0, pieces1)
    hidden, normed = project(scalars, o_lat, w_ukv, w_out, residual, norm_gain.reshape(1, D))
    ids_t = expert_ids.T
    gates_t = gate_values.T
    sent_a = dispatch(dispatch_kernel, D, ids_t, normed, "dispatch_a")
    sent_b = dispatch(dispatch_packed_kernel, WIDTH_B, ids_t, normed, "dispatch_b")
    rows_a = exchange(sent_a)
    rows_b = exchange(sent_b)
    made_a = run_expert(expert_kernel, rows_a, expert_gate_up, expert_down, "expert_a")
    made_b = run_expert(expert_packed_kernel, rows_b, expert_gate_up, expert_down, "expert_b")
    back_a = exchange(made_a)
    back_b = exchange(made_b)
    part = combine(combine_kernel, ids_t, gates_t, hidden, back_a, f32, "combine_a")
    return combine(combine_packed_kernel, ids_t, gates_t, part, back_b, bf16, "combine_b")


def solution(mesh):
    return jax.shard_map(
        body,
        mesh=mesh,
        in_specs=(
            P(("req", "wide"), None),
            P(("req", "wide"), None),
            P(None, ("req", "wide")),
            P(("req", "wide"), None),
            P("req", None, "wide", None),
            P("req", None, None, "wide"),
            P(("req", "wide"), None),
            P(("req", "wide"), None),
            P(),
            P(),
            P(),
            P(("req", "wide"), None),
            P(("req", "wide"), None),
            P(("req", "wide"), None, None),
            P(("req", "wide"), None, None),
        ),
        out_specs=P(("req", "wide"), None),
        check_vma=False,
    )
```

```python
import jax
import jax.numpy as jnp
from jax import lax
from jax.experimental import pallas as pl
from jax.experimental.pallas import tpu as pltpu
from jax.sharding import PartitionSpec as P


D = 2048
HEADS = 16
NOPE = 128
ROPE = 64
LAT = 512
TOP = 6
PREF = 2
EXPERTS = 64
TOK = 128
REQS = 4
TILE = 16
CAP = 13
SLOTS_A = 8
HALF = D // 2
PIECE = D // 8
WIDTH_B = HALF + PIECE
BLK = 144
EPS = 1e-06
SCALE = 1.0 / (NOPE + ROPE) ** 0.5
LOG2E = 1.4426950408889634
NEG = -1e30
bf16 = jnp.bfloat16
f32 = jnp.float32


def request_scalars(sc_ref):
    lens = [sc_ref[r] for r in range(REQS)]
    own = [sc_ref[REQS + r] for r in range(REQS)]
    starts, total = [], 0
    for r in range(REQS):
        starts.append(total)
        total = total + lens[r]
    zero_count = sum(jnp.where(own[r] == 0, lens[r], 0) for r in range(REQS))
    bases, next0, next1 = [], 0, zero_count
    for r in range(REQS):
        is0 = own[r] == 0
        bases.append(jnp.where(is0, next0, next1))
        next0 = next0 + jnp.where(is0, lens[r], 0)
        next1 = next1 + jnp.where(is0, 0, lens[r])
    return lens, starts, bases, zero_count


def place_of(tokens, starts, bases):
    place = tokens - starts[0] + bases[0]
    for r in range(1, REQS):
        place = jnp.where(tokens >= starts[r], tokens - starts[r] + bases[r], place)
    return place


def sort_matrix(sc_ref, transposed):
    _, starts, bases, _ = request_scalars(sc_ref)
    token_dim = 0 if transposed else 1
    tokens = lax.broadcasted_iota(jnp.int32, (TOK, TOK), token_dim)
    slots = lax.broadcasted_iota(jnp.int32, (TOK, TOK), 1 - token_dim)
    return jnp.where(place_of(tokens, starts, bases) == slots, 1.0, 0.0).astype(bf16)


def mm(a, b):
    return jnp.dot(a, b, preferred_element_type=f32)


def mm_nt(a, b):
    return lax.dot_general(a, b, (((1,), (1,)), ((), ())), preferred_element_type=f32)


def mm_tn(a, b):
    return lax.dot_general(a, b, (((0,), (0,)), ((), ())), preferred_element_type=f32)


HG = 4


def query_kernel(sc_ref, q_ref, qr_ref, w_ref, qa_ref, qo_ref):
    order = sort_matrix(sc_ref, False)
    nope = mm(order, q_ref[...]).astype(bf16)
    rope = mm(order, qr_ref[...]).astype(bf16)
    for h in range(HG):
        keys = w_ref[:, h * 256 : h * 256 + 128]
        qa_ref[h] = mm_nt(nope[:, h * 128 : (h + 1) * 128], keys).astype(bf16)
        qo_ref[h] = rope[:, h * ROPE : (h + 1) * ROPE]


def prepare_queries(scalars, queries, w_ukv):
    return pl.pallas_call(
        query_kernel,
        out_shape=(
            jax.ShapeDtypeStruct((HEADS, TOK, LAT), bf16),
            jax.ShapeDtypeStruct((HEADS, TOK, ROPE), bf16),
        ),
        grid_spec=pltpu.PrefetchScalarGridSpec(
            num_scalar_prefetch=1,
            grid=(HEADS // HG,),
            in_specs=[
                pl.BlockSpec((TOK, HG * NOPE), lambda i, s: (0, i)),
                pl.BlockSpec((TOK, HG * ROPE), lambda i, s: (0, HEADS * NOPE // (HG * ROPE) + i)),
                pl.BlockSpec((LAT, HG * 2 * NOPE), lambda i, s: (0, i)),
            ],
            out_specs=[
                pl.BlockSpec((HG, TOK, LAT), lambda i, s: (i, 0, 0)),
                pl.BlockSpec((HG, TOK, ROPE), lambda i, s: (i, 0, 0)),
            ],
        ),
        name="query_prep",
    )(scalars, queries, queries, w_ukv)


ROWS = HEADS * TILE


def block_views(refs):
    views = []
    for ref in refs:
        for b in range(ref.shape[0] // BLK):
            views.append((ref, b * BLK))
    return views


def attention_kernel(n_pieces, stage, sc_ref, qa_ref, qr_ref, *rest):
    rest = list(rest)
    local = [rest.pop(0), rest.pop(0)]
    pieces = (rest[:n_pieces], rest[n_pieces : 2 * n_pieces])
    rest = rest[2 * n_pieces :]
    if stage == LAST:
        o_ref, s_scr, m_scr, l_scr, acc_scr = rest
    else:
        ml_ref, acc_out, s_scr, m_scr, l_scr, acc_scr = rest
    lens, starts, bases, zero_count = request_scalars(sc_ref)
    first = pl.program_id(0) * TILE
    c = SCALE * LOG2E
    q = qa_ref[...].reshape(ROWS, LAT)
    qr = qr_ref[...].reshape(ROWS, ROPE)

    if stage == FIRST:
        ll_ref, lr_ref = local
        places = first + lax.broadcasted_iota(jnp.int32, (TILE, TOK), 0)
        keys_at = lax.broadcasted_iota(jnp.int32, (TILE, TOK), 1)
        bias = jnp.full((TILE, TOK), NEG, f32)
        for r in range(REQS):
            mine = (places >= bases[r]) & (places < bases[r] + lens[r])
            tok = places - bases[r] + starts[r]
            ok = mine & (keys_at >= starts[r]) & (keys_at <= tok)
            bias = jnp.where(ok, 0.0, bias)
        local_lat = ll_ref[...]
        s = mm_nt(q, local_lat) + mm(qr, lr_ref[...])
        s = (s.reshape(HEADS, TILE, TOK) + bias[None]).reshape(ROWS, TOK)
        m = jnp.max(s, axis=1, keepdims=True)
        p = jnp.exp2((s - m) * c)
        m_scr[...] = jnp.broadcast_to(m, (ROWS, 128))
        l_scr[...] = jnp.broadcast_to(jnp.sum(p, axis=1, keepdims=True), (ROWS, 128))
        acc_scr[...] = mm(p.astype(bf16), local_lat)
    else:
        ml_in, acc_in = local
        ml = ml_in[...].reshape(ROWS, 128)
        m_scr[...] = jnp.broadcast_to(ml[:, :1], (ROWS, 128))
        l_scr[...] = jnp.broadcast_to(ml[:, 1:2], (ROWS, 128))
        acc_scr[...] = acc_in[...].reshape(ROWS, LAT)

    for pre in range(PREF):
        needed = (first < zero_count) if pre == 0 else (first + TILE > zero_count)

        @pl.when(needed)
        def _(pre=pre):
            views = block_views(pieces[pre])
            place = first + lax.broadcasted_iota(jnp.int32, (ROWS, 1), 0) % TILE
            mine = (place < zero_count) if pre == 0 else (place >= zero_count)
            row_bias = jnp.where(mine, 0.0, NEG)
            chunks = [views[k : k + 4] for k in range(0, len(views), 4)]
            m_old = m_scr[:, :1]
            m_new = m_old
            for k, chunk in enumerate(chunks):
                lat = jnp.concatenate([ref[at : at + 128, :] for ref, at in chunk], axis=0)
                rope = jnp.concatenate(
                    [
                        jnp.concatenate(
                            [ref[at + 128 : at + 144, j * 128 : (j + 1) * 128] for j in range(4)],
                            axis=0,
                        )
                        for ref, at in chunk
                    ],
                    axis=1,
                )
                s = mm_nt(q, lat) + mm(qr, rope) + row_bias
                s_scr[k] = s
                m_new = jnp.maximum(m_new, jnp.max(s, axis=1, keepdims=True))
            scale_old = jnp.exp2((m_old - m_new) * c)
            total = l_scr[:, :1] * scale_old
            acc = acc_scr[...] * scale_old
            for k, chunk in enumerate(chunks):
                lat = jnp.concatenate([ref[at : at + 128, :] for ref, at in chunk], axis=0)
                p = jnp.exp2((s_scr[k] - m_new) * c)
                total = total + jnp.sum(p, axis=1, keepdims=True)
                acc = acc + mm(p.astype(bf16), lat)
            m_scr[...] = jnp.broadcast_to(m_new, (ROWS, 128))
            l_scr[...] = jnp.broadcast_to(total, (ROWS, 128))
            acc_scr[...] = acc

    if stage == LAST:
        out = acc_scr[...] / l_scr[:, :1]
        o_ref[...] = out.astype(bf16).reshape(HEADS, TILE, LAT)
    else:
        lane = lax.broadcasted_iota(jnp.int32, (ROWS, 128), 1)
        ml = jnp.where(lane == 0, m_scr[...], l_scr[...])
        ml_ref[...] = ml.reshape(HEADS, TILE, 128)
        acc_out[...] = acc_scr[...].reshape(HEADS, TILE, LAT)


FIRST, MIDDLE, LAST = 0, 1, 2


def attend(stage, scalars, qa, qr, local, pieces0, pieces1):
    n_pieces = len(pieces0)
    whole = lambda a: pl.BlockSpec(a.shape, lambda i, s: (0,) * a.ndim)
    tiled = lambda width: pl.BlockSpec((HEADS, TILE, width), lambda i, s: (0, i, 0))
    pieces = [*pieces0, *pieces1]
    local_specs = [whole(a) for a in local] if stage == FIRST else [tiled(128), tiled(LAT)]
    if stage == LAST:
        out_shape = jax.ShapeDtypeStruct((HEADS, TOK, LAT), bf16)
        out_specs = tiled(LAT)
    else:
        out_shape = (
            jax.ShapeDtypeStruct((HEADS, TOK, 128), f32),
            jax.ShapeDtypeStruct((HEADS, TOK, LAT), f32),
        )
        out_specs = [tiled(128), tiled(LAT)]
    keys = sum(a.shape[0] // BLK for a in pieces0)
    return pl.pallas_call(
        lambda *refs: attention_kernel(n_pieces, stage, *refs),
        out_shape=out_shape,
        grid_spec=pltpu.PrefetchScalarGridSpec(
            num_scalar_prefetch=1,
            grid=(TOK // TILE,),
            in_specs=[tiled(LAT), tiled(ROPE), *local_specs, *[whole(a) for a in pieces]],
            out_specs=out_specs,
            scratch_shapes=[
                pltpu.VMEM((max(keys // 4, 1), ROWS, 512), f32),
                pltpu.VMEM((ROWS, 128), f32),
                pltpu.VMEM((ROWS, 128), f32),
                pltpu.VMEM((ROWS, LAT), f32),
            ],
        ),
    )(scalars, qa, qr, *local, *pieces)


def project_kernel(sc_ref, o_ref, w_ref, wo_ref, res_ref, gain_ref, hid_ref, norm_ref, acc_ref):
    step = pl.program_id(0)

    @pl.when(step == 0)
    def _():
        acc_ref[...] = res_ref[...].astype(f32)

    back = sort_matrix(sc_ref, True)
    heads = [mm(o_ref[h], w_ref[:, h * 256 + 128 : h * 256 + 256]).astype(bf16) for h in range(HG)]
    head_out = mm(back, jnp.concatenate(heads, axis=1)).astype(bf16)
    acc_ref[...] += mm(head_out, wo_ref[...])

    @pl.when(step == HEADS // HG - 1)
    def _():
        hidden = acc_ref[...].astype(bf16)
        hid_ref[...] = hidden
        h32 = hidden.astype(f32)
        inverse = lax.rsqrt(jnp.mean(h32 * h32, axis=1, keepdims=True) + EPS)
        norm_ref[...] = (h32 * inverse * gain_ref[...].astype(f32)).astype(bf16)


def project(scalars, o_lat, w_ukv, w_out, residual, gain):
    return pl.pallas_call(
        project_kernel,
        out_shape=(
            jax.ShapeDtypeStruct((TOK, D), bf16),
            jax.ShapeDtypeStruct((TOK, D), bf16),
        ),
        grid_spec=pltpu.PrefetchScalarGridSpec(
            num_scalar_prefetch=1,
            grid=(HEADS // HG,),
            in_specs=[
                pl.BlockSpec((HG, TOK, LAT), lambda i, s: (i, 0, 0)),
                pl.BlockSpec((LAT, HG * 2 * NOPE), lambda i, s: (0, i)),
                pl.BlockSpec((HG * NOPE, D), lambda i, s: (i, 0)),
                pl.BlockSpec((TOK, D), lambda i, s: (0, 0)),
                pl.BlockSpec((1, D), lambda i, s: (0, 0)),
            ],
            out_specs=[
                pl.BlockSpec((TOK, D), lambda i, s: (0, 0)),
                pl.BlockSpec((TOK, D), lambda i, s: (0, 0)),
            ],
            scratch_shapes=[pltpu.VMEM((TOK, D), f32)],
        ),
        name="project",
    )(scalars, o_lat, w_ukv, w_out, residual, gain)


def rank_table(ids_ref):
    expert = lax.broadcasted_iota(jnp.int32, (EXPERTS, TOK), 0)
    named = ids_ref[0:1, :] == expert
    for k in range(1, TOP):
        named = named | (ids_ref[k : k + 1, :] == expert)
    earlier = lax.broadcasted_iota(jnp.int32, (TOK, TOK), 0) < lax.broadcasted_iota(
        jnp.int32, (TOK, TOK), 1
    )
    rank = mm(jnp.where(named, 1.0, 0.0).astype(bf16), jnp.where(earlier, 1.0, 0.0).astype(bf16))
    return jnp.where(named, rank, -1.0)


def gate_table(ids_ref, gates_ref):
    expert = lax.broadcasted_iota(jnp.int32, (EXPERTS, TOK), 0)
    gates = jnp.zeros((EXPERTS, TOK), f32)
    for k in range(TOP):
        gates = gates + jnp.where(ids_ref[k : k + 1, :] == expert, gates_ref[k : k + 1, :], 0.0)
    return gates


def whole_rows(ranks, experts, copies, values=None):
    slot = lax.broadcasted_iota(jnp.int32, (SLOTS_A, TOK), 0).astype(f32)
    rows = []
    for e in range(experts):
        on = 1.0 if values is None else values[e : e + 1, :]
        rows += [jnp.where(ranks[e : e + 1, :] == slot, on, 0.0)] * copies
    return jnp.concatenate(rows, axis=0)


def packed_rows(ranks, experts, copies, values=None):
    row = lax.broadcasted_iota(jnp.int32, (8, TOK), 0)
    slot = (SLOTS_A + row // 2).astype(f32)
    even = row % 2 == 0
    lower, upper, last = [], [], []
    for e in range(experts):
        rank = ranks[e : e + 1, :]
        on = 1.0 if values is None else values[e : e + 1, :]
        hit = jnp.where(rank == slot, on, 0.0)
        lower += [jnp.where(even, hit, 0.0)] * copies
        upper += [jnp.where(even, 0.0, hit)] * copies
        last += [jnp.where(jnp.broadcast_to(rank, (8, TOK)) == CAP - 1.0, on, 0.0)] * copies
    return [jnp.concatenate(part, axis=0) for part in (lower, upper, last)]


def pieces_of(last):
    row = lax.broadcasted_iota(jnp.int32, last.shape, 0) % 8
    return [jnp.where(row == q, last, 0.0) for q in range(8)]


EG = 16


def dispatch_kernel(ids_ref, norm_ref, out_ref, rank_scr):
    step = pl.program_id(0)

    @pl.when(step == 0)
    def _():
        rank_scr[...] = rank_table(ids_ref)

    ranks = rank_scr[pl.ds(step * EG, EG), :]
    sent = mm(whole_rows(ranks, EG, 1).astype(bf16), norm_ref[...]).astype(bf16)
    for e in range(EG):
        part = sent[e * SLOTS_A : (e + 1) * SLOTS_A]
        out_ref[2 * e] = part
        out_ref[2 * e + 1] = part


def dispatch_packed_kernel(ids_ref, norm_ref, out_ref, rank_scr):
    step = pl.program_id(0)

    @pl.when(step == 0)
    def _():
        rank_scr[...] = rank_table(ids_ref)

    ranks = rank_scr[pl.ds(step * EG, EG), :]
    lower, upper, last = packed_rows(ranks, EG, 1)
    sent = (
        mm(lower.astype(bf16), norm_ref[:, :HALF]) + mm(upper.astype(bf16), norm_ref[:, HALF:])
    ).astype(bf16)
    tail = jnp.zeros((EG * 8, PIECE), f32)
    for q, piece in enumerate(pieces_of(last)):
        tail = tail + mm(piece.astype(bf16), norm_ref[:, q * PIECE : (q + 1) * PIECE])
    tail = tail.astype(bf16)
    for e in range(EG):
        for copy in range(2):
            out_ref[2 * e + copy, :, :HALF] = sent[e * 8 : (e + 1) * 8]
            out_ref[2 * e + copy, :, HALF:] = tail[e * 8 : (e + 1) * 8]


def dispatch(kernel, width, ids_t, normed):
    return pl.pallas_call(
        kernel,
        out_shape=jax.ShapeDtypeStruct((2 * EXPERTS, 8, width), bf16),
        grid=(EXPERTS // EG,),
        in_specs=[
            pl.BlockSpec((TOP, TOK), lambda i: (0, 0)),
            pl.BlockSpec((TOK, D), lambda i: (0, 0)),
        ],
        out_specs=pl.BlockSpec((2 * EG, 8, width), lambda i: (i, 0, 0)),
        scratch_shapes=[pltpu.VMEM((EXPERTS, TOK), f32)],
    )(ids_t, normed)


def expert_rows(x, wg_ref, wd_ref):
    gate_up = mm(x, wg_ref[0])
    half = gate_up.shape[1] // 2
    gate, up = gate_up[:, :half], gate_up[:, half:]
    act = (gate / (1.0 + jnp.exp(-gate)) * up).astype(bf16)
    return mm(act, wd_ref[0]).astype(bf16)


def expert_kernel(x_ref, wg_ref, wd_ref, out_ref):
    x = x_ref[...].reshape(-1, D)
    out_ref[...] = expert_rows(x, wg_ref, wd_ref).reshape(out_ref.shape)


def select(rows, columns, stride, offset):
    r = lax.broadcasted_iota(jnp.int32, (rows, columns), 0)
    c = lax.broadcasted_iota(jnp.int32, (rows, columns), 1)
    return jnp.where(c == r * stride + offset, 1.0, 0.0).astype(bf16)


def expert_packed_kernel(x_ref, wg_ref, wd_ref, out_ref):
    n = x_ref.shape[0]
    x = x_ref[...].reshape(8 * n, WIDTH_B)
    even, odd = select(4 * n, 8 * n, 2, 0), select(4 * n, 8 * n, 2, 1)
    each = [select(n, 8 * n, 8, q) for q in range(8)]
    main = jnp.concatenate([mm(even, x[:, :HALF]), mm(odd, x[:, :HALF])], axis=1)
    last = jnp.concatenate([mm(pick, x[:, HALF:]) for pick in each], axis=1)
    y = expert_rows(jnp.concatenate([main, last], axis=0).astype(bf16), wg_ref, wd_ref)
    main, last = y[: 4 * n], y[4 * n :]
    out = mm_tn(even, main[:, :HALF]) + mm_tn(odd, main[:, HALF:])
    tail = jnp.zeros((8 * n, PIECE), f32)
    for q, pick in enumerate(each):
        tail = tail + mm_tn(pick, last[:, q * PIECE : (q + 1) * PIECE])
    out_ref[:, :, :HALF] = out.astype(bf16).reshape(n, 8, HALF)
    out_ref[:, :, HALF:] = tail.astype(bf16).reshape(n, 8, PIECE)


def run_expert(kernel, rows, w_gate_up, w_down):
    width = rows.shape[2]
    per = 32
    return pl.pallas_call(
        kernel,
        out_shape=jax.ShapeDtypeStruct(rows.shape, bf16),
        grid=(rows.shape[0] // per,),
        in_specs=[
            pl.BlockSpec((per, 8, width), lambda i: (i, 0, 0)),
            pl.BlockSpec(w_gate_up.shape, lambda i: (0, 0, 0), pipeline_mode=pl.Buffered(1)),
            pl.BlockSpec(w_down.shape, lambda i: (0, 0, 0), pipeline_mode=pl.Buffered(1)),
        ],
        out_specs=pl.BlockSpec((per, 8, width), lambda i: (i, 0, 0)),
    )(rows, w_gate_up, w_down)


def weighted(weight, back):
    high = weight.astype(bf16)
    low = (weight - high.astype(f32)).astype(bf16)
    both = mm_tn(jnp.concatenate([high, low], axis=1), back)
    return both[:TOK] + both[TOK:]


def combine_kernel(ids_ref, gates_ref, hid_ref, back_ref, out_ref, rank_scr, gate_scr):
    step = pl.program_id(0)

    @pl.when(step == 0)
    def _():
        rank_scr[...] = rank_table(ids_ref)
        gate_scr[...] = gate_table(ids_ref, gates_ref)
        out_ref[...] = hid_ref[...].astype(f32)

    ranks = rank_scr[pl.ds(step * EG, EG), :]
    gates = gate_scr[pl.ds(step * EG, EG), :]
    back = back_ref[...].reshape(2 * EG * SLOTS_A, D)
    out_ref[...] += weighted(whole_rows(ranks, EG, 2, gates), back)


def combine_packed_kernel(
    ids_ref, gates_ref, sum_ref, back_ref, out_ref, rank_scr, gate_scr, acc_ref
):
    step = pl.program_id(0)

    @pl.when(step == 0)
    def _():
        rank_scr[...] = rank_table(ids_ref)
        gate_scr[...] = gate_table(ids_ref, gates_ref)
        acc_ref[...] = sum_ref[...]

    ranks = rank_scr[pl.ds(step * EG, EG), :]
    gates = gate_scr[pl.ds(step * EG, EG), :]
    back = back_ref[...].reshape(2 * EG * 8, WIDTH_B)
    lower, upper, last = packed_rows(ranks, EG, 2, gates)
    acc_ref[:, :HALF] += weighted(lower, back[:, :HALF])
    acc_ref[:, HALF:] += weighted(upper, back[:, :HALF])
    for q, piece in enumerate(pieces_of(last)):
        acc_ref[:, q * PIECE : (q + 1) * PIECE] += weighted(piece, back[:, HALF:])

    @pl.when(step == EXPERTS // EG - 1)
    def _():
        out_ref[...] = acc_ref[...].astype(bf16)


def combine(kernel, ids_t, gates_t, base, back, out_type):
    scratch = [pltpu.VMEM((EXPERTS, TOK), f32), pltpu.VMEM((EXPERTS, TOK), f32)]
    if out_type == bf16:
        scratch.append(pltpu.VMEM((TOK, D), f32))
    return pl.pallas_call(
        kernel,
        out_shape=jax.ShapeDtypeStruct((TOK, D), out_type),
        grid=(EXPERTS // EG,),
        in_specs=[
            pl.BlockSpec((TOP, TOK), lambda i: (0, 0)),
            pl.BlockSpec((TOP, TOK), lambda i: (0, 0)),
            pl.BlockSpec((TOK, D), lambda i: (0, 0)),
            pl.BlockSpec((2 * EG, 8, back.shape[2]), lambda i: (i, 0, 0)),
        ],
        out_specs=pl.BlockSpec((TOK, D), lambda i: (0, 0)),
        scratch_shapes=scratch,
    )(ids_t, gates_t, base, back)


def shift(axis, k):
    pairs = []
    for x in range(4):
        for y in range(4):
            tx, ty = ((x + k) % 4, y) if axis == "x" else (x, (y + k) % 4)
            pairs.append((x * 4 + y, tx * 4 + ty))
    return pairs


def hop(a, axis, k):
    return lax.ppermute(a, "wide", shift(axis, k))


def gather_row(own, first):
    ahead, behind = hop(own, first, 1), hop(own, first, -1)
    far = hop(own, first, 2)
    return jnp.concatenate([own, ahead, behind, far], axis=0)


def gather_rest(row, second):
    ahead, behind = hop(row, second, 1), hop(row, second, -1)
    far = hop(row, second, 2)
    return ahead, behind, far


def pack_prefix(latent, rope):
    packed = rope.reshape(4, 16, TOK).transpose(1, 0, 2).reshape(16, 4 * TOK)
    return jnp.concatenate([latent, packed], axis=0)


def exchange(a):
    return lax.all_to_all(a, ("req", "wide"), split_axis=0, concat_axis=0, tiled=True)


def layer(
    queries,
    suffix_latent,
    suffix_rope,
    residual,
    prefix_latent,
    prefix_rope,
    suffix_lengths,
    prefix_ids,
    w_ukv,
    w_out,
    norm_gain,
    expert_ids,
    gate_values,
    expert_gate_up,
    expert_down,
):
    scalars = jnp.concatenate([suffix_lengths[0], prefix_ids[0]])
    row0 = gather_row(pack_prefix(prefix_latent[0, 0], prefix_rope[0, 0]), "x")
    row1 = gather_row(pack_prefix(prefix_latent[0, 1], prefix_rope[0, 1]), "y")
    qa, qr = prepare_queries(scalars, queries, w_ukv)
    ahead0, behind0, far0 = gather_rest(row0, "y")
    ahead1, behind1, far1 = gather_rest(row1, "x")
    state = attend(FIRST, scalars, qa, qr, (suffix_latent, suffix_rope), [row0], [row1])
    state = attend(MIDDLE, scalars, qa, qr, state, [ahead0, behind0], [ahead1, behind1])
    o_lat = attend(LAST, scalars, qa, qr, state, [far0], [far1])
    hidden, normed = project(scalars, o_lat, w_ukv, w_out, residual, norm_gain.reshape(1, D))
    ids_t = expert_ids.T
    gates_t = gate_values.T
    sent_a = dispatch(dispatch_kernel, D, ids_t, normed)
    sent_b = dispatch(dispatch_packed_kernel, WIDTH_B, ids_t, normed)
    rows_a = exchange(sent_a)
    rows_b = exchange(sent_b)
    made_a = run_expert(expert_kernel, rows_a, expert_gate_up, expert_down)
    made_b = run_expert(expert_packed_kernel, rows_b, expert_gate_up, expert_down)
    back_a = exchange(made_a)
    back_b = exchange(made_b)
    part = combine(combine_kernel, ids_t, gates_t, hidden, back_a, f32)
    return combine(combine_packed_kernel, ids_t, gates_t, part, back_b, bf16)


def solution(mesh):
    return jax.shard_map(
        layer,
        mesh=mesh,
        in_specs=(
            P(("req", "wide"), None),
            P(("req", "wide"), None),
            P(None, ("req", "wide")),
            P(("req", "wide"), None),
            P("req", None, "wide", None),
            P("req", None, None, "wide"),
            P(("req", "wide"), None),
            P(("req", "wide"), None),
            P(),
            P(),
            P(),
            P(("req", "wide"), None),
            P(("req", "wide"), None),
            P(("req", "wide"), None, None),
            P(("req", "wide"), None, None),
        ),
        out_specs=P(("req", "wide"), None),
        check_vma=False,
    )
```

```python
import jax
import jax.numpy as jnp
from jax import lax
from jax.experimental import pallas as pl
from jax.experimental.pallas import tpu as pltpu
from jax.sharding import PartitionSpec as P


D = 2048
HEADS = 16
NOPE = 128
ROPE = 64
LAT = 512
TOP = 6
PREF = 2
EXPERTS = 64
TOK = 128
REQS = 4
TILE = 16
CAP = 13
SLOTS_A = 8
HALF = D // 2
PIECE = D // 8
WIDTH_B = HALF + PIECE
BLK = 144
EPS = 1e-06
SCALE = 1.0 / (NOPE + ROPE) ** 0.5
LOG2E = 1.4426950408889634
NEG = -1e30
bf16 = jnp.bfloat16
f32 = jnp.float32


def request_scalars(sc_ref):
    lens = [sc_ref[r] for r in range(REQS)]
    own = [sc_ref[REQS + r] for r in range(REQS)]
    starts, total = [], 0
    for r in range(REQS):
        starts.append(total)
        total = total + lens[r]
    zero_count = sum(jnp.where(own[r] == 0, lens[r], 0) for r in range(REQS))
    bases, next0, next1 = [], 0, zero_count
    for r in range(REQS):
        is0 = own[r] == 0
        bases.append(jnp.where(is0, next0, next1))
        next0 = next0 + jnp.where(is0, lens[r], 0)
        next1 = next1 + jnp.where(is0, 0, lens[r])
    return lens, starts, bases, zero_count


def place_of(tokens, starts, bases):
    place = tokens - starts[0] + bases[0]
    for r in range(1, REQS):
        place = jnp.where(tokens >= starts[r], tokens - starts[r] + bases[r], place)
    return place


def sort_matrix(sc_ref, transposed):
    _, starts, bases, _ = request_scalars(sc_ref)
    token_dim = 0 if transposed else 1
    tokens = lax.broadcasted_iota(jnp.int32, (TOK, TOK), token_dim)
    slots = lax.broadcasted_iota(jnp.int32, (TOK, TOK), 1 - token_dim)
    return jnp.where(place_of(tokens, starts, bases) == slots, 1.0, 0.0).astype(bf16)


def mm(a, b):
    return jnp.dot(a, b, preferred_element_type=f32)


def mm_nt(a, b):
    return lax.dot_general(a, b, (((1,), (1,)), ((), ())), preferred_element_type=f32)


def mm_tn(a, b):
    return lax.dot_general(a, b, (((0,), (0,)), ((), ())), preferred_element_type=f32)


HG = 4


def query_kernel(sc_ref, q_ref, qr_ref, w_ref, qa_ref, qo_ref):
    order = sort_matrix(sc_ref, False)
    nope = mm(order, q_ref[...]).astype(bf16)
    rope = mm(order, qr_ref[...]).astype(bf16)
    for h in range(HG):
        keys = w_ref[:, h * 256 : h * 256 + 128]
        qa_ref[h] = mm_nt(nope[:, h * 128 : (h + 1) * 128], keys).astype(bf16)
        qo_ref[h] = rope[:, h * ROPE : (h + 1) * ROPE]


def prepare_queries(scalars, queries, w_ukv):
    return pl.pallas_call(
        query_kernel,
        out_shape=(
            jax.ShapeDtypeStruct((HEADS, TOK, LAT), bf16),
            jax.ShapeDtypeStruct((HEADS, TOK, ROPE), bf16),
        ),
        grid_spec=pltpu.PrefetchScalarGridSpec(
            num_scalar_prefetch=1,
            grid=(HEADS // HG,),
            in_specs=[
                pl.BlockSpec((TOK, HG * NOPE), lambda i, s: (0, i)),
                pl.BlockSpec((TOK, HG * ROPE), lambda i, s: (0, HEADS * NOPE // (HG * ROPE) + i)),
                pl.BlockSpec((LAT, HG * 2 * NOPE), lambda i, s: (0, i)),
            ],
            out_specs=[
                pl.BlockSpec((HG, TOK, LAT), lambda i, s: (i, 0, 0)),
                pl.BlockSpec((HG, TOK, ROPE), lambda i, s: (i, 0, 0)),
            ],
        ),
        name="query_prep",
    )(scalars, queries, queries, w_ukv)


ROWS = HEADS * TILE


def block_views(refs):
    views = []
    for ref in refs:
        for b in range(ref.shape[0] // BLK):
            views.append((ref, b * BLK))
    return views


def attention_kernel(n_pieces, sc_ref, qa_ref, qr_ref, ll_ref, lr_ref, *rest):
    pieces = (rest[:n_pieces], rest[n_pieces : 2 * n_pieces])
    o_ref, s_scr, m_scr, l_scr, acc_scr = rest[2 * n_pieces :]
    lens, starts, bases, zero_count = request_scalars(sc_ref)
    first = pl.program_id(0) * TILE
    c = SCALE * LOG2E
    q = qa_ref[...].reshape(ROWS, LAT)
    qr = qr_ref[...].reshape(ROWS, ROPE)

    places = first + lax.broadcasted_iota(jnp.int32, (TILE, TOK), 0)
    keys_at = lax.broadcasted_iota(jnp.int32, (TILE, TOK), 1)
    bias = jnp.full((TILE, TOK), NEG, f32)
    for r in range(REQS):
        mine = (places >= bases[r]) & (places < bases[r] + lens[r])
        tok = places - bases[r] + starts[r]
        ok = mine & (keys_at >= starts[r]) & (keys_at <= tok)
        bias = jnp.where(ok, 0.0, bias)
    local_lat = ll_ref[...]
    s = mm_nt(q, local_lat) + mm(qr, lr_ref[...])
    s = (s.reshape(HEADS, TILE, TOK) + bias[None]).reshape(ROWS, TOK)
    m = jnp.max(s, axis=1, keepdims=True)
    p = jnp.exp2((s - m) * c)
    m_scr[...] = jnp.broadcast_to(m, (ROWS, 128))
    l_scr[...] = jnp.broadcast_to(jnp.sum(p, axis=1, keepdims=True), (ROWS, 128))
    acc_scr[...] = mm(p.astype(bf16), local_lat)

    for pre in range(PREF):
        needed = (first < zero_count) if pre == 0 else (first + TILE > zero_count)

        @pl.when(needed)
        def _(pre=pre):
            views = block_views(pieces[pre])
            place = first + lax.broadcasted_iota(jnp.int32, (ROWS, 1), 0) % TILE
            mine = (place < zero_count) if pre == 0 else (place >= zero_count)
            row_bias = jnp.where(mine, 0.0, NEG)
            per = 4
            chunks = [views[k : k + per] for k in range(0, len(views), per)]
            m_old = m_scr[:, :1]
            m_new = m_old
            for k, chunk in enumerate(chunks):
                lat = jnp.concatenate([ref[at : at + 128, :] for ref, at in chunk], axis=0)
                rope = jnp.concatenate(
                    [
                        jnp.concatenate(
                            [ref[at + 128 : at + 144, j * 128 : (j + 1) * 128] for j in range(4)],
                            axis=0,
                        )
                        for ref, at in chunk
                    ],
                    axis=1,
                )
                s = mm_nt(q, lat) + mm(qr, rope) + row_bias
                s_scr[k] = s
                m_new = jnp.maximum(m_new, jnp.max(s, axis=1, keepdims=True))
            scale_old = jnp.exp2((m_old - m_new) * c)
            total = l_scr[:, :1] * scale_old
            acc = acc_scr[...] * scale_old
            for k, chunk in enumerate(chunks):
                lat = jnp.concatenate([ref[at : at + 128, :] for ref, at in chunk], axis=0)
                p = jnp.exp2((s_scr[k] - m_new) * c)
                total = total + jnp.sum(p, axis=1, keepdims=True)
                acc = acc + mm(p.astype(bf16), lat)
            m_scr[...] = jnp.broadcast_to(m_new, (ROWS, 128))
            l_scr[...] = jnp.broadcast_to(total, (ROWS, 128))
            acc_scr[...] = acc

    out = acc_scr[...] / l_scr[:, :1]
    o_ref[...] = out.astype(bf16).reshape(HEADS, TILE, LAT)


def attend(scalars, qa, qr, local_lat, local_rope, pieces0, pieces1):
    n_pieces = len(pieces0)
    whole = lambda a: pl.BlockSpec(a.shape, lambda i, s: (0,) * a.ndim)
    pieces = [*pieces0, *pieces1]
    return pl.pallas_call(
        lambda *refs: attention_kernel(n_pieces, *refs),
        out_shape=jax.ShapeDtypeStruct((HEADS, TOK, LAT), bf16),
        grid_spec=pltpu.PrefetchScalarGridSpec(
            num_scalar_prefetch=1,
            grid=(TOK // TILE,),
            in_specs=[
                pl.BlockSpec((HEADS, TILE, LAT), lambda i, s: (0, i, 0)),
                pl.BlockSpec((HEADS, TILE, ROPE), lambda i, s: (0, i, 0)),
                whole(local_lat),
                whole(local_rope),
                *[pl.BlockSpec(memory_space=pltpu.VMEM) for _ in pieces],
            ],
            out_specs=pl.BlockSpec((HEADS, TILE, LAT), lambda i, s: (0, i, 0)),
            scratch_shapes=[
                pltpu.VMEM((4, ROWS, 512), f32),
                pltpu.VMEM((ROWS, 128), f32),
                pltpu.VMEM((ROWS, 128), f32),
                pltpu.VMEM((ROWS, LAT), f32),
            ],
        ),
        name="attention",
    )(scalars, qa, qr, local_lat, local_rope, *pieces)


def project_kernel(sc_ref, o_ref, w_ref, wo_ref, res_ref, gain_ref, hid_ref, norm_ref, acc_ref):
    step = pl.program_id(0)

    @pl.when(step == 0)
    def _():
        acc_ref[...] = res_ref[...].astype(f32)

    back = sort_matrix(sc_ref, True)
    heads = [mm(o_ref[h], w_ref[:, h * 256 + 128 : h * 256 + 256]).astype(bf16) for h in range(HG)]
    head_out = mm(back, jnp.concatenate(heads, axis=1)).astype(bf16)
    acc_ref[...] += mm(head_out, wo_ref[...])

    @pl.when(step == HEADS // HG - 1)
    def _():
        hidden = acc_ref[...].astype(bf16)
        hid_ref[...] = hidden
        h32 = hidden.astype(f32)
        inverse = lax.rsqrt(jnp.mean(h32 * h32, axis=1, keepdims=True) + EPS)
        norm_ref[...] = (h32 * inverse * gain_ref[...].astype(f32)).astype(bf16)


def project(scalars, o_lat, w_ukv, w_out, residual, gain):
    return pl.pallas_call(
        project_kernel,
        out_shape=(
            jax.ShapeDtypeStruct((TOK, D), bf16),
            jax.ShapeDtypeStruct((TOK, D), bf16),
        ),
        grid_spec=pltpu.PrefetchScalarGridSpec(
            num_scalar_prefetch=1,
            grid=(HEADS // HG,),
            in_specs=[
                pl.BlockSpec((HG, TOK, LAT), lambda i, s: (i, 0, 0)),
                pl.BlockSpec((LAT, HG * 2 * NOPE), lambda i, s: (0, i)),
                pl.BlockSpec((HG * NOPE, D), lambda i, s: (i, 0)),
                pl.BlockSpec((TOK, D), lambda i, s: (0, 0)),
                pl.BlockSpec((1, D), lambda i, s: (0, 0)),
            ],
            out_specs=[
                pl.BlockSpec((TOK, D), lambda i, s: (0, 0)),
                pl.BlockSpec((TOK, D), lambda i, s: (0, 0)),
            ],
            scratch_shapes=[pltpu.VMEM((TOK, D), f32)],
        ),
        name="project",
    )(scalars, o_lat, w_ukv, w_out, residual, gain)


def rank_table(ids_ref):
    expert = lax.broadcasted_iota(jnp.int32, (EXPERTS, TOK), 0)
    named = ids_ref[0:1, :] == expert
    for k in range(1, TOP):
        named = named | (ids_ref[k : k + 1, :] == expert)
    earlier = lax.broadcasted_iota(jnp.int32, (TOK, TOK), 0) < lax.broadcasted_iota(
        jnp.int32, (TOK, TOK), 1
    )
    rank = mm(jnp.where(named, 1.0, 0.0).astype(bf16), jnp.where(earlier, 1.0, 0.0).astype(bf16))
    return jnp.where(named, rank, -1.0)


def gate_table(ids_ref, gates_ref):
    expert = lax.broadcasted_iota(jnp.int32, (EXPERTS, TOK), 0)
    gates = jnp.zeros((EXPERTS, TOK), f32)
    for k in range(TOP):
        gates = gates + jnp.where(ids_ref[k : k + 1, :] == expert, gates_ref[k : k + 1, :], 0.0)
    return gates


def whole_rows(ranks, experts, copies, values=None):
    slot = lax.broadcasted_iota(jnp.int32, (SLOTS_A, TOK), 0).astype(f32)
    rows = []
    for e in range(experts):
        on = 1.0 if values is None else values[e : e + 1, :]
        rows += [jnp.where(ranks[e : e + 1, :] == slot, on, 0.0)] * copies
    return jnp.concatenate(rows, axis=0)


def packed_rows(ranks, experts, copies, values=None):
    row = lax.broadcasted_iota(jnp.int32, (8, TOK), 0)
    slot = (SLOTS_A + row // 2).astype(f32)
    even = row % 2 == 0
    lower, upper, last = [], [], []
    for e in range(experts):
        rank = ranks[e : e + 1, :]
        on = 1.0 if values is None else values[e : e + 1, :]
        hit = jnp.where(rank == slot, on, 0.0)
        lower += [jnp.where(even, hit, 0.0)] * copies
        upper += [jnp.where(even, 0.0, hit)] * copies
        last += [jnp.where(jnp.broadcast_to(rank, (8, TOK)) == CAP - 1.0, on, 0.0)] * copies
    return [jnp.concatenate(part, axis=0) for part in (lower, upper, last)]


def pieces_of(last):
    row = lax.broadcasted_iota(jnp.int32, last.shape, 0) % 8
    return [jnp.where(row == q, last, 0.0) for q in range(8)]


EG = 16


def dispatch_kernel(ids_ref, norm_ref, out_ref, rank_scr):
    step = pl.program_id(0)

    @pl.when(step == 0)
    def _():
        rank_scr[...] = rank_table(ids_ref)

    ranks = rank_scr[pl.ds(step * EG, EG), :]
    sent = mm(whole_rows(ranks, EG, 1).astype(bf16), norm_ref[...]).astype(bf16)
    for e in range(EG):
        part = sent[e * SLOTS_A : (e + 1) * SLOTS_A]
        out_ref[2 * e] = part
        out_ref[2 * e + 1] = part


def dispatch_packed_kernel(ids_ref, norm_ref, out_ref, rank_scr):
    step = pl.program_id(0)

    @pl.when(step == 0)
    def _():
        rank_scr[...] = rank_table(ids_ref)

    ranks = rank_scr[pl.ds(step * EG, EG), :]
    lower, upper, last = packed_rows(ranks, EG, 1)
    sent = (
        mm(lower.astype(bf16), norm_ref[:, :HALF]) + mm(upper.astype(bf16), norm_ref[:, HALF:])
    ).astype(bf16)
    tail = jnp.zeros((EG * 8, PIECE), f32)
    for q, piece in enumerate(pieces_of(last)):
        tail = tail + mm(piece.astype(bf16), norm_ref[:, q * PIECE : (q + 1) * PIECE])
    tail = tail.astype(bf16)
    for e in range(EG):
        for copy in range(2):
            out_ref[2 * e + copy, :, :HALF] = sent[e * 8 : (e + 1) * 8]
            out_ref[2 * e + copy, :, HALF:] = tail[e * 8 : (e + 1) * 8]


def dispatch(kernel, width, ids_t, normed):
    return pl.pallas_call(
        kernel,
        out_shape=jax.ShapeDtypeStruct((2 * EXPERTS, 8, width), bf16),
        grid=(EXPERTS // EG,),
        in_specs=[
            pl.BlockSpec((TOP, TOK), lambda i: (0, 0)),
            pl.BlockSpec((TOK, D), lambda i: (0, 0)),
        ],
        out_specs=pl.BlockSpec((2 * EG, 8, width), lambda i: (i, 0, 0)),
        scratch_shapes=[pltpu.VMEM((EXPERTS, TOK), f32)],
    )(ids_t, normed)


def activate(x, wg_ref):
    gate_up = mm(x, wg_ref[0])
    gate, up = gate_up[:, :HIDDEN], gate_up[:, HIDDEN:]
    return gate / (1.0 + jnp.exp(-gate)) * up


def up_kernel(side_ref, x_ref, wg_ref, own_ref, other_ref):
    n = x_ref.shape[0] // 2
    act = activate(x_ref[...].reshape(-1, D), wg_ref).reshape(n, 2, 8, HIDDEN)
    even = side_ref[0] == 0
    own_ref[...] = jnp.where(even, act[:, 0], act[:, 1]).astype(bf16)
    other_ref[...] = jnp.where(even, act[:, 1], act[:, 0]).astype(bf16)


def pick(rows, columns, stride, offset):
    r = lax.broadcasted_iota(jnp.int32, (rows, columns), 0)
    c = lax.broadcasted_iota(jnp.int32, (rows, columns), 1)
    return jnp.where(c == r * stride + offset, 1.0, 0.0).astype(bf16)


def pick_main(n, side, half):
    r = lax.broadcasted_iota(jnp.int32, (4 * n, 16 * n), 0)
    c = lax.broadcasted_iota(jnp.int32, (4 * n, 16 * n), 1)
    at = (2 * (r // 4) + side) * 8 + 2 * (r % 4) + half
    return jnp.where(c == at, 1.0, 0.0).astype(bf16)


def up_packed_kernel(side_ref, x_ref, wg_ref, own_ref, other_ref):
    n = x_ref.shape[0] // 2
    x = x_ref[...].reshape(16 * n, WIDTH_B)
    wide, tail = x[:, :HALF], x[:, HALF:]
    own, other = side_ref[0], 1 - side_ref[0]
    halves = [
        mm(jnp.concatenate([pick_main(n, own, h), pick_main(n, other, h)], axis=0), wide)
        for h in range(2)
    ]
    main = jnp.concatenate(halves, axis=1)
    parts = []
    for q in range(8):
        chosen = [pick(n, 16 * n, 16, 8 * own + q), pick(n, 16 * n, 16, 8 * other + q)]
        parts.append(mm(jnp.concatenate(chosen, axis=0), tail))
    last = jnp.concatenate(parts, axis=1)
    act = activate(jnp.concatenate([main, last], axis=0).astype(bf16), wg_ref).astype(bf16)
    own_ref[0, : 4 * n] = act[: 4 * n]
    own_ref[0, 4 * n :] = act[8 * n : 9 * n]
    other_ref[0, : 4 * n] = act[4 * n : 8 * n]
    other_ref[0, 4 * n :] = act[9 * n :]


PER = 16
HIDDEN = 704


def run_up(kernel, side, rows, w_gate_up):
    width = rows.shape[2]
    steps = rows.shape[0] // (2 * PER)
    if width == D:
        shape, block = (PER * steps, 8, HIDDEN), (PER, 8, HIDDEN)
    else:
        shape, block = (steps, 5 * PER, HIDDEN), (1, 5 * PER, HIDDEN)
    return pl.pallas_call(
        kernel,
        out_shape=(jax.ShapeDtypeStruct(shape, bf16),) * 2,
        grid_spec=pltpu.PrefetchScalarGridSpec(
            num_scalar_prefetch=1,
            grid=(steps,),
            in_specs=[
                pl.BlockSpec((2 * PER, 8, width), lambda i, s: (i, 0, 0)),
                pl.BlockSpec(
                    w_gate_up.shape, lambda i, s: (0, 0, 0), pipeline_mode=pl.Buffered(1)
                ),
            ],
            out_specs=[pl.BlockSpec(block, lambda i, s: (i, 0, 0))] * 2,
        ),
    )(side, rows, w_gate_up)


def down_kernel(own_ref, came_ref, wo_ref, wc_ref, out_ref):
    own = own_ref[...].reshape(-1, HIDDEN)
    came = came_ref[...].reshape(-1, HIDDEN)
    out = mm(own, wo_ref[0]) + mm(came, wc_ref[0])
    out_ref[...] = out.astype(bf16).reshape(out_ref.shape)


def down_packed_kernel(own_ref, came_ref, wo_ref, wc_ref, out_ref):
    n = out_ref.shape[0]
    y = (mm(own_ref[0], wo_ref[0]) + mm(came_ref[0], wc_ref[0])).astype(bf16)
    main, last = y[: 4 * n], y[4 * n :]
    even, odd = pick(4 * n, 8 * n, 2, 0), pick(4 * n, 8 * n, 2, 1)
    out = mm_tn(even, main[:, :HALF]) + mm_tn(odd, main[:, HALF:])
    tail = jnp.zeros((8 * n, PIECE), f32)
    for q in range(8):
        tail = tail + mm_tn(pick(n, 8 * n, 8, q), last[:, q * PIECE : (q + 1) * PIECE])
    out_ref[:, :, :HALF] = out.astype(bf16).reshape(n, 8, HALF)
    out_ref[:, :, HALF:] = tail.astype(bf16).reshape(n, 8, PIECE)


def run_down(kernel, own, came, w_own, w_came, width):
    blocks = 2 if width == D else 1
    steps = EXPERTS // PER // blocks
    act = pl.BlockSpec((own.shape[0] // steps, *own.shape[1:]), lambda i: (i, 0, 0))
    weight = pl.BlockSpec(w_own.shape, lambda i: (0, 0, 0), pipeline_mode=pl.Buffered(1))
    return pl.pallas_call(
        kernel,
        out_shape=jax.ShapeDtypeStruct((EXPERTS, 8, width), bf16),
        grid=(steps,),
        in_specs=[act, act, weight, weight],
        out_specs=pl.BlockSpec((EXPERTS // steps, 8, width), lambda i: (i, 0, 0)),
    )(own, came, w_own, w_came)


def weighted(weight, back):
    high = weight.astype(bf16)
    low = (weight - high.astype(f32)).astype(bf16)
    both = mm_tn(jnp.concatenate([high, low], axis=1), back)
    return both[:TOK] + both[TOK:]


CG = 32


def combine_kernel(ids_ref, gates_ref, hid_ref, back_ref, out_ref, rank_scr, gate_scr):
    step = pl.program_id(0)

    @pl.when(step == 0)
    def _():
        rank_scr[...] = rank_table(ids_ref)
        gate_scr[...] = gate_table(ids_ref, gates_ref)
        out_ref[...] = hid_ref[...].astype(f32)

    ranks = rank_scr[pl.ds(step * CG, CG), :]
    gates = gate_scr[pl.ds(step * CG, CG), :]
    back = back_ref[...].reshape(CG * SLOTS_A, D)
    out_ref[...] += weighted(whole_rows(ranks, CG, 1, gates), back)


def combine(ids_t, gates_t, hidden, back):
    return pl.pallas_call(
        combine_kernel,
        out_shape=jax.ShapeDtypeStruct((TOK, D), f32),
        grid=(EXPERTS // CG,),
        in_specs=[
            pl.BlockSpec((TOP, TOK), lambda i: (0, 0)),
            pl.BlockSpec((TOP, TOK), lambda i: (0, 0)),
            pl.BlockSpec((TOK, D), lambda i: (0, 0)),
            pl.BlockSpec((CG, 8, D), lambda i: (i, 0, 0)),
        ],
        out_specs=pl.BlockSpec((TOK, D), lambda i: (0, 0)),
        scratch_shapes=[pltpu.VMEM((EXPERTS, TOK), f32), pltpu.VMEM((EXPERTS, TOK), f32)],
        name="combine_a",
    )(ids_t, gates_t, hidden, back)


def combine_packed_kernel(ids_ref, gates_ref, sum_ref, back_ref, out_ref, acc_ref):
    ranks = rank_table(ids_ref)
    gates = gate_table(ids_ref, gates_ref)
    back = back_ref[...].reshape(EXPERTS * 8, WIDTH_B)
    lower, upper, last = packed_rows(ranks, EXPERTS, 1, gates)
    acc_ref[:, :HALF] = sum_ref[:, :HALF] + weighted(lower, back[:, :HALF])
    acc_ref[:, HALF:] = sum_ref[:, HALF:] + weighted(upper, back[:, :HALF])
    for q, piece in enumerate(pieces_of(last)):
        acc_ref[:, q * PIECE : (q + 1) * PIECE] += weighted(piece, back[:, HALF:])
    out_ref[...] = acc_ref[...].astype(bf16)


def combine_packed(ids_t, gates_t, base, back):
    return pl.pallas_call(
        combine_packed_kernel,
        out_shape=jax.ShapeDtypeStruct((TOK, D), bf16),
        in_specs=[pl.BlockSpec(memory_space=pltpu.VMEM)] * 4,
        out_specs=pl.BlockSpec(memory_space=pltpu.VMEM),
        scratch_shapes=[pltpu.VMEM((TOK, D), f32)],
        name="combine_b",
    )(ids_t, gates_t, base, back)


def shift(axis, k):
    pairs = []
    for x in range(4):
        for y in range(4):
            tx, ty = ((x + k) % 4, y) if axis == "x" else (x, (y + k) % 4)
            pairs.append((x * 4 + y, tx * 4 + ty))
    return pairs


def hop(a, axis, k):
    return lax.ppermute(a, "wide", shift(axis, k))


def gather_row(own, first):
    ahead, behind = hop(own, first, 1), hop(own, first, -1)
    far = hop(own, first, 2)
    return jnp.concatenate([own, ahead, behind, far], axis=0)


def gather_rest(row, second):
    ahead, behind = hop(row, second, 1), hop(row, second, -1)
    far = hop(row, second, 2)
    return [row, ahead, behind, far]


def swap(a):
    return lax.ppermute(a, "wide", [(w, w ^ 1) for w in range(16)])


def pack_prefix(latent, rope):
    packed = rope.reshape(4, 16, TOK).transpose(1, 0, 2).reshape(16, 4 * TOK)
    return jnp.concatenate([latent, packed], axis=0)


def exchange(a):
    return lax.all_to_all(a, ("req", "wide"), split_axis=0, concat_axis=0, tiled=True)


def give_back(a):
    sides = [list(range(side, 2 * EXPERTS, 2)) for side in range(2)]
    return lax.all_to_all(
        a, ("req", "wide"), split_axis=0, concat_axis=0, axis_index_groups=sides, tiled=True
    )


def layer(
    queries,
    suffix_latent,
    suffix_rope,
    residual,
    prefix_latent,
    prefix_rope,
    suffix_lengths,
    prefix_ids,
    w_ukv,
    w_out,
    norm_gain,
    expert_ids,
    gate_values,
    expert_gate_up,
    expert_down,
):
    scalars = jnp.concatenate([suffix_lengths[0], prefix_ids[0]])
    row0 = gather_row(pack_prefix(prefix_latent[0, 0], prefix_rope[0, 0]), "x")
    row1 = gather_row(pack_prefix(prefix_latent[0, 1], prefix_rope[0, 1]), "y")
    pieces0 = gather_rest(row0, "y")
    pieces1 = gather_rest(row1, "x")
    down_came = swap(expert_down)
    side = (lax.axis_index("wide") % 2).reshape(1)
    qa, qr = prepare_queries(scalars, queries, w_ukv)
    o_lat = attend(scalars, qa, qr, suffix_latent, suffix_rope, pieces0, pieces1)
    hidden, normed = project(scalars, o_lat, w_ukv, w_out, residual, norm_gain.reshape(1, D))
    ids_t = expert_ids.T
    gates_t = gate_values.T
    sent_a = dispatch(dispatch_kernel, D, ids_t, normed)
    sent_b = dispatch(dispatch_packed_kernel, WIDTH_B, ids_t, normed)
    rows_a = exchange(sent_a)
    rows_b = exchange(sent_b)
    own_a, other_a = run_up(up_kernel, side, rows_a, expert_gate_up)
    came_a = swap(other_a)
    made_a = run_down(down_kernel, own_a, came_a, expert_down, down_came, D)
    own_b, other_b = run_up(up_packed_kernel, side, rows_b, expert_gate_up)
    came_b = swap(other_b)
    made_b = run_down(down_packed_kernel, own_b, came_b, expert_down, down_came, WIDTH_B)
    back_a = give_back(made_a)
    back_b = give_back(made_b)
    part = combine(ids_t, gates_t, hidden, back_a)
    return combine_packed(ids_t, gates_t, part, back_b)


def solution(mesh):
    return jax.shard_map(
        layer,
        mesh=mesh,
        in_specs=(
            P(("req", "wide"), None),
            P(("req", "wide"), None),
            P(None, ("req", "wide")),
            P(("req", "wide"), None),
            P("req", None, "wide", None),
            P("req", None, None, "wide"),
            P(("req", "wide"), None),
            P(("req", "wide"), None),
            P(),
            P(),
            P(),
            P(("req", "wide"), None),
            P(("req", "wide"), None),
            P(("req", "wide"), None, None),
            P(("req", "wide"), None, None),
        ),
        out_specs=P(("req", "wide"), None),
        check_vma=False,
    )
```

```python
import jax
import jax.numpy as jnp
from jax import lax
from jax.experimental import pallas as pl
from jax.experimental.pallas import tpu as pltpu
from jax.sharding import PartitionSpec as P


D = 2048
HEADS = 16
NOPE = 128
ROPE = 64
LAT = 512
TOP = 6
PREF = 2
EXPERTS = 64
TOK = 128
REQS = 4
TILE = 16
CAP = 13
SLOTS_A = 8
HALF = D // 2
PIECE = D // 8
WIDTH_B = HALF + PIECE
BLK = 144
EPS = 1e-06
SCALE = 1.0 / (NOPE + ROPE) ** 0.5
LOG2E = 1.4426950408889634
NEG = -1e30
bf16 = jnp.bfloat16
f32 = jnp.float32


def request_scalars(sc_ref):
    lens = [sc_ref[r] for r in range(REQS)]
    own = [sc_ref[REQS + r] for r in range(REQS)]
    starts, total = [], 0
    for r in range(REQS):
        starts.append(total)
        total = total + lens[r]
    zero_count = sum(jnp.where(own[r] == 0, lens[r], 0) for r in range(REQS))
    bases, next0, next1 = [], 0, zero_count
    for r in range(REQS):
        is0 = own[r] == 0
        bases.append(jnp.where(is0, next0, next1))
        next0 = next0 + jnp.where(is0, lens[r], 0)
        next1 = next1 + jnp.where(is0, 0, lens[r])
    return lens, starts, bases, zero_count


def place_of(tokens, starts, bases):
    place = tokens - starts[0] + bases[0]
    for r in range(1, REQS):
        place = jnp.where(tokens >= starts[r], tokens - starts[r] + bases[r], place)
    return place


def sort_matrix(sc_ref, transposed):
    _, starts, bases, _ = request_scalars(sc_ref)
    token_dim = 0 if transposed else 1
    tokens = lax.broadcasted_iota(jnp.int32, (TOK, TOK), token_dim)
    slots = lax.broadcasted_iota(jnp.int32, (TOK, TOK), 1 - token_dim)
    return jnp.where(place_of(tokens, starts, bases) == slots, 1.0, 0.0).astype(bf16)


def grant(mib):
    return pltpu.CompilerParams(vmem_limit_bytes=mib << 20)


def mm(a, b):
    return jnp.dot(a, b, preferred_element_type=f32)


def mm_nt(a, b):
    return lax.dot_general(a, b, (((1,), (1,)), ((), ())), preferred_element_type=f32)


def mm_tn(a, b):
    return lax.dot_general(a, b, (((0,), (0,)), ((), ())), preferred_element_type=f32)


HG = 4


def query_kernel(sc_ref, q_ref, qr_ref, w_ref, qa_ref, qo_ref):
    order = sort_matrix(sc_ref, False)
    nope = mm(order, q_ref[...]).astype(bf16)
    rope = mm(order, qr_ref[...]).astype(bf16)
    for h in range(HG):
        keys = w_ref[:, h * 256 : h * 256 + 128]
        qa_ref[h] = mm_nt(nope[:, h * 128 : (h + 1) * 128], keys).astype(bf16)
        qo_ref[h] = rope[:, h * ROPE : (h + 1) * ROPE]


def prepare_queries(scalars, queries, w_ukv):
    return pl.pallas_call(
        query_kernel,
        out_shape=(
            jax.ShapeDtypeStruct((HEADS, TOK, LAT), bf16),
            jax.ShapeDtypeStruct((HEADS, TOK, ROPE), bf16),
        ),
        grid_spec=pltpu.PrefetchScalarGridSpec(
            num_scalar_prefetch=1,
            grid=(HEADS // HG,),
            in_specs=[
                pl.BlockSpec((TOK, HG * NOPE), lambda i, s: (0, i)),
                pl.BlockSpec((TOK, HG * ROPE), lambda i, s: (0, HEADS * NOPE // (HG * ROPE) + i)),
                pl.BlockSpec((LAT, HG * 2 * NOPE), lambda i, s: (0, i)),
            ],
            out_specs=[
                pl.BlockSpec((HG, TOK, LAT), lambda i, s: (i, 0, 0)),
                pl.BlockSpec((HG, TOK, ROPE), lambda i, s: (i, 0, 0)),
            ],
        ),
        name="query_prep",
        compiler_params=grant(24),
    )(scalars, queries, queries, w_ukv)


ROWS = HEADS * TILE


def block_views(refs):
    views = []
    for ref in refs:
        for b in range(ref.shape[0] // BLK):
            views.append((ref, b * BLK))
    return views


def attention_kernel(n_pieces, sc_ref, qa_ref, qr_ref, ll_ref, lr_ref, *rest):
    pieces = (rest[:n_pieces], rest[n_pieces : 2 * n_pieces])
    o_ref, s_scr, m_scr, l_scr, acc_scr = rest[2 * n_pieces :]
    lens, starts, bases, zero_count = request_scalars(sc_ref)
    first = pl.program_id(0) * TILE
    c = SCALE * LOG2E
    q = qa_ref[...].reshape(ROWS, LAT)
    qr = qr_ref[...].reshape(ROWS, ROPE)

    places = first + lax.broadcasted_iota(jnp.int32, (TILE, TOK), 0)
    keys_at = lax.broadcasted_iota(jnp.int32, (TILE, TOK), 1)
    bias = jnp.full((TILE, TOK), NEG, f32)
    for r in range(REQS):
        mine = (places >= bases[r]) & (places < bases[r] + lens[r])
        tok = places - bases[r] + starts[r]
        ok = mine & (keys_at >= starts[r]) & (keys_at <= tok)
        bias = jnp.where(ok, 0.0, bias)
    local_lat = ll_ref[...]
    s = mm_nt(q, local_lat) + mm(qr, lr_ref[...])
    s = (s.reshape(HEADS, TILE, TOK) + bias[None]).reshape(ROWS, TOK)
    m = jnp.max(s, axis=1, keepdims=True)
    p = jnp.exp2((s - m) * c)
    m_scr[...] = jnp.broadcast_to(m, (ROWS, 128))
    l_scr[...] = jnp.broadcast_to(jnp.sum(p, axis=1, keepdims=True), (ROWS, 128))
    acc_scr[...] = mm(p.astype(bf16), local_lat)

    for pre in range(PREF):
        needed = (first < zero_count) if pre == 0 else (first + TILE > zero_count)

        @pl.when(needed)
        def _(pre=pre):
            views = block_views(pieces[pre])
            place = first + lax.broadcasted_iota(jnp.int32, (ROWS, 1), 0) % TILE
            mine = (place < zero_count) if pre == 0 else (place >= zero_count)
            row_bias = jnp.where(mine, 0.0, NEG)
            per = 4
            chunks = [views[k : k + per] for k in range(0, len(views), per)]
            m_old = m_scr[:, :1]
            m_new = m_old
            for k, chunk in enumerate(chunks):
                lat = jnp.concatenate([ref[at : at + 128, :] for ref, at in chunk], axis=0)
                rope = jnp.concatenate(
                    [
                        jnp.concatenate(
                            [ref[at + 128 : at + 144, j * 128 : (j + 1) * 128] for j in range(4)],
                            axis=0,
                        )
                        for ref, at in chunk
                    ],
                    axis=1,
                )
                s = mm_nt(q, lat) + mm(qr, rope) + row_bias
                s_scr[k] = s
                m_new = jnp.maximum(m_new, jnp.max(s, axis=1, keepdims=True))
            scale_old = jnp.exp2((m_old - m_new) * c)
            total = l_scr[:, :1] * scale_old
            acc = acc_scr[...] * scale_old
            for k, chunk in enumerate(chunks):
                lat = jnp.concatenate([ref[at : at + 128, :] for ref, at in chunk], axis=0)
                p = jnp.exp2((s_scr[k] - m_new) * c)
                total = total + jnp.sum(p, axis=1, keepdims=True)
                acc = acc + mm(p.astype(bf16), lat)
            m_scr[...] = jnp.broadcast_to(m_new, (ROWS, 128))
            l_scr[...] = jnp.broadcast_to(total, (ROWS, 128))
            acc_scr[...] = acc

    out = acc_scr[...] / l_scr[:, :1]
    o_ref[...] = out.astype(bf16).reshape(HEADS, TILE, LAT)


def attend(scalars, qa, qr, local_lat, local_rope, pieces0, pieces1):
    n_pieces = len(pieces0)
    whole = lambda a: pl.BlockSpec(a.shape, lambda i, s: (0,) * a.ndim)
    pieces = [*pieces0, *pieces1]
    return pl.pallas_call(
        lambda *refs: attention_kernel(n_pieces, *refs),
        out_shape=jax.ShapeDtypeStruct((HEADS, TOK, LAT), bf16),
        grid_spec=pltpu.PrefetchScalarGridSpec(
            num_scalar_prefetch=1,
            grid=(TOK // TILE,),
            in_specs=[
                pl.BlockSpec((HEADS, TILE, LAT), lambda i, s: (0, i, 0)),
                pl.BlockSpec((HEADS, TILE, ROPE), lambda i, s: (0, i, 0)),
                whole(local_lat),
                whole(local_rope),
                *[pl.BlockSpec(memory_space=pltpu.VMEM) for _ in pieces],
            ],
            out_specs=pl.BlockSpec((HEADS, TILE, LAT), lambda i, s: (0, i, 0)),
            scratch_shapes=[
                pltpu.VMEM((4, ROWS, 512), f32),
                pltpu.VMEM((ROWS, 128), f32),
                pltpu.VMEM((ROWS, 128), f32),
                pltpu.VMEM((ROWS, LAT), f32),
            ],
        ),
        name="attention",
        compiler_params=grant(24),
    )(scalars, qa, qr, local_lat, local_rope, *pieces)


def project_kernel(sc_ref, o_ref, w_ref, wo_ref, res_ref, gain_ref, hid_ref, norm_ref, acc_ref):
    step = pl.program_id(0)

    @pl.when(step == 0)
    def _():
        acc_ref[...] = res_ref[...].astype(f32)

    back = sort_matrix(sc_ref, True)
    heads = [mm(o_ref[h], w_ref[:, h * 256 + 128 : h * 256 + 256]).astype(bf16) for h in range(HG)]
    head_out = mm(back, jnp.concatenate(heads, axis=1)).astype(bf16)
    acc_ref[...] += mm(head_out, wo_ref[...])

    @pl.when(step == HEADS // HG - 1)
    def _():
        hidden = acc_ref[...].astype(bf16)
        hid_ref[...] = hidden
        h32 = hidden.astype(f32)
        inverse = lax.rsqrt(jnp.mean(h32 * h32, axis=1, keepdims=True) + EPS)
        norm_ref[...] = (h32 * inverse * gain_ref[...].astype(f32)).astype(bf16)


def project(scalars, o_lat, w_ukv, w_out, residual, gain):
    return pl.pallas_call(
        project_kernel,
        out_shape=(
            jax.ShapeDtypeStruct((TOK, D), bf16),
            jax.ShapeDtypeStruct((TOK, D), bf16),
        ),
        grid_spec=pltpu.PrefetchScalarGridSpec(
            num_scalar_prefetch=1,
            grid=(HEADS // HG,),
            in_specs=[
                pl.BlockSpec((HG, TOK, LAT), lambda i, s: (i, 0, 0)),
                pl.BlockSpec((LAT, HG * 2 * NOPE), lambda i, s: (0, i)),
                pl.BlockSpec((HG * NOPE, D), lambda i, s: (i, 0)),
                pl.BlockSpec((TOK, D), lambda i, s: (0, 0)),
                pl.BlockSpec((1, D), lambda i, s: (0, 0)),
            ],
            out_specs=[
                pl.BlockSpec((TOK, D), lambda i, s: (0, 0)),
                pl.BlockSpec((TOK, D), lambda i, s: (0, 0)),
            ],
            scratch_shapes=[pltpu.VMEM((TOK, D), f32)],
        ),
        name="project",
        compiler_params=grant(24),
    )(scalars, o_lat, w_ukv, w_out, residual, gain)


def rank_table(ids_ref):
    expert = lax.broadcasted_iota(jnp.int32, (EXPERTS, TOK), 0)
    named = ids_ref[0:1, :] == expert
    for k in range(1, TOP):
        named = named | (ids_ref[k : k + 1, :] == expert)
    earlier = lax.broadcasted_iota(jnp.int32, (TOK, TOK), 0) < lax.broadcasted_iota(
        jnp.int32, (TOK, TOK), 1
    )
    rank = mm(jnp.where(named, 1.0, 0.0).astype(bf16), jnp.where(earlier, 1.0, 0.0).astype(bf16))
    return jnp.where(named, rank, -1.0)


def gate_table(ids_ref, gates_ref):
    expert = lax.broadcasted_iota(jnp.int32, (EXPERTS, TOK), 0)
    gates = jnp.zeros((EXPERTS, TOK), f32)
    for k in range(TOP):
        gates = gates + jnp.where(ids_ref[k : k + 1, :] == expert, gates_ref[k : k + 1, :], 0.0)
    return gates


def whole_rows(ranks, experts, copies, values=None):
    slot = lax.broadcasted_iota(jnp.int32, (SLOTS_A, TOK), 0).astype(f32)
    rows = []
    for e in range(experts):
        on = 1.0 if values is None else values[e : e + 1, :]
        rows += [jnp.where(ranks[e : e + 1, :] == slot, on, 0.0)] * copies
    return jnp.concatenate(rows, axis=0)


def packed_rows(ranks, experts, copies, values=None):
    row = lax.broadcasted_iota(jnp.int32, (8, TOK), 0)
    slot = (SLOTS_A + row // 2).astype(f32)
    even = row % 2 == 0
    lower, upper, last = [], [], []
    for e in range(experts):
        rank = ranks[e : e + 1, :]
        on = 1.0 if values is None else values[e : e + 1, :]
        hit = jnp.where(rank == slot, on, 0.0)
        lower += [jnp.where(even, hit, 0.0)] * copies
        upper += [jnp.where(even, 0.0, hit)] * copies
        last += [jnp.where(jnp.broadcast_to(rank, (8, TOK)) == CAP - 1.0, on, 0.0)] * copies
    return [jnp.concatenate(part, axis=0) for part in (lower, upper, last)]


def pieces_of(last):
    row = lax.broadcasted_iota(jnp.int32, last.shape, 0) % 8
    return [jnp.where(row == q, last, 0.0) for q in range(8)]


EG = 16


def dispatch_kernel(ids_ref, norm_ref, out_ref, rank_scr):
    step = pl.program_id(0)

    @pl.when(step == 0)
    def _():
        rank_scr[...] = rank_table(ids_ref)

    ranks = rank_scr[pl.ds(step * EG, EG), :]
    sent = mm(whole_rows(ranks, EG, 1).astype(bf16), norm_ref[...]).astype(bf16)
    for e in range(EG):
        part = sent[e * SLOTS_A : (e + 1) * SLOTS_A]
        out_ref[2 * e] = part
        out_ref[2 * e + 1] = part


def dispatch_packed_kernel(ids_ref, norm_ref, out_ref, rank_scr):
    step = pl.program_id(0)

    @pl.when(step == 0)
    def _():
        rank_scr[...] = rank_table(ids_ref)

    ranks = rank_scr[pl.ds(step * EG, EG), :]
    lower, upper, last = packed_rows(ranks, EG, 1)
    sent = (
        mm(lower.astype(bf16), norm_ref[:, :HALF]) + mm(upper.astype(bf16), norm_ref[:, HALF:])
    ).astype(bf16)
    tail = jnp.zeros((EG * 8, PIECE), f32)
    for q, piece in enumerate(pieces_of(last)):
        tail = tail + mm(piece.astype(bf16), norm_ref[:, q * PIECE : (q + 1) * PIECE])
    tail = tail.astype(bf16)
    for e in range(EG):
        for copy in range(2):
            out_ref[2 * e + copy, :, :HALF] = sent[e * 8 : (e + 1) * 8]
            out_ref[2 * e + copy, :, HALF:] = tail[e * 8 : (e + 1) * 8]


def dispatch(kernel, width, ids_t, normed):
    return pl.pallas_call(
        kernel,
        out_shape=jax.ShapeDtypeStruct((2 * EXPERTS, 8, width), bf16),
        grid=(EXPERTS // EG,),
        in_specs=[
            pl.BlockSpec((TOP, TOK), lambda i: (0, 0)),
            pl.BlockSpec((TOK, D), lambda i: (0, 0)),
        ],
        out_specs=pl.BlockSpec((2 * EG, 8, width), lambda i: (i, 0, 0)),
        scratch_shapes=[pltpu.VMEM((EXPERTS, TOK), f32)],
        compiler_params=grant(32),
    )(ids_t, normed)


def activate(x, wg_ref):
    gate_up = mm(x, wg_ref[0])
    gate, up = gate_up[:, :HIDDEN], gate_up[:, HIDDEN:]
    return gate / (1.0 + jnp.exp(-gate)) * up


def side_of(pair, side):
    return (side + pair // 2) % 2


def up_kernel(side_ref, x_ref, wg_ref, own_ref, other_ref):
    n = x_ref.shape[0] // 2
    act = activate(x_ref[...].reshape(-1, D), wg_ref).reshape(n, 2, 8, HIDDEN)
    pair = lax.broadcasted_iota(jnp.int32, (n, 8, HIDDEN), 0)
    even = side_of(pair, side_ref[0]) == 0
    own_ref[...] = jnp.where(even, act[:, 0], act[:, 1]).astype(bf16)
    other_ref[...] = jnp.where(even, act[:, 1], act[:, 0]).astype(bf16)


def pick(rows, columns, stride, offset):
    r = lax.broadcasted_iota(jnp.int32, (rows, columns), 0)
    c = lax.broadcasted_iota(jnp.int32, (rows, columns), 1)
    return jnp.where(c == r * stride + offset, 1.0, 0.0).astype(bf16)


def pick_main(n, side, half):
    r = lax.broadcasted_iota(jnp.int32, (4 * n, 16 * n), 0)
    c = lax.broadcasted_iota(jnp.int32, (4 * n, 16 * n), 1)
    at = (2 * (r // 4) + side_of(r // 4, side)) * 8 + 2 * (r % 4) + half
    return jnp.where(c == at, 1.0, 0.0).astype(bf16)


def pick_last(n, side, q):
    r = lax.broadcasted_iota(jnp.int32, (n, 16 * n), 0)
    c = lax.broadcasted_iota(jnp.int32, (n, 16 * n), 1)
    return jnp.where(c == (2 * r + side_of(r, side)) * 8 + q, 1.0, 0.0).astype(bf16)


def up_packed_kernel(side_ref, x_ref, wg_ref, own_ref, other_ref):
    n = x_ref.shape[0] // 2
    x = x_ref[...].reshape(16 * n, WIDTH_B)
    wide, tail = x[:, :HALF], x[:, HALF:]
    own, other = side_ref[0], 1 - side_ref[0]
    halves = [
        mm(jnp.concatenate([pick_main(n, own, h), pick_main(n, other, h)], axis=0), wide)
        for h in range(2)
    ]
    main = jnp.concatenate(halves, axis=1)
    parts = []
    for q in range(8):
        chosen = [pick_last(n, own, q), pick_last(n, other, q)]
        parts.append(mm(jnp.concatenate(chosen, axis=0), tail))
    last = jnp.concatenate(parts, axis=1)
    act = activate(jnp.concatenate([main, last], axis=0).astype(bf16), wg_ref).astype(bf16)
    own_ref[0, : 4 * n] = act[: 4 * n]
    own_ref[0, 4 * n :] = act[8 * n : 9 * n]
    other_ref[0, : 4 * n] = act[4 * n : 8 * n]
    other_ref[0, 4 * n :] = act[9 * n :]


PER = 16
HIDDEN = 704


def run_up(kernel, side, rows, w_gate_up):
    width = rows.shape[2]
    steps = rows.shape[0] // (2 * PER)
    if width == D:
        shape, block = (PER * steps, 8, HIDDEN), (PER, 8, HIDDEN)
    else:
        shape, block = (steps, 5 * PER, HIDDEN), (1, 5 * PER, HIDDEN)
    return pl.pallas_call(
        kernel,
        out_shape=(jax.ShapeDtypeStruct(shape, bf16),) * 2,
        grid_spec=pltpu.PrefetchScalarGridSpec(
            num_scalar_prefetch=1,
            grid=(steps,),
            in_specs=[
                pl.BlockSpec((2 * PER, 8, width), lambda i, s: (i, 0, 0)),
                pl.BlockSpec(
                    w_gate_up.shape, lambda i, s: (0, 0, 0), pipeline_mode=pl.Buffered(1)
                ),
            ],
            out_specs=[pl.BlockSpec(block, lambda i, s: (i, 0, 0))] * 2,
        ),
        compiler_params=grant(32),
    )(side, rows, w_gate_up)


def down_kernel(own_ref, came_ref, wo_ref, wc_ref, out_ref):
    own = own_ref[...].reshape(-1, HIDDEN)
    came = came_ref[...].reshape(-1, HIDDEN)
    out = mm(own, wo_ref[0]) + mm(came, wc_ref[0])
    out_ref[...] = out.astype(bf16).reshape(out_ref.shape)


def down_packed_kernel(own_ref, came_ref, wo_ref, wc_ref, out_ref):
    n = out_ref.shape[0]
    y = (mm(own_ref[0], wo_ref[0]) + mm(came_ref[0], wc_ref[0])).astype(bf16)
    main, last = y[: 4 * n], y[4 * n :]
    even, odd = pick(4 * n, 8 * n, 2, 0), pick(4 * n, 8 * n, 2, 1)
    out = mm_tn(even, main[:, :HALF]) + mm_tn(odd, main[:, HALF:])
    tail = jnp.zeros((8 * n, PIECE), f32)
    for q in range(8):
        tail = tail + mm_tn(pick(n, 8 * n, 8, q), last[:, q * PIECE : (q + 1) * PIECE])
    out_ref[:, :, :HALF] = out.astype(bf16).reshape(n, 8, HALF)
    out_ref[:, :, HALF:] = tail.astype(bf16).reshape(n, 8, PIECE)


def run_down(kernel, own, came, w_own, w_came, width):
    blocks = 2 if width == D else 1
    steps = EXPERTS // PER // blocks
    act = pl.BlockSpec((own.shape[0] // steps, *own.shape[1:]), lambda i: (i, 0, 0))
    weight = pl.BlockSpec(w_own.shape, lambda i: (0, 0, 0), pipeline_mode=pl.Buffered(1))
    return pl.pallas_call(
        kernel,
        out_shape=jax.ShapeDtypeStruct((EXPERTS, 8, width), bf16),
        grid=(steps,),
        in_specs=[act, act, weight, weight],
        out_specs=pl.BlockSpec((EXPERTS // steps, 8, width), lambda i: (i, 0, 0)),
        compiler_params=grant(32),
    )(own, came, w_own, w_came)


def weighted(weight, back):
    high = weight.astype(bf16)
    low = (weight - high.astype(f32)).astype(bf16)
    both = mm_tn(jnp.concatenate([high, low], axis=1), back)
    return both[:TOK] + both[TOK:]


CG = 32


def combine_kernel(ids_ref, gates_ref, hid_ref, back_ref, out_ref, rank_scr, gate_scr):
    step = pl.program_id(0)

    @pl.when(step == 0)
    def _():
        rank_scr[...] = rank_table(ids_ref)
        gate_scr[...] = gate_table(ids_ref, gates_ref)
        out_ref[...] = hid_ref[...].astype(f32)

    ranks = rank_scr[pl.ds(step * CG, CG), :]
    gates = gate_scr[pl.ds(step * CG, CG), :]
    back = back_ref[...].reshape(CG * SLOTS_A, D)
    out_ref[...] += weighted(whole_rows(ranks, CG, 1, gates), back)


def combine(ids_t, gates_t, hidden, back):
    return pl.pallas_call(
        combine_kernel,
        out_shape=jax.ShapeDtypeStruct((TOK, D), f32),
        grid=(EXPERTS // CG,),
        in_specs=[
            pl.BlockSpec((TOP, TOK), lambda i: (0, 0)),
            pl.BlockSpec((TOP, TOK), lambda i: (0, 0)),
            pl.BlockSpec((TOK, D), lambda i: (0, 0)),
            pl.BlockSpec((CG, 8, D), lambda i: (i, 0, 0)),
        ],
        out_specs=pl.BlockSpec((TOK, D), lambda i: (0, 0)),
        scratch_shapes=[pltpu.VMEM((EXPERTS, TOK), f32), pltpu.VMEM((EXPERTS, TOK), f32)],
        name="combine_a",
        compiler_params=grant(32),
    )(ids_t, gates_t, hidden, back)


def combine_packed_kernel(ids_ref, gates_ref, sum_ref, back_ref, out_ref, acc_ref):
    ranks = rank_table(ids_ref)
    gates = gate_table(ids_ref, gates_ref)
    back = back_ref[...].reshape(EXPERTS * 8, WIDTH_B)
    lower, upper, last = packed_rows(ranks, EXPERTS, 1, gates)
    acc_ref[:, :HALF] = sum_ref[:, :HALF] + weighted(lower, back[:, :HALF])
    acc_ref[:, HALF:] = sum_ref[:, HALF:] + weighted(upper, back[:, :HALF])
    for q, piece in enumerate(pieces_of(last)):
        acc_ref[:, q * PIECE : (q + 1) * PIECE] += weighted(piece, back[:, HALF:])
    out_ref[...] = acc_ref[...].astype(bf16)


def combine_packed(ids_t, gates_t, base, back):
    return pl.pallas_call(
        combine_packed_kernel,
        out_shape=jax.ShapeDtypeStruct((TOK, D), bf16),
        in_specs=[pl.BlockSpec(memory_space=pltpu.VMEM)] * 4,
        out_specs=pl.BlockSpec(memory_space=pltpu.VMEM),
        scratch_shapes=[pltpu.VMEM((TOK, D), f32)],
        name="combine_b",
        compiler_params=grant(24),
    )(ids_t, gates_t, base, back)


def shift(axis, k):
    pairs = []
    for x in range(4):
        for y in range(4):
            tx, ty = ((x + k) % 4, y) if axis == "x" else (x, (y + k) % 4)
            pairs.append((x * 4 + y, tx * 4 + ty))
    return pairs


def hop(a, axis, k):
    return lax.ppermute(a, "wide", shift(axis, k))


def gather_blocks(own, first, second):
    row = jnp.concatenate([own, hop(own, first, 1), hop(own, first, -1), hop(own, first, 2)], axis=0)
    ahead, behind = hop(row, second, 1), hop(row, second, -1)
    half = row.shape[0] // 2
    far0, far1 = hop(ahead[:half], second, 1), hop(behind[half:], second, -1)
    return [row, ahead, behind, far0, far1]


def swap(a):
    return lax.ppermute(a, "wide", [(w, w ^ 1) for w in range(16)])


def pack_prefix(latent, rope):
    packed = rope.reshape(4, 16, TOK).transpose(1, 0, 2).reshape(16, 4 * TOK)
    return jnp.concatenate([latent, packed], axis=0)


def exchange(a):
    return lax.all_to_all(a, ("req", "wide"), split_axis=0, concat_axis=0, tiled=True)


def give_back(a):
    sides = [[n for n in range(2 * EXPERTS) if (n + n // 4) % 2 == side] for side in range(2)]
    return lax.all_to_all(
        a, ("req", "wide"), split_axis=0, concat_axis=0, axis_index_groups=sides, tiled=True
    )


def layer(
    queries,
    suffix_latent,
    suffix_rope,
    residual,
    prefix_latent,
    prefix_rope,
    suffix_lengths,
    prefix_ids,
    w_ukv,
    w_out,
    norm_gain,
    expert_ids,
    gate_values,
    expert_gate_up,
    expert_down,
):
    scalars = jnp.concatenate([suffix_lengths[0], prefix_ids[0]])
    pieces0 = gather_blocks(pack_prefix(prefix_latent[0, 0], prefix_rope[0, 0]), "x", "y")
    pieces1 = gather_blocks(pack_prefix(prefix_latent[0, 1], prefix_rope[0, 1]), "y", "x")
    down_came = swap(expert_down)
    place = lax.axis_index("wide")
    side = ((place + place // 4) % 2).reshape(1)
    qa, qr = prepare_queries(scalars, queries, w_ukv)
    o_lat = attend(scalars, qa, qr, suffix_latent, suffix_rope, pieces0, pieces1)
    hidden, normed = project(scalars, o_lat, w_ukv, w_out, residual, norm_gain.reshape(1, D))
    ids_t = expert_ids.T
    gates_t = gate_values.T
    sent_a = dispatch(dispatch_kernel, D, ids_t, normed)
    sent_b = dispatch(dispatch_packed_kernel, WIDTH_B, ids_t, normed)
    rows_a = exchange(sent_a)
    rows_b = exchange(sent_b)
    own_a, other_a = run_up(up_kernel, side, rows_a, expert_gate_up)
    came_a = swap(other_a)
    made_a = run_down(down_kernel, own_a, came_a, expert_down, down_came, D)
    own_b, other_b = run_up(up_packed_kernel, side, rows_b, expert_gate_up)
    came_b = swap(other_b)
    made_b = run_down(down_packed_kernel, own_b, came_b, expert_down, down_came, WIDTH_B)
    back_a = give_back(made_a)
    back_b = give_back(made_b)
    part = combine(ids_t, gates_t, hidden, back_a)
    return combine_packed(ids_t, gates_t, part, back_b)


def solution(mesh):
    return jax.shard_map(
        layer,
        mesh=mesh,
        in_specs=(
            P(("req", "wide"), None),
            P(("req", "wide"), None),
            P(None, ("req", "wide")),
            P(("req", "wide"), None),
            P("req", None, "wide", None),
            P("req", None, None, "wide"),
            P(("req", "wide"), None),
            P(("req", "wide"), None),
            P(),
            P(),
            P(),
            P(("req", "wide"), None),
            P(("req", "wide"), None),
            P(("req", "wide"), None, None),
            P(("req", "wide"), None, None),
        ),
        out_specs=P(("req", "wide"), None),
        check_vma=False,
    )
```

```python
import jax
import jax.numpy as jnp
from jax import lax
from jax.experimental import pallas as pl
from jax.experimental.pallas import tpu as pltpu
from jax.sharding import PartitionSpec as P


D = 2048
HEADS = 16
NOPE = 128
ROPE = 64
LAT = 512
TOP = 6
PREF = 2
EXPERTS = 64
TOK = 128
REQS = 4
TILE = 16
CAP = 13
SLOTS_A = 8
HALF = D // 2
PIECE = D // 8
WIDTH_B = HALF + PIECE
BLK = 144
EPS = 1e-06
SCALE = 1.0 / (NOPE + ROPE) ** 0.5
LOG2E = 1.4426950408889634
NEG = -1e30
bf16 = jnp.bfloat16
f32 = jnp.float32


def request_scalars(sc_ref):
    lens = [sc_ref[r] for r in range(REQS)]
    own = [sc_ref[REQS + r] for r in range(REQS)]
    starts, total = [], 0
    for r in range(REQS):
        starts.append(total)
        total = total + lens[r]
    zero_count = sum(jnp.where(own[r] == 0, lens[r], 0) for r in range(REQS))
    bases, next0, next1 = [], 0, zero_count
    for r in range(REQS):
        is0 = own[r] == 0
        bases.append(jnp.where(is0, next0, next1))
        next0 = next0 + jnp.where(is0, lens[r], 0)
        next1 = next1 + jnp.where(is0, 0, lens[r])
    return lens, starts, bases, zero_count


def place_of(tokens, starts, bases):
    place = tokens - starts[0] + bases[0]
    for r in range(1, REQS):
        place = jnp.where(tokens >= starts[r], tokens - starts[r] + bases[r], place)
    return place


def sort_matrix(sc_ref, transposed):
    _, starts, bases, _ = request_scalars(sc_ref)
    token_dim = 0 if transposed else 1
    tokens = lax.broadcasted_iota(jnp.int32, (TOK, TOK), token_dim)
    slots = lax.broadcasted_iota(jnp.int32, (TOK, TOK), 1 - token_dim)
    return jnp.where(place_of(tokens, starts, bases) == slots, 1.0, 0.0).astype(bf16)


def grant(mib):
    return pltpu.CompilerParams(vmem_limit_bytes=mib << 20)


def mm(a, b):
    return jnp.dot(a, b, preferred_element_type=f32)


def mm_nt(a, b):
    return lax.dot_general(a, b, (((1,), (1,)), ((), ())), preferred_element_type=f32)


def mm_tn(a, b):
    return lax.dot_general(a, b, (((0,), (0,)), ((), ())), preferred_element_type=f32)


HG = 4


def query_kernel(sc_ref, q_ref, qr_ref, w_ref, qa_ref, qo_ref):
    order = sort_matrix(sc_ref, False)
    nope = mm(order, q_ref[...]).astype(bf16)
    rope = mm(order, qr_ref[...]).astype(bf16)
    for h in range(HG):
        keys = w_ref[:, h * 256 : h * 256 + 128]
        qa_ref[h] = mm_nt(nope[:, h * 128 : (h + 1) * 128], keys).astype(bf16)
        qo_ref[h] = rope[:, h * ROPE : (h + 1) * ROPE]


def prepare_queries(scalars, queries, w_ukv):
    return pl.pallas_call(
        query_kernel,
        out_shape=(
            jax.ShapeDtypeStruct((HEADS, TOK, LAT), bf16),
            jax.ShapeDtypeStruct((HEADS, TOK, ROPE), bf16),
        ),
        grid_spec=pltpu.PrefetchScalarGridSpec(
            num_scalar_prefetch=1,
            grid=(HEADS // HG,),
            in_specs=[
                pl.BlockSpec((TOK, HG * NOPE), lambda i, s: (0, i)),
                pl.BlockSpec((TOK, HG * ROPE), lambda i, s: (0, HEADS * NOPE // (HG * ROPE) + i)),
                pl.BlockSpec((LAT, HG * 2 * NOPE), lambda i, s: (0, i)),
            ],
            out_specs=[
                pl.BlockSpec((HG, TOK, LAT), lambda i, s: (i, 0, 0)),
                pl.BlockSpec((HG, TOK, ROPE), lambda i, s: (i, 0, 0)),
            ],
        ),
        name="query_prep",
        compiler_params=grant(24),
    )(scalars, queries, queries, w_ukv)


ROWS = HEADS * TILE


def block_views(refs):
    views = []
    for ref in refs:
        for b in range(ref.shape[0] // BLK):
            views.append((ref, b * BLK))
    return views


def attention_kernel(n_pieces, stage, sc_ref, qa_ref, qr_ref, *rest):
    rest = list(rest)
    local = [rest.pop(0), rest.pop(0)]
    pieces = (rest[:n_pieces], rest[n_pieces : 2 * n_pieces])
    rest = rest[2 * n_pieces :]
    if stage == LAST:
        o_ref, s_scr, m_scr, l_scr, acc_scr = rest
    else:
        ml_ref, acc_out, s_scr, m_scr, l_scr, acc_scr = rest
    lens, starts, bases, zero_count = request_scalars(sc_ref)
    first = pl.program_id(0) * TILE
    c = SCALE * LOG2E
    q = qa_ref[...].reshape(ROWS, LAT)
    qr = qr_ref[...].reshape(ROWS, ROPE)

    if stage == FIRST:
        ll_ref, lr_ref = local
        places = first + lax.broadcasted_iota(jnp.int32, (TILE, TOK), 0)
        keys_at = lax.broadcasted_iota(jnp.int32, (TILE, TOK), 1)
        bias = jnp.full((TILE, TOK), NEG, f32)
        for r in range(REQS):
            mine = (places >= bases[r]) & (places < bases[r] + lens[r])
            tok = places - bases[r] + starts[r]
            ok = mine & (keys_at >= starts[r]) & (keys_at <= tok)
            bias = jnp.where(ok, 0.0, bias)
        local_lat = ll_ref[...]
        s = mm_nt(q, local_lat) + mm(qr, lr_ref[...])
        s = (s.reshape(HEADS, TILE, TOK) + bias[None]).reshape(ROWS, TOK)
        m = jnp.max(s, axis=1, keepdims=True)
        p = jnp.exp2((s - m) * c)
        m_scr[...] = jnp.broadcast_to(m, (ROWS, 128))
        l_scr[...] = jnp.broadcast_to(jnp.sum(p, axis=1, keepdims=True), (ROWS, 128))
        acc_scr[...] = mm(p.astype(bf16), local_lat)
    else:
        ml_in, acc_in = local
        ml = ml_in[...].reshape(ROWS, 128)
        m_scr[...] = jnp.broadcast_to(ml[:, :1], (ROWS, 128))
        l_scr[...] = jnp.broadcast_to(ml[:, 1:2], (ROWS, 128))
        acc_scr[...] = acc_in[...].reshape(ROWS, LAT)

    for pre in range(PREF):
        needed = (first < zero_count) if pre == 0 else (first + TILE > zero_count)

        @pl.when(needed)
        def _(pre=pre):
            views = block_views(pieces[pre])
            place = first + lax.broadcasted_iota(jnp.int32, (ROWS, 1), 0) % TILE
            mine = (place < zero_count) if pre == 0 else (place >= zero_count)
            row_bias = jnp.where(mine, 0.0, NEG)
            chunks = [views[k : k + 4] for k in range(0, len(views), 4)]
            m_old = m_scr[:, :1]
            m_new = m_old
            for k, chunk in enumerate(chunks):
                lat = jnp.concatenate([ref[at : at + 128, :] for ref, at in chunk], axis=0)
                rope = jnp.concatenate(
                    [
                        jnp.concatenate(
                            [ref[at + 128 : at + 144, j * 128 : (j + 1) * 128] for j in range(4)],
                            axis=0,
                        )
                        for ref, at in chunk
                    ],
                    axis=1,
                )
                s = mm_nt(q, lat) + mm(qr, rope) + row_bias
                s_scr[k] = s
                m_new = jnp.maximum(m_new, jnp.max(s, axis=1, keepdims=True))
            scale_old = jnp.exp2((m_old - m_new) * c)
            total = l_scr[:, :1] * scale_old
            acc = acc_scr[...] * scale_old
            for k, chunk in enumerate(chunks):
                lat = jnp.concatenate([ref[at : at + 128, :] for ref, at in chunk], axis=0)
                p = jnp.exp2((s_scr[k] - m_new) * c)
                total = total + jnp.sum(p, axis=1, keepdims=True)
                acc = acc + mm(p.astype(bf16), lat)
            m_scr[...] = jnp.broadcast_to(m_new, (ROWS, 128))
            l_scr[...] = jnp.broadcast_to(total, (ROWS, 128))
            acc_scr[...] = acc

    if stage == LAST:
        out = acc_scr[...] / l_scr[:, :1]
        o_ref[...] = out.astype(bf16).reshape(HEADS, TILE, LAT)
    else:
        lane = lax.broadcasted_iota(jnp.int32, (ROWS, 128), 1)
        ml = jnp.where(lane == 0, m_scr[...], l_scr[...])
        ml_ref[...] = ml.reshape(HEADS, TILE, 128)
        acc_out[...] = acc_scr[...].reshape(HEADS, TILE, LAT)


FIRST, LAST = 0, 2


def attend(stage, scalars, qa, qr, local, pieces0, pieces1):
    n_pieces = len(pieces0)
    whole = lambda a: pl.BlockSpec(a.shape, lambda i, s: (0,) * a.ndim)
    tiled = lambda width: pl.BlockSpec((HEADS, TILE, width), lambda i, s: (0, i, 0))
    pieces = [*pieces0, *pieces1]
    local_specs = [whole(a) for a in local] if stage == FIRST else [tiled(128), tiled(LAT)]
    if stage == LAST:
        out_shape = jax.ShapeDtypeStruct((HEADS, TOK, LAT), bf16)
        out_specs = tiled(LAT)
    else:
        out_shape = (
            jax.ShapeDtypeStruct((HEADS, TOK, 128), f32),
            jax.ShapeDtypeStruct((HEADS, TOK, LAT), f32),
        )
        out_specs = [tiled(128), tiled(LAT)]
    keys = sum(a.shape[0] // BLK for a in pieces0)
    return pl.pallas_call(
        lambda *refs: attention_kernel(n_pieces, stage, *refs),
        out_shape=out_shape,
        grid_spec=pltpu.PrefetchScalarGridSpec(
            num_scalar_prefetch=1,
            grid=(TOK // TILE,),
            in_specs=[tiled(LAT), tiled(ROPE), *local_specs, *[pl.BlockSpec(memory_space=pltpu.VMEM) for _ in pieces]],
            out_specs=out_specs,
            scratch_shapes=[
                pltpu.VMEM((max(keys // 4, 1), ROWS, 512), f32),
                pltpu.VMEM((ROWS, 128), f32),
                pltpu.VMEM((ROWS, 128), f32),
                pltpu.VMEM((ROWS, LAT), f32),
            ],
        ),
        compiler_params=grant(24),
    )(scalars, qa, qr, *local, *pieces)


def project_kernel(sc_ref, o_ref, w_ref, wo_ref, res_ref, gain_ref, hid_ref, norm_ref, acc_ref):
    step = pl.program_id(0)

    @pl.when(step == 0)
    def _():
        acc_ref[...] = res_ref[...].astype(f32)

    back = sort_matrix(sc_ref, True)
    heads = [mm(o_ref[h], w_ref[:, h * 256 + 128 : h * 256 + 256]).astype(bf16) for h in range(HG)]
    head_out = mm(back, jnp.concatenate(heads, axis=1)).astype(bf16)
    acc_ref[...] += mm(head_out, wo_ref[...])

    @pl.when(step == HEADS // HG - 1)
    def _():
        hidden = acc_ref[...].astype(bf16)
        hid_ref[...] = hidden
        h32 = hidden.astype(f32)
        inverse = lax.rsqrt(jnp.mean(h32 * h32, axis=1, keepdims=True) + EPS)
        norm_ref[...] = (h32 * inverse * gain_ref[...].astype(f32)).astype(bf16)


def project(scalars, o_lat, w_ukv, w_out, residual, gain):
    return pl.pallas_call(
        project_kernel,
        out_shape=(
            jax.ShapeDtypeStruct((TOK, D), bf16),
            jax.ShapeDtypeStruct((TOK, D), bf16),
        ),
        grid_spec=pltpu.PrefetchScalarGridSpec(
            num_scalar_prefetch=1,
            grid=(HEADS // HG,),
            in_specs=[
                pl.BlockSpec((HG, TOK, LAT), lambda i, s: (i, 0, 0)),
                pl.BlockSpec((LAT, HG * 2 * NOPE), lambda i, s: (0, i)),
                pl.BlockSpec((HG * NOPE, D), lambda i, s: (i, 0)),
                pl.BlockSpec((TOK, D), lambda i, s: (0, 0)),
                pl.BlockSpec((1, D), lambda i, s: (0, 0)),
            ],
            out_specs=[
                pl.BlockSpec((TOK, D), lambda i, s: (0, 0)),
                pl.BlockSpec((TOK, D), lambda i, s: (0, 0)),
            ],
            scratch_shapes=[pltpu.VMEM((TOK, D), f32)],
        ),
        name="project",
        compiler_params=grant(24),
    )(scalars, o_lat, w_ukv, w_out, residual, gain)


def rank_table(ids_ref):
    expert = lax.broadcasted_iota(jnp.int32, (EXPERTS, TOK), 0)
    named = ids_ref[0:1, :] == expert
    for k in range(1, TOP):
        named = named | (ids_ref[k : k + 1, :] == expert)
    earlier = lax.broadcasted_iota(jnp.int32, (TOK, TOK), 0) < lax.broadcasted_iota(
        jnp.int32, (TOK, TOK), 1
    )
    rank = mm(jnp.where(named, 1.0, 0.0).astype(bf16), jnp.where(earlier, 1.0, 0.0).astype(bf16))
    return jnp.where(named, rank, -1.0)


def gate_table(ids_ref, gates_ref):
    expert = lax.broadcasted_iota(jnp.int32, (EXPERTS, TOK), 0)
    gates = jnp.zeros((EXPERTS, TOK), f32)
    for k in range(TOP):
        gates = gates + jnp.where(ids_ref[k : k + 1, :] == expert, gates_ref[k : k + 1, :], 0.0)
    return gates


def whole_rows(ranks, experts, copies, values=None):
    slot = lax.broadcasted_iota(jnp.int32, (SLOTS_A, TOK), 0).astype(f32)
    rows = []
    for e in range(experts):
        on = 1.0 if values is None else values[e : e + 1, :]
        rows += [jnp.where(ranks[e : e + 1, :] == slot, on, 0.0)] * copies
    return jnp.concatenate(rows, axis=0)


def packed_rows(ranks, experts, copies, values=None):
    row = lax.broadcasted_iota(jnp.int32, (8, TOK), 0)
    slot = (SLOTS_A + row // 2).astype(f32)
    even = row % 2 == 0
    lower, upper, last = [], [], []
    for e in range(experts):
        rank = ranks[e : e + 1, :]
        on = 1.0 if values is None else values[e : e + 1, :]
        hit = jnp.where(rank == slot, on, 0.0)
        lower += [jnp.where(even, hit, 0.0)] * copies
        upper += [jnp.where(even, 0.0, hit)] * copies
        last += [jnp.where(jnp.broadcast_to(rank, (8, TOK)) == CAP - 1.0, on, 0.0)] * copies
    return [jnp.concatenate(part, axis=0) for part in (lower, upper, last)]


def pieces_of(last):
    row = lax.broadcasted_iota(jnp.int32, last.shape, 0) % 8
    return [jnp.where(row == q, last, 0.0) for q in range(8)]


EG = 16


def dispatch_kernel(ids_ref, norm_ref, out_ref, rank_scr):
    step = pl.program_id(0)

    @pl.when(step == 0)
    def _():
        rank_scr[...] = rank_table(ids_ref)

    ranks = rank_scr[pl.ds(step * EG, EG), :]
    sent = mm(whole_rows(ranks, EG, 1).astype(bf16), norm_ref[...]).astype(bf16)
    for e in range(EG):
        part = sent[e * SLOTS_A : (e + 1) * SLOTS_A]
        out_ref[2 * e] = part
        out_ref[2 * e + 1] = part


def dispatch_packed_kernel(ids_ref, norm_ref, out_ref, rank_scr):
    step = pl.program_id(0)

    @pl.when(step == 0)
    def _():
        rank_scr[...] = rank_table(ids_ref)

    ranks = rank_scr[pl.ds(step * EG, EG), :]
    lower, upper, last = packed_rows(ranks, EG, 1)
    sent = (
        mm(lower.astype(bf16), norm_ref[:, :HALF]) + mm(upper.astype(bf16), norm_ref[:, HALF:])
    ).astype(bf16)
    tail = jnp.zeros((EG * 8, PIECE), f32)
    for q, piece in enumerate(pieces_of(last)):
        tail = tail + mm(piece.astype(bf16), norm_ref[:, q * PIECE : (q + 1) * PIECE])
    tail = tail.astype(bf16)
    for e in range(EG):
        for copy in range(2):
            out_ref[2 * e + copy, :, :HALF] = sent[e * 8 : (e + 1) * 8]
            out_ref[2 * e + copy, :, HALF:] = tail[e * 8 : (e + 1) * 8]


def dispatch(kernel, width, ids_t, normed):
    return pl.pallas_call(
        kernel,
        out_shape=jax.ShapeDtypeStruct((2 * EXPERTS, 8, width), bf16),
        grid=(EXPERTS // EG,),
        in_specs=[
            pl.BlockSpec((TOP, TOK), lambda i: (0, 0)),
            pl.BlockSpec((TOK, D), lambda i: (0, 0)),
        ],
        out_specs=pl.BlockSpec((2 * EG, 8, width), lambda i: (i, 0, 0)),
        scratch_shapes=[pltpu.VMEM((EXPERTS, TOK), f32)],
        compiler_params=grant(32),
    )(ids_t, normed)


def expert_rows(x, wg_ref, wd_ref):
    gate_up = mm(x, wg_ref[0])
    half = gate_up.shape[1] // 2
    gate, up = gate_up[:, :half], gate_up[:, half:]
    act = (gate / (1.0 + jnp.exp(-gate)) * up).astype(bf16)
    return mm(act, wd_ref[0]).astype(bf16)


def expert_kernel(x_ref, wg_ref, wd_ref, out_ref):
    x = x_ref[...].reshape(-1, D)
    out_ref[...] = expert_rows(x, wg_ref, wd_ref).reshape(out_ref.shape)


def select(rows, columns, stride, offset):
    r = lax.broadcasted_iota(jnp.int32, (rows, columns), 0)
    c = lax.broadcasted_iota(jnp.int32, (rows, columns), 1)
    return jnp.where(c == r * stride + offset, 1.0, 0.0).astype(bf16)


def expert_packed_kernel(x_ref, wg_ref, wd_ref, out_ref):
    n = x_ref.shape[0]
    x = x_ref[...].reshape(8 * n, WIDTH_B)
    even, odd = select(4 * n, 8 * n, 2, 0), select(4 * n, 8 * n, 2, 1)
    each = [select(n, 8 * n, 8, q) for q in range(8)]
    main = jnp.concatenate([mm(even, x[:, :HALF]), mm(odd, x[:, :HALF])], axis=1)
    last = jnp.concatenate([mm(pick, x[:, HALF:]) for pick in each], axis=1)
    y = expert_rows(jnp.concatenate([main, last], axis=0).astype(bf16), wg_ref, wd_ref)
    main, last = y[: 4 * n], y[4 * n :]
    out = mm_tn(even, main[:, :HALF]) + mm_tn(odd, main[:, HALF:])
    tail = jnp.zeros((8 * n, PIECE), f32)
    for q, pick in enumerate(each):
        tail = tail + mm_tn(pick, last[:, q * PIECE : (q + 1) * PIECE])
    out_ref[:, :, :HALF] = out.astype(bf16).reshape(n, 8, HALF)
    out_ref[:, :, HALF:] = tail.astype(bf16).reshape(n, 8, PIECE)


def run_expert(kernel, rows, w_gate_up, w_down):
    width = rows.shape[2]
    per = 32
    return pl.pallas_call(
        kernel,
        out_shape=jax.ShapeDtypeStruct(rows.shape, bf16),
        grid=(rows.shape[0] // per,),
        in_specs=[
            pl.BlockSpec((per, 8, width), lambda i: (i, 0, 0)),
            pl.BlockSpec(w_gate_up.shape, lambda i: (0, 0, 0), pipeline_mode=pl.Buffered(1)),
            pl.BlockSpec(w_down.shape, lambda i: (0, 0, 0), pipeline_mode=pl.Buffered(1)),
        ],
        out_specs=pl.BlockSpec((per, 8, width), lambda i: (i, 0, 0)),
        compiler_params=grant(32),
    )(rows, w_gate_up, w_down)


def weighted(weight, back):
    high = weight.astype(bf16)
    low = (weight - high.astype(f32)).astype(bf16)
    both = mm_tn(jnp.concatenate([high, low], axis=1), back)
    return both[:TOK] + both[TOK:]


CG = 16


def combine_kernel(ids_ref, gates_ref, hid_ref, back_ref, out_ref, rank_scr, gate_scr):
    step = pl.program_id(0)

    @pl.when(step == 0)
    def _():
        rank_scr[...] = rank_table(ids_ref)
        gate_scr[...] = gate_table(ids_ref, gates_ref)
        out_ref[...] = hid_ref[...].astype(f32)

    ranks = rank_scr[pl.ds(step * CG, CG), :]
    gates = gate_scr[pl.ds(step * CG, CG), :]
    back = back_ref[...].reshape(2 * CG * SLOTS_A, D)
    out_ref[...] += weighted(whole_rows(ranks, CG, 2, gates), back)


def combine(ids_t, gates_t, hidden, back):
    return pl.pallas_call(
        combine_kernel,
        out_shape=jax.ShapeDtypeStruct((TOK, D), f32),
        grid=(EXPERTS // CG,),
        in_specs=[
            pl.BlockSpec((TOP, TOK), lambda i: (0, 0)),
            pl.BlockSpec((TOP, TOK), lambda i: (0, 0)),
            pl.BlockSpec((TOK, D), lambda i: (0, 0)),
            pl.BlockSpec((2 * CG, 8, D), lambda i: (i, 0, 0)),
        ],
        out_specs=pl.BlockSpec((TOK, D), lambda i: (0, 0)),
        scratch_shapes=[pltpu.VMEM((EXPERTS, TOK), f32), pltpu.VMEM((EXPERTS, TOK), f32)],
        name="combine_a",
        compiler_params=grant(32),
    )(ids_t, gates_t, hidden, back)


def combine_packed_kernel(ids_ref, gates_ref, sum_ref, back_ref, out_ref, acc_ref):
    ranks = rank_table(ids_ref)
    gates = gate_table(ids_ref, gates_ref)
    back = back_ref[...].reshape(2 * EXPERTS * 8, WIDTH_B)
    lower, upper, last = packed_rows(ranks, EXPERTS, 2, gates)
    acc_ref[:, :HALF] = sum_ref[:, :HALF] + weighted(lower, back[:, :HALF])
    acc_ref[:, HALF:] = sum_ref[:, HALF:] + weighted(upper, back[:, :HALF])
    for q, piece in enumerate(pieces_of(last)):
        acc_ref[:, q * PIECE : (q + 1) * PIECE] += weighted(piece, back[:, HALF:])
    out_ref[...] = acc_ref[...].astype(bf16)


def combine_packed(ids_t, gates_t, base, back):
    return pl.pallas_call(
        combine_packed_kernel,
        out_shape=jax.ShapeDtypeStruct((TOK, D), bf16),
        in_specs=[pl.BlockSpec(memory_space=pltpu.VMEM)] * 4,
        out_specs=pl.BlockSpec(memory_space=pltpu.VMEM),
        scratch_shapes=[pltpu.VMEM((TOK, D), f32)],
        name="combine_b",
        compiler_params=grant(24),
    )(ids_t, gates_t, base, back)


def shift(axis, k):
    pairs = []
    for x in range(4):
        for y in range(4):
            tx, ty = ((x + k) % 4, y) if axis == "x" else (x, (y + k) % 4)
            pairs.append((x * 4 + y, tx * 4 + ty))
    return pairs


def hop(a, axis, k):
    return lax.ppermute(a, "wide", shift(axis, k))


def gather_row(own, first):
    return jnp.concatenate([own, hop(own, first, 1), hop(own, first, -1), hop(own, first, 2)], axis=0)


def gather_rest(row, second):
    ahead, behind = hop(row, second, 1), hop(row, second, -1)
    half = row.shape[0] // 2
    far0, far1 = hop(ahead[:half], second, 1), hop(behind[half:], second, -1)
    return [ahead, behind, far0, far1]


def pack_prefix(latent, rope):
    packed = rope.reshape(4, 16, TOK).transpose(1, 0, 2).reshape(16, 4 * TOK)
    return jnp.concatenate([latent, packed], axis=0)


def exchange(a):
    return lax.all_to_all(a, ("req", "wide"), split_axis=0, concat_axis=0, tiled=True)


def layer(
    queries,
    suffix_latent,
    suffix_rope,
    residual,
    prefix_latent,
    prefix_rope,
    suffix_lengths,
    prefix_ids,
    w_ukv,
    w_out,
    norm_gain,
    expert_ids,
    gate_values,
    expert_gate_up,
    expert_down,
):
    scalars = jnp.concatenate([suffix_lengths[0], prefix_ids[0]])
    row0 = gather_row(pack_prefix(prefix_latent[0, 0], prefix_rope[0, 0]), "x")
    row1 = gather_row(pack_prefix(prefix_latent[0, 1], prefix_rope[0, 1]), "y")
    rest0 = gather_rest(row0, "y")
    rest1 = gather_rest(row1, "x")
    qa, qr = prepare_queries(scalars, queries, w_ukv)
    state = attend(FIRST, scalars, qa, qr, (suffix_latent, suffix_rope), [row0], [row1])
    o_lat = attend(LAST, scalars, qa, qr, state, rest0, rest1)
    hidden, normed = project(scalars, o_lat, w_ukv, w_out, residual, norm_gain.reshape(1, D))
    ids_t = expert_ids.T
    gates_t = gate_values.T
    sent_a = dispatch(dispatch_kernel, D, ids_t, normed)
    sent_b = dispatch(dispatch_packed_kernel, WIDTH_B, ids_t, normed)
    rows_a = exchange(sent_a)
    rows_b = exchange(sent_b)
    made_a = run_expert(expert_kernel, rows_a, expert_gate_up, expert_down)
    made_b = run_expert(expert_packed_kernel, rows_b, expert_gate_up, expert_down)
    back_a = exchange(made_a)
    back_b = exchange(made_b)
    part = combine(ids_t, gates_t, hidden, back_a)
    return combine_packed(ids_t, gates_t, part, back_b)


def solution(mesh):
    return jax.shard_map(
        layer,
        mesh=mesh,
        in_specs=(
            P(("req", "wide"), None),
            P(("req", "wide"), None),
            P(None, ("req", "wide")),
            P(("req", "wide"), None),
            P("req", None, "wide", None),
            P("req", None, None, "wide"),
            P(("req", "wide"), None),
            P(("req", "wide"), None),
            P(),
            P(),
            P(),
            P(("req", "wide"), None),
            P(("req", "wide"), None),
            P(("req", "wide"), None, None),
            P(("req", "wide"), None, None),
        ),
        out_specs=P(("req", "wide"), None),
        check_vma=False,
    )
```

```python
import jax
import jax.numpy as jnp
from jax import lax
from jax.experimental import pallas as pl
from jax.experimental.pallas import tpu as pltpu
from jax.sharding import PartitionSpec as P


D = 2048
HEADS = 16
NOPE = 128
ROPE = 64
LAT = 512
TOP = 6
PREF = 2
EXPERTS = 64
TOK = 128
REQS = 4
TILE = 16
CAP = 13
SLOTS_A = 8
HALF = D // 2
PIECE = D // 8
WIDTH_B = HALF + PIECE
BLK = 144
EPS = 1e-06
SCALE = 1.0 / (NOPE + ROPE) ** 0.5
LOG2E = 1.4426950408889634
NEG = -1e30
bf16 = jnp.bfloat16
f32 = jnp.float32


def request_scalars(sc_ref):
    lens = [sc_ref[r] for r in range(REQS)]
    own = [sc_ref[REQS + r] for r in range(REQS)]
    starts, total = [], 0
    for r in range(REQS):
        starts.append(total)
        total = total + lens[r]
    zero_count = sum(jnp.where(own[r] == 0, lens[r], 0) for r in range(REQS))
    bases, next0, next1 = [], 0, zero_count
    for r in range(REQS):
        is0 = own[r] == 0
        bases.append(jnp.where(is0, next0, next1))
        next0 = next0 + jnp.where(is0, lens[r], 0)
        next1 = next1 + jnp.where(is0, 0, lens[r])
    return lens, starts, bases, zero_count


def place_of(tokens, starts, bases):
    place = tokens - starts[0] + bases[0]
    for r in range(1, REQS):
        place = jnp.where(tokens >= starts[r], tokens - starts[r] + bases[r], place)
    return place


def sort_matrix(sc_ref, transposed):
    _, starts, bases, _ = request_scalars(sc_ref)
    token_dim = 0 if transposed else 1
    tokens = lax.broadcasted_iota(jnp.int32, (TOK, TOK), token_dim)
    slots = lax.broadcasted_iota(jnp.int32, (TOK, TOK), 1 - token_dim)
    return jnp.where(place_of(tokens, starts, bases) == slots, 1.0, 0.0).astype(bf16)


def grant(mib):
    return pltpu.CompilerParams(vmem_limit_bytes=mib << 20)


def mm(a, b):
    return jnp.dot(a, b, preferred_element_type=f32)


def mm_nt(a, b):
    return lax.dot_general(a, b, (((1,), (1,)), ((), ())), preferred_element_type=f32)


def mm_tn(a, b):
    return lax.dot_general(a, b, (((0,), (0,)), ((), ())), preferred_element_type=f32)


HG = 4


def query_kernel(sc_ref, q_ref, qr_ref, w_ref, qa_ref, qo_ref):
    order = sort_matrix(sc_ref, False)
    nope = mm(order, q_ref[...]).astype(bf16)
    rope = mm(order, qr_ref[...]).astype(bf16)
    for h in range(HG):
        keys = w_ref[:, h * 256 : h * 256 + 128]
        qa_ref[h] = mm_nt(nope[:, h * 128 : (h + 1) * 128], keys).astype(bf16)
        qo_ref[h] = rope[:, h * ROPE : (h + 1) * ROPE]


def prepare_queries(scalars, queries, w_ukv):
    return pl.pallas_call(
        query_kernel,
        out_shape=(
            jax.ShapeDtypeStruct((HEADS, TOK, LAT), bf16),
            jax.ShapeDtypeStruct((HEADS, TOK, ROPE), bf16),
        ),
        grid_spec=pltpu.PrefetchScalarGridSpec(
            num_scalar_prefetch=1,
            grid=(HEADS // HG,),
            in_specs=[
                pl.BlockSpec((TOK, HG * NOPE), lambda i, s: (0, i)),
                pl.BlockSpec((TOK, HG * ROPE), lambda i, s: (0, HEADS * NOPE // (HG * ROPE) + i)),
                pl.BlockSpec((LAT, HG * 2 * NOPE), lambda i, s: (0, i)),
            ],
            out_specs=[
                pl.BlockSpec((HG, TOK, LAT), lambda i, s: (i, 0, 0)),
                pl.BlockSpec((HG, TOK, ROPE), lambda i, s: (i, 0, 0)),
            ],
        ),
        name="query_prep",
        compiler_params=grant(24),
    )(scalars, queries, queries, w_ukv)


ROWS = HEADS * TILE


def block_views(refs):
    views = []
    for ref in refs:
        for b in range(ref.shape[0] // BLK):
            views.append((ref, b * BLK))
    return views


def unpack_rope(ref, at):
    return jnp.concatenate(
        [ref[at + 128 : at + 144, j * 128 : (j + 1) * 128] for j in range(4)], axis=0
    )


def attention_kernel(n_pieces, sc_ref, qa_ref, qr_ref, ll_ref, lr_ref, *rest):
    pieces = (rest[:n_pieces], rest[n_pieces : 2 * n_pieces])
    o_ref, s_scr, n_scr = rest[2 * n_pieces :]
    lens, starts, bases, zero_count = request_scalars(sc_ref)
    first = pl.program_id(0) * TILE
    c = SCALE * LOG2E

    for pre in range(PREF):
        needed = (first < zero_count) if pre == 0 else (first + TILE > zero_count)

        @pl.when(needed)
        def _(pre=pre):
            q = qa_ref[...].reshape(ROWS, LAT)
            qr = qr_ref[...].reshape(ROWS, ROPE)
            places = first + lax.broadcasted_iota(jnp.int32, (TILE, TOK), 0)
            keys_at = lax.broadcasted_iota(jnp.int32, (TILE, TOK), 1)
            bias = jnp.full((TILE, TOK), NEG, f32)
            for r in range(REQS):
                mine = (places >= bases[r]) & (places < bases[r] + lens[r])
                tok = places - bases[r] + starts[r]
                ok = mine & (keys_at >= starts[r]) & (keys_at <= tok)
                bias = jnp.where(ok, 0.0, bias)
            local_lat = ll_ref[...]
            s = mm_nt(q, local_lat) + mm(qr, lr_ref[...])
            s = (s.reshape(HEADS, TILE, TOK) + bias[None]).reshape(ROWS, TOK)
            n_scr[...] = s
            m = jnp.max(s, axis=1, keepdims=True)
            views = block_views(pieces[pre])
            chunks = [views[k : k + 4] for k in range(0, len(views), 4)]
            for k, chunk in enumerate(chunks):
                lat = jnp.concatenate([ref[at : at + 128, :] for ref, at in chunk], axis=0)
                rope = jnp.concatenate([unpack_rope(ref, at) for ref, at in chunk], axis=1)
                s = mm_nt(q, lat) + mm(qr, rope)
                s_scr[k] = s
                m = jnp.maximum(m, jnp.max(s, axis=1, keepdims=True))
            p = jnp.exp2((n_scr[...] - m) * c)
            total = jnp.sum(p, axis=1, keepdims=True)
            acc = mm(p.astype(bf16), local_lat)
            for k, chunk in enumerate(chunks):
                lat = jnp.concatenate([ref[at : at + 128, :] for ref, at in chunk], axis=0)
                p = jnp.exp2((s_scr[k] - m) * c)
                total = total + jnp.sum(p, axis=1, keepdims=True)
                acc = acc + mm(p.astype(bf16), lat)
            out = (acc / total).astype(bf16).reshape(HEADS, TILE, LAT)
            if pre == 0:
                o_ref[...] = out
            else:
                place = first + lax.broadcasted_iota(jnp.int32, (HEADS, TILE, LAT), 1)
                o_ref[...] = jnp.where(place >= zero_count, out, o_ref[...])


def attend(scalars, qa, qr, local_lat, local_rope, pieces0, pieces1):
    n_pieces = len(pieces0)
    whole = lambda a: pl.BlockSpec(a.shape, lambda i, s: (0,) * a.ndim)
    tiled = lambda width: pl.BlockSpec((HEADS, TILE, width), lambda i, s: (0, i, 0))
    pieces = [*pieces0, *pieces1]
    return pl.pallas_call(
        lambda *refs: attention_kernel(n_pieces, *refs),
        out_shape=jax.ShapeDtypeStruct((HEADS, TOK, LAT), bf16),
        grid_spec=pltpu.PrefetchScalarGridSpec(
            num_scalar_prefetch=1,
            grid=(TOK // TILE,),
            in_specs=[
                tiled(LAT),
                tiled(ROPE),
                whole(local_lat),
                whole(local_rope),
                *[pl.BlockSpec(memory_space=pltpu.VMEM) for _ in pieces],
            ],
            out_specs=tiled(LAT),
            scratch_shapes=[pltpu.VMEM((4, ROWS, 512), f32), pltpu.VMEM((ROWS, TOK), f32)],
        ),
        name="attention",
        compiler_params=grant(24),
    )(scalars, qa, qr, local_lat, local_rope, *pieces)


def project_kernel(sc_ref, o_ref, w_ref, wo_ref, res_ref, gain_ref, hid_ref, norm_ref, acc_ref):
    step = pl.program_id(0)

    @pl.when(step == 0)
    def _():
        acc_ref[...] = res_ref[...].astype(f32)

    back = sort_matrix(sc_ref, True)
    heads = [mm(o_ref[h], w_ref[:, h * 256 + 128 : h * 256 + 256]).astype(bf16) for h in range(HG)]
    head_out = mm(back, jnp.concatenate(heads, axis=1)).astype(bf16)
    acc_ref[...] += mm(head_out, wo_ref[...])

    @pl.when(step == HEADS // HG - 1)
    def _():
        hidden = acc_ref[...].astype(bf16)
        hid_ref[...] = hidden
        h32 = hidden.astype(f32)
        inverse = lax.rsqrt(jnp.mean(h32 * h32, axis=1, keepdims=True) + EPS)
        norm_ref[...] = (h32 * inverse * gain_ref[...].astype(f32)).astype(bf16)


def project(scalars, o_lat, w_ukv, w_out, residual, gain):
    return pl.pallas_call(
        project_kernel,
        out_shape=(
            jax.ShapeDtypeStruct((TOK, D), bf16),
            jax.ShapeDtypeStruct((TOK, D), bf16),
        ),
        grid_spec=pltpu.PrefetchScalarGridSpec(
            num_scalar_prefetch=1,
            grid=(HEADS // HG,),
            in_specs=[
                pl.BlockSpec((HG, TOK, LAT), lambda i, s: (i, 0, 0)),
                pl.BlockSpec((LAT, HG * 2 * NOPE), lambda i, s: (0, i)),
                pl.BlockSpec((HG * NOPE, D), lambda i, s: (i, 0)),
                pl.BlockSpec((TOK, D), lambda i, s: (0, 0)),
                pl.BlockSpec((1, D), lambda i, s: (0, 0)),
            ],
            out_specs=[
                pl.BlockSpec((TOK, D), lambda i, s: (0, 0)),
                pl.BlockSpec((TOK, D), lambda i, s: (0, 0)),
            ],
            scratch_shapes=[pltpu.VMEM((TOK, D), f32)],
        ),
        name="project",
        compiler_params=grant(24),
    )(scalars, o_lat, w_ukv, w_out, residual, gain)


def rank_table(ids_ref):
    expert = lax.broadcasted_iota(jnp.int32, (EXPERTS, TOK), 0)
    named = ids_ref[0:1, :] == expert
    for k in range(1, TOP):
        named = named | (ids_ref[k : k + 1, :] == expert)
    earlier = lax.broadcasted_iota(jnp.int32, (TOK, TOK), 0) < lax.broadcasted_iota(
        jnp.int32, (TOK, TOK), 1
    )
    rank = mm(jnp.where(named, 1.0, 0.0).astype(bf16), jnp.where(earlier, 1.0, 0.0).astype(bf16))
    return jnp.where(named, rank, -1.0)


def gate_table(ids_ref, gates_ref):
    expert = lax.broadcasted_iota(jnp.int32, (EXPERTS, TOK), 0)
    gates = jnp.zeros((EXPERTS, TOK), f32)
    for k in range(TOP):
        gates = gates + jnp.where(ids_ref[k : k + 1, :] == expert, gates_ref[k : k + 1, :], 0.0)
    return gates


def whole_rows(ranks, experts, copies, values=None):
    slot = lax.broadcasted_iota(jnp.int32, (SLOTS_A, TOK), 0).astype(f32)
    rows = []
    for e in range(experts):
        on = 1.0 if values is None else values[e : e + 1, :]
        rows += [jnp.where(ranks[e : e + 1, :] == slot, on, 0.0)] * copies
    return jnp.concatenate(rows, axis=0)


def packed_rows(ranks, experts, copies, values=None):
    row = lax.broadcasted_iota(jnp.int32, (8, TOK), 0)
    slot = (SLOTS_A + row // 2).astype(f32)
    even = row % 2 == 0
    lower, upper, last = [], [], []
    for e in range(experts):
        rank = ranks[e : e + 1, :]
        on = 1.0 if values is None else values[e : e + 1, :]
        hit = jnp.where(rank == slot, on, 0.0)
        lower += [jnp.where(even, hit, 0.0)] * copies
        upper += [jnp.where(even, 0.0, hit)] * copies
        last += [jnp.where(jnp.broadcast_to(rank, (8, TOK)) == CAP - 1.0, on, 0.0)] * copies
    return [jnp.concatenate(part, axis=0) for part in (lower, upper, last)]


def pieces_of(last):
    row = lax.broadcasted_iota(jnp.int32, last.shape, 0) % 8
    return [jnp.where(row == q, last, 0.0) for q in range(8)]


EG = 16


def dispatch_kernel(ids_ref, norm_ref, out_ref, rank_scr):
    step = pl.program_id(0)

    @pl.when(step == 0)
    def _():
        rank_scr[...] = rank_table(ids_ref)

    ranks = rank_scr[pl.ds(step * EG, EG), :]
    sent = mm(whole_rows(ranks, EG, 1).astype(bf16), norm_ref[...]).astype(bf16)
    for e in range(EG):
        part = sent[e * SLOTS_A : (e + 1) * SLOTS_A]
        out_ref[2 * e] = part
        out_ref[2 * e + 1] = part


def dispatch_packed_kernel(ids_ref, norm_ref, out_ref, rank_scr):
    step = pl.program_id(0)

    @pl.when(step == 0)
    def _():
        rank_scr[...] = rank_table(ids_ref)

    ranks = rank_scr[pl.ds(step * EG, EG), :]
    lower, upper, last = packed_rows(ranks, EG, 1)
    sent = (
        mm(lower.astype(bf16), norm_ref[:, :HALF]) + mm(upper.astype(bf16), norm_ref[:, HALF:])
    ).astype(bf16)
    tail = jnp.zeros((EG * 8, PIECE), f32)
    for q, piece in enumerate(pieces_of(last)):
        tail = tail + mm(piece.astype(bf16), norm_ref[:, q * PIECE : (q + 1) * PIECE])
    tail = tail.astype(bf16)
    for e in range(EG):
        for copy in range(2):
            out_ref[2 * e + copy, :, :HALF] = sent[e * 8 : (e + 1) * 8]
            out_ref[2 * e + copy, :, HALF:] = tail[e * 8 : (e + 1) * 8]


def dispatch(kernel, width, ids_t, normed):
    return pl.pallas_call(
        kernel,
        out_shape=jax.ShapeDtypeStruct((2 * EXPERTS, 8, width), bf16),
        grid=(EXPERTS // EG,),
        in_specs=[
            pl.BlockSpec((TOP, TOK), lambda i: (0, 0)),
            pl.BlockSpec((TOK, D), lambda i: (0, 0)),
        ],
        out_specs=pl.BlockSpec((2 * EG, 8, width), lambda i: (i, 0, 0)),
        scratch_shapes=[pltpu.VMEM((EXPERTS, TOK), f32)],
        compiler_params=grant(32),
    )(ids_t, normed)


def expert_rows(x, wg_ref, wd_ref):
    gate_up = mm(x, wg_ref[0])
    half = gate_up.shape[1] // 2
    gate, up = gate_up[:, :half], gate_up[:, half:]
    act = (gate / (1.0 + jnp.exp(-gate)) * up).astype(bf16)
    return mm(act, wd_ref[0]).astype(bf16)


def expert_kernel(x_ref, wg_ref, wd_ref, out_ref):
    x = x_ref[...].reshape(-1, D)
    out_ref[...] = expert_rows(x, wg_ref, wd_ref).reshape(out_ref.shape)


def select(rows, columns, stride, offset):
    r = lax.broadcasted_iota(jnp.int32, (rows, columns), 0)
    c = lax.broadcasted_iota(jnp.int32, (rows, columns), 1)
    return jnp.where(c == r * stride + offset, 1.0, 0.0).astype(bf16)


def expert_packed_kernel(x_ref, wg_ref, wd_ref, out_ref):
    n = x_ref.shape[0]
    x = x_ref[...].reshape(8 * n, WIDTH_B)
    even, odd = select(4 * n, 8 * n, 2, 0), select(4 * n, 8 * n, 2, 1)
    each = [select(n, 8 * n, 8, q) for q in range(8)]
    main = jnp.concatenate([mm(even, x[:, :HALF]), mm(odd, x[:, :HALF])], axis=1)
    last = jnp.concatenate([mm(pick, x[:, HALF:]) for pick in each], axis=1)
    y = expert_rows(jnp.concatenate([main, last], axis=0).astype(bf16), wg_ref, wd_ref)
    main, last = y[: 4 * n], y[4 * n :]
    out = mm_tn(even, main[:, :HALF]) + mm_tn(odd, main[:, HALF:])
    tail = jnp.zeros((8 * n, PIECE), f32)
    for q, pick in enumerate(each):
        tail = tail + mm_tn(pick, last[:, q * PIECE : (q + 1) * PIECE])
    out_ref[:, :, :HALF] = out.astype(bf16).reshape(n, 8, HALF)
    out_ref[:, :, HALF:] = tail.astype(bf16).reshape(n, 8, PIECE)


def run_expert(kernel, rows, w_gate_up, w_down):
    width = rows.shape[2]
    per = 32
    return pl.pallas_call(
        kernel,
        out_shape=jax.ShapeDtypeStruct(rows.shape, bf16),
        grid=(rows.shape[0] // per,),
        in_specs=[
            pl.BlockSpec((per, 8, width), lambda i: (i, 0, 0)),
            pl.BlockSpec(w_gate_up.shape, lambda i: (0, 0, 0), pipeline_mode=pl.Buffered(1)),
            pl.BlockSpec(w_down.shape, lambda i: (0, 0, 0), pipeline_mode=pl.Buffered(1)),
        ],
        out_specs=pl.BlockSpec((per, 8, width), lambda i: (i, 0, 0)),
        compiler_params=grant(32),
    )(rows, w_gate_up, w_down)


def weighted(weight, back):
    high = weight.astype(bf16)
    low = (weight - high.astype(f32)).astype(bf16)
    both = mm_tn(jnp.concatenate([high, low], axis=1), back)
    return both[:TOK] + both[TOK:]


CG = 16


def combine_kernel(ids_ref, gates_ref, hid_ref, back_ref, out_ref, rank_scr, gate_scr):
    step = pl.program_id(0)

    @pl.when(step == 0)
    def _():
        rank_scr[...] = rank_table(ids_ref)
        gate_scr[...] = gate_table(ids_ref, gates_ref)
        out_ref[...] = hid_ref[...].astype(f32)

    ranks = rank_scr[pl.ds(step * CG, CG), :]
    gates = gate_scr[pl.ds(step * CG, CG), :]
    back = back_ref[...].reshape(2 * CG * SLOTS_A, D)
    out_ref[...] += weighted(whole_rows(ranks, CG, 2, gates), back)


def combine(ids_t, gates_t, hidden, back):
    return pl.pallas_call(
        combine_kernel,
        out_shape=jax.ShapeDtypeStruct((TOK, D), f32),
        grid=(EXPERTS // CG,),
        in_specs=[
            pl.BlockSpec((TOP, TOK), lambda i: (0, 0)),
            pl.BlockSpec((TOP, TOK), lambda i: (0, 0)),
            pl.BlockSpec((TOK, D), lambda i: (0, 0)),
            pl.BlockSpec((2 * CG, 8, D), lambda i: (i, 0, 0)),
        ],
        out_specs=pl.BlockSpec((TOK, D), lambda i: (0, 0)),
        scratch_shapes=[pltpu.VMEM((EXPERTS, TOK), f32), pltpu.VMEM((EXPERTS, TOK), f32)],
        name="combine_a",
        compiler_params=grant(32),
    )(ids_t, gates_t, hidden, back)


def combine_packed_kernel(ids_ref, gates_ref, sum_ref, back_ref, out_ref, acc_ref):
    ranks = rank_table(ids_ref)
    gates = gate_table(ids_ref, gates_ref)
    back = back_ref[...].reshape(2 * EXPERTS * 8, WIDTH_B)
    lower, upper, last = packed_rows(ranks, EXPERTS, 2, gates)
    acc_ref[:, :HALF] = sum_ref[:, :HALF] + weighted(lower, back[:, :HALF])
    acc_ref[:, HALF:] = sum_ref[:, HALF:] + weighted(upper, back[:, :HALF])
    for q, piece in enumerate(pieces_of(last)):
        acc_ref[:, q * PIECE : (q + 1) * PIECE] += weighted(piece, back[:, HALF:])
    out_ref[...] = acc_ref[...].astype(bf16)


def combine_packed(ids_t, gates_t, base, back):
    return pl.pallas_call(
        combine_packed_kernel,
        out_shape=jax.ShapeDtypeStruct((TOK, D), bf16),
        in_specs=[pl.BlockSpec(memory_space=pltpu.VMEM)] * 4,
        out_specs=pl.BlockSpec(memory_space=pltpu.VMEM),
        scratch_shapes=[pltpu.VMEM((TOK, D), f32)],
        name="combine_b",
        compiler_params=grant(24),
    )(ids_t, gates_t, base, back)


def shift(axis, k):
    pairs = []
    for x in range(4):
        for y in range(4):
            tx, ty = ((x + k) % 4, y) if axis == "x" else (x, (y + k) % 4)
            pairs.append((x * 4 + y, tx * 4 + ty))
    return pairs


def hop(a, axis, k):
    return lax.ppermute(a, "wide", shift(axis, k))


def gather_row(own, first):
    far = hop(own, first, 2)
    near = [hop(own, first, 1), hop(own, first, -1)]
    return jnp.concatenate([own, *near, far], axis=0)


def gather_rest(row, second):
    ahead, behind = hop(row, second, 1), hop(row, second, -1)
    half = row.shape[0] // 2
    far0, far1 = hop(ahead[:half], second, 1), hop(behind[half:], second, -1)
    return [ahead, behind, far0, far1]


def pack_prefix(latent, rope):
    packed = rope.reshape(4, 16, TOK).transpose(1, 0, 2).reshape(16, 4 * TOK)
    return jnp.concatenate([latent, packed], axis=0)


def exchange(a):
    return lax.all_to_all(a, ("req", "wide"), split_axis=0, concat_axis=0, tiled=True)


def layer(
    queries,
    suffix_latent,
    suffix_rope,
    residual,
    prefix_latent,
    prefix_rope,
    suffix_lengths,
    prefix_ids,
    w_ukv,
    w_out,
    norm_gain,
    expert_ids,
    gate_values,
    expert_gate_up,
    expert_down,
):
    scalars = jnp.concatenate([suffix_lengths[0], prefix_ids[0]])
    row0 = gather_row(pack_prefix(prefix_latent[0, 0], prefix_rope[0, 0]), "x")
    row1 = gather_row(pack_prefix(prefix_latent[0, 1], prefix_rope[0, 1]), "y")
    rest0 = gather_rest(row0, "y")
    rest1 = gather_rest(row1, "x")
    qa, qr = prepare_queries(scalars, queries, w_ukv)
    o_lat = attend(scalars, qa, qr, suffix_latent, suffix_rope, [row0, *rest0], [row1, *rest1])
    hidden, normed = project(scalars, o_lat, w_ukv, w_out, residual, norm_gain.reshape(1, D))
    ids_t = expert_ids.T
    gates_t = gate_values.T
    sent_a = dispatch(dispatch_kernel, D, ids_t, normed)
    sent_b = dispatch(dispatch_packed_kernel, WIDTH_B, ids_t, normed)
    rows_a = exchange(sent_a)
    rows_b = exchange(sent_b)
    made_a = run_expert(expert_kernel, rows_a, expert_gate_up, expert_down)
    made_b = run_expert(expert_packed_kernel, rows_b, expert_gate_up, expert_down)
    back_a = exchange(made_a)
    back_b = exchange(made_b)
    part = combine(ids_t, gates_t, hidden, back_a)
    return combine_packed(ids_t, gates_t, part, back_b)


def solution(mesh):
    return jax.shard_map(
        layer,
        mesh=mesh,
        in_specs=(
            P(("req", "wide"), None),
            P(("req", "wide"), None),
            P(None, ("req", "wide")),
            P(("req", "wide"), None),
            P("req", None, "wide", None),
            P("req", None, None, "wide"),
            P(("req", "wide"), None),
            P(("req", "wide"), None),
            P(),
            P(),
            P(),
            P(("req", "wide"), None),
            P(("req", "wide"), None),
            P(("req", "wide"), None, None),
            P(("req", "wide"), None, None),
        ),
        out_specs=P(("req", "wide"), None),
        check_vma=False,
    )
```

```python
import jax
import jax.numpy as jnp
from jax import lax
from jax.experimental import pallas as pl
from jax.experimental.pallas import tpu as pltpu
from jax.sharding import PartitionSpec as P


D = 2048
HEADS = 16
NOPE = 128
ROPE = 64
LAT = 512
TOP = 6
PREF = 2
EXPERTS = 64
TOK = 128
REQS = 4
TILE = 16
CAP = 13
SLOTS_A = 8
HALF = D // 2
PIECE = D // 8
WIDTH_B = HALF + PIECE
BLK = 144
EPS = 1e-06
SCALE = 1.0 / (NOPE + ROPE) ** 0.5
LOG2E = 1.4426950408889634
NEG = -1e30
bf16 = jnp.bfloat16
f32 = jnp.float32


def request_scalars(sc_ref):
    lens = [sc_ref[r] for r in range(REQS)]
    own = [sc_ref[REQS + r] for r in range(REQS)]
    starts, total = [], 0
    for r in range(REQS):
        starts.append(total)
        total = total + lens[r]
    zero_count = sum(jnp.where(own[r] == 0, lens[r], 0) for r in range(REQS))
    bases, next0, next1 = [], 0, zero_count
    for r in range(REQS):
        is0 = own[r] == 0
        bases.append(jnp.where(is0, next0, next1))
        next0 = next0 + jnp.where(is0, lens[r], 0)
        next1 = next1 + jnp.where(is0, 0, lens[r])
    return lens, starts, bases, zero_count


def place_of(tokens, starts, bases):
    place = tokens - starts[0] + bases[0]
    for r in range(1, REQS):
        place = jnp.where(tokens >= starts[r], tokens - starts[r] + bases[r], place)
    return place


def sort_matrix(sc_ref, transposed):
    _, starts, bases, _ = request_scalars(sc_ref)
    token_dim = 0 if transposed else 1
    tokens = lax.broadcasted_iota(jnp.int32, (TOK, TOK), token_dim)
    slots = lax.broadcasted_iota(jnp.int32, (TOK, TOK), 1 - token_dim)
    return jnp.where(place_of(tokens, starts, bases) == slots, 1.0, 0.0).astype(bf16)


def grant(mib):
    return pltpu.CompilerParams(vmem_limit_bytes=mib << 20)


def mm(a, b):
    return jnp.dot(a, b, preferred_element_type=f32)


def mm_nt(a, b):
    return lax.dot_general(a, b, (((1,), (1,)), ((), ())), preferred_element_type=f32)


def mm_tn(a, b):
    return lax.dot_general(a, b, (((0,), (0,)), ((), ())), preferred_element_type=f32)


HG = 4


def query_kernel(sc_ref, q_ref, qr_ref, w_ref, qa_ref, qo_ref):
    order = sort_matrix(sc_ref, False)
    nope = mm(order, q_ref[...]).astype(bf16)
    rope = mm(order, qr_ref[...]).astype(bf16)
    for h in range(HG):
        keys = w_ref[:, h * 256 : h * 256 + 128]
        qa_ref[h] = mm_nt(nope[:, h * 128 : (h + 1) * 128], keys).astype(bf16)
        qo_ref[h] = rope[:, h * ROPE : (h + 1) * ROPE]


def prepare_queries(scalars, queries, w_ukv):
    return pl.pallas_call(
        query_kernel,
        out_shape=(
            jax.ShapeDtypeStruct((HEADS, TOK, LAT), bf16),
            jax.ShapeDtypeStruct((HEADS, TOK, ROPE), bf16),
        ),
        grid_spec=pltpu.PrefetchScalarGridSpec(
            num_scalar_prefetch=1,
            grid=(HEADS // HG,),
            in_specs=[
                pl.BlockSpec((TOK, HG * NOPE), lambda i, s: (0, i)),
                pl.BlockSpec((TOK, HG * ROPE), lambda i, s: (0, HEADS * NOPE // (HG * ROPE) + i)),
                pl.BlockSpec((LAT, HG * 2 * NOPE), lambda i, s: (0, i)),
            ],
            out_specs=[
                pl.BlockSpec((HG, TOK, LAT), lambda i, s: (i, 0, 0)),
                pl.BlockSpec((HG, TOK, ROPE), lambda i, s: (i, 0, 0)),
            ],
        ),
        name="query_prep",
        compiler_params=grant(24),
    )(scalars, queries, queries, w_ukv)


ROWS = HEADS * TILE


def block_views(refs):
    views = []
    for ref in refs:
        for b in range(ref.shape[0] // BLK):
            views.append((ref, b * BLK))
    return views


def unpack_rope(ref, at):
    return jnp.concatenate(
        [ref[at + 128 : at + 144, j * 128 : (j + 1) * 128] for j in range(4)], axis=0
    )


def attention_kernel(n_pieces, sc_ref, qa_ref, qr_ref, ll_ref, lr_ref, *rest):
    pieces = (rest[:n_pieces], rest[n_pieces : 2 * n_pieces])
    o_ref, s_scr, n_scr = rest[2 * n_pieces :]
    lens, starts, bases, zero_count = request_scalars(sc_ref)
    first = pl.program_id(0) * TILE
    c = SCALE * LOG2E

    for pre in range(PREF):
        needed = (first < zero_count) if pre == 0 else (first + TILE > zero_count)

        @pl.when(needed)
        def _(pre=pre):
            q = qa_ref[...].reshape(ROWS, LAT)
            qr = qr_ref[...].reshape(ROWS, ROPE)
            places = first + lax.broadcasted_iota(jnp.int32, (TILE, TOK), 0)
            keys_at = lax.broadcasted_iota(jnp.int32, (TILE, TOK), 1)
            bias = jnp.full((TILE, TOK), NEG, f32)
            for r in range(REQS):
                mine = (places >= bases[r]) & (places < bases[r] + lens[r])
                tok = places - bases[r] + starts[r]
                ok = mine & (keys_at >= starts[r]) & (keys_at <= tok)
                bias = jnp.where(ok, 0.0, bias)
            local_lat = ll_ref[...]
            s = mm_nt(q, local_lat) + mm(qr, lr_ref[...])
            s = (s.reshape(HEADS, TILE, TOK) + bias[None]).reshape(ROWS, TOK)
            n_scr[...] = s
            m = jnp.max(s, axis=1, keepdims=True)
            views = block_views(pieces[pre])
            chunks = [views[k : k + 4] for k in range(0, len(views), 4)]
            for k, chunk in enumerate(chunks):
                lat = jnp.concatenate([ref[at : at + 128, :] for ref, at in chunk], axis=0)
                rope = jnp.concatenate([unpack_rope(ref, at) for ref, at in chunk], axis=1)
                s = mm_nt(q, lat) + mm(qr, rope)
                s_scr[k] = s
                m = jnp.maximum(m, jnp.max(s, axis=1, keepdims=True))
            p = jnp.exp2((n_scr[...] - m) * c)
            total = jnp.sum(p, axis=1, keepdims=True)
            acc = mm(p.astype(bf16), local_lat)
            for k, chunk in enumerate(chunks):
                lat = jnp.concatenate([ref[at : at + 128, :] for ref, at in chunk], axis=0)
                p = jnp.exp2((s_scr[k] - m) * c)
                total = total + jnp.sum(p, axis=1, keepdims=True)
                acc = acc + mm(p.astype(bf16), lat)
            out = (acc / total).astype(bf16).reshape(HEADS, TILE, LAT)
            if pre == 0:
                o_ref[...] = out
            else:
                place = first + lax.broadcasted_iota(jnp.int32, (HEADS, TILE, LAT), 1)
                o_ref[...] = jnp.where(place >= zero_count, out, o_ref[...])


def attend(scalars, qa, qr, local_lat, local_rope, pieces0, pieces1):
    n_pieces = len(pieces0)
    whole = lambda a: pl.BlockSpec(a.shape, lambda i, s: (0,) * a.ndim)
    tiled = lambda width: pl.BlockSpec((HEADS, TILE, width), lambda i, s: (0, i, 0))
    pieces = [*pieces0, *pieces1]
    return pl.pallas_call(
        lambda *refs: attention_kernel(n_pieces, *refs),
        out_shape=jax.ShapeDtypeStruct((HEADS, TOK, LAT), bf16),
        grid_spec=pltpu.PrefetchScalarGridSpec(
            num_scalar_prefetch=1,
            grid=(TOK // TILE,),
            in_specs=[
                tiled(LAT),
                tiled(ROPE),
                whole(local_lat),
                whole(local_rope),
                *[pl.BlockSpec(memory_space=pltpu.VMEM) for _ in pieces],
            ],
            out_specs=tiled(LAT),
            scratch_shapes=[pltpu.VMEM((4, ROWS, 512), f32), pltpu.VMEM((ROWS, TOK), f32)],
        ),
        name="attention",
        compiler_params=grant(24),
    )(scalars, qa, qr, local_lat, local_rope, *pieces)


def project_kernel(
    sc_ref, o_ref, w_ref, wo_ref, res_ref, gain_ref, ids_ref,
    hid_ref, norm_ref, sent_ref, acc_ref, rank_scr, sent_scr, sems,
):
    step = pl.program_id(0)

    @pl.when(step == 0)
    def _():
        acc_ref[...] = res_ref[...].astype(f32)
        rank_scr[...] = rank_table(ids_ref)

    back = sort_matrix(sc_ref, True)
    heads = [mm(o_ref[h], w_ref[:, h * 256 + 128 : h * 256 + 256]).astype(bf16) for h in range(HG)]
    head_out = mm(back, jnp.concatenate(heads, axis=1)).astype(bf16)
    acc_ref[...] += mm(head_out, wo_ref[...])

    @pl.when(step == HEADS // HG - 1)
    def _():
        hidden = acc_ref[...].astype(bf16)
        hid_ref[...] = hidden
        h32 = hidden.astype(f32)
        inverse = lax.rsqrt(jnp.mean(h32 * h32, axis=1, keepdims=True) + EPS)
        norm_ref[...] = (h32 * inverse * gain_ref[...].astype(f32)).astype(bf16)
        copies = []
        for g in range(EXPERTS // EG):
            part = pl.ds(g * EG, EG)
            rows = whole_rows(rank_scr[g * EG : (g + 1) * EG, :], EG, 1).astype(bf16)
            sent = mm(rows, norm_ref[...]).astype(bf16)
            sent_scr[part] = sent.reshape(EG, SLOTS_A, D)
            for half in range(2):
                copy = pltpu.make_async_copy(
                    sent_scr.at[part], sent_ref.at[part, half], sems.at[g, half]
                )
                copy.start()
                copies.append(copy)
        for copy in copies:
            copy.wait()


def project(scalars, o_lat, w_ukv, w_out, residual, gain, ids_t):
    return pl.pallas_call(
        project_kernel,
        out_shape=(
            pltpu.HBM((TOK, D), bf16),
            jax.ShapeDtypeStruct((TOK, D), bf16),
            pltpu.HBM((EXPERTS, 2, SLOTS_A, D), bf16),
        ),
        grid_spec=pltpu.PrefetchScalarGridSpec(
            num_scalar_prefetch=1,
            grid=(HEADS // HG,),
            in_specs=[
                pl.BlockSpec((HG, TOK, LAT), lambda i, s: (i, 0, 0)),
                pl.BlockSpec((LAT, HG * 2 * NOPE), lambda i, s: (0, i)),
                pl.BlockSpec((HG * NOPE, D), lambda i, s: (i, 0)),
                pl.BlockSpec((TOK, D), lambda i, s: (0, 0)),
                pl.BlockSpec((1, D), lambda i, s: (0, 0)),
                pl.BlockSpec((TOP, TOK), lambda i, s: (0, 0)),
            ],
            out_specs=[
                pl.BlockSpec((TOK, D), lambda i, s: (0, 0)),
                pl.BlockSpec((TOK, D), lambda i, s: (0, 0)),
                pl.BlockSpec(memory_space=pltpu.HBM),
            ],
            scratch_shapes=[
                pltpu.VMEM((TOK, D), f32),
                pltpu.VMEM((EXPERTS, TOK), f32),
                pltpu.VMEM((EXPERTS, SLOTS_A, D), bf16),
                pltpu.SemaphoreType.DMA((EXPERTS // EG, 2)),
            ],
        ),
        name="project",
        compiler_params=grant(24),
    )(scalars, o_lat, w_ukv, w_out, residual, gain, ids_t)


def rank_table(ids_ref):
    expert = lax.broadcasted_iota(jnp.int32, (EXPERTS, TOK), 0)
    named = ids_ref[0:1, :] == expert
    for k in range(1, TOP):
        named = named | (ids_ref[k : k + 1, :] == expert)
    earlier = lax.broadcasted_iota(jnp.int32, (TOK, TOK), 0) < lax.broadcasted_iota(
        jnp.int32, (TOK, TOK), 1
    )
    rank = mm(jnp.where(named, 1.0, 0.0).astype(bf16), jnp.where(earlier, 1.0, 0.0).astype(bf16))
    return jnp.where(named, rank, -1.0)


def gate_table(ids_ref, gates_ref):
    expert = lax.broadcasted_iota(jnp.int32, (EXPERTS, TOK), 0)
    gates = jnp.zeros((EXPERTS, TOK), f32)
    for k in range(TOP):
        gates = gates + jnp.where(ids_ref[k : k + 1, :] == expert, gates_ref[k : k + 1, :], 0.0)
    return gates


def whole_rows(ranks, experts, copies, values=None):
    slot = lax.broadcasted_iota(jnp.int32, (SLOTS_A, TOK), 0).astype(f32)
    rows = []
    for e in range(experts):
        on = 1.0 if values is None else values[e : e + 1, :]
        rows += [jnp.where(ranks[e : e + 1, :] == slot, on, 0.0)] * copies
    return jnp.concatenate(rows, axis=0)


def packed_rows(ranks, experts, copies, values=None):
    row = lax.broadcasted_iota(jnp.int32, (8, TOK), 0)
    slot = (SLOTS_A + row // 2).astype(f32)
    even = row % 2 == 0
    lower, upper, last = [], [], []
    for e in range(experts):
        rank = ranks[e : e + 1, :]
        on = 1.0 if values is None else values[e : e + 1, :]
        hit = jnp.where(rank == slot, on, 0.0)
        lower += [jnp.where(even, hit, 0.0)] * copies
        upper += [jnp.where(even, 0.0, hit)] * copies
        last += [jnp.where(jnp.broadcast_to(rank, (8, TOK)) == CAP - 1.0, on, 0.0)] * copies
    return [jnp.concatenate(part, axis=0) for part in (lower, upper, last)]


def pieces_of(last):
    row = lax.broadcasted_iota(jnp.int32, last.shape, 0) % 8
    return [jnp.where(row == q, last, 0.0) for q in range(8)]


EG = 16


def dispatch_packed_kernel(ids_ref, norm_ref, out_ref, rank_scr):
    step = pl.program_id(0)

    @pl.when(step == 0)
    def _():
        rank_scr[...] = rank_table(ids_ref)

    ranks = rank_scr[pl.ds(step * EG, EG), :]
    lower, upper, last = packed_rows(ranks, EG, 1)
    sent = (
        mm(lower.astype(bf16), norm_ref[:, :HALF]) + mm(upper.astype(bf16), norm_ref[:, HALF:])
    ).astype(bf16)
    tail = jnp.zeros((EG * 8, PIECE), f32)
    for q, piece in enumerate(pieces_of(last)):
        tail = tail + mm(piece.astype(bf16), norm_ref[:, q * PIECE : (q + 1) * PIECE])
    tail = tail.astype(bf16)
    for e in range(EG):
        for copy in range(2):
            out_ref[2 * e + copy, :, :HALF] = sent[e * 8 : (e + 1) * 8]
            out_ref[2 * e + copy, :, HALF:] = tail[e * 8 : (e + 1) * 8]


def dispatch(kernel, width, ids_t, normed):
    return pl.pallas_call(
        kernel,
        out_shape=jax.ShapeDtypeStruct((2 * EXPERTS, 8, width), bf16),
        grid=(EXPERTS // EG,),
        in_specs=[
            pl.BlockSpec((TOP, TOK), lambda i: (0, 0)),
            pl.BlockSpec((TOK, D), lambda i: (0, 0)),
        ],
        out_specs=pl.BlockSpec((2 * EG, 8, width), lambda i: (i, 0, 0)),
        scratch_shapes=[pltpu.VMEM((EXPERTS, TOK), f32)],
        compiler_params=grant(32),
    )(ids_t, normed)


def expert_rows(x, wg_ref, wd_ref):
    gate_up = mm(x, wg_ref[0])
    half = gate_up.shape[1] // 2
    gate, up = gate_up[:, :half], gate_up[:, half:]
    act = (gate / (1.0 + jnp.exp(-gate)) * up).astype(bf16)
    return mm(act, wd_ref[0]).astype(bf16)


def expert_kernel(x_ref, wg_ref, wd_ref, out_ref):
    x = x_ref[...].reshape(-1, D)
    out_ref[...] = expert_rows(x, wg_ref, wd_ref).reshape(out_ref.shape)


def select(rows, columns, stride, offset):
    r = lax.broadcasted_iota(jnp.int32, (rows, columns), 0)
    c = lax.broadcasted_iota(jnp.int32, (rows, columns), 1)
    return jnp.where(c == r * stride + offset, 1.0, 0.0).astype(bf16)


def expert_packed_kernel(x_ref, wg_ref, wd_ref, out_ref):
    n = x_ref.shape[0]
    x = x_ref[...].reshape(8 * n, WIDTH_B)
    even, odd = select(4 * n, 8 * n, 2, 0), select(4 * n, 8 * n, 2, 1)
    each = [select(n, 8 * n, 8, q) for q in range(8)]
    main = jnp.concatenate([mm(even, x[:, :HALF]), mm(odd, x[:, :HALF])], axis=1)
    last = jnp.concatenate([mm(pick, x[:, HALF:]) for pick in each], axis=1)
    y = expert_rows(jnp.concatenate([main, last], axis=0).astype(bf16), wg_ref, wd_ref)
    main, last = y[: 4 * n], y[4 * n :]
    out = mm_tn(even, main[:, :HALF]) + mm_tn(odd, main[:, HALF:])
    tail = jnp.zeros((8 * n, PIECE), f32)
    for q, pick in enumerate(each):
        tail = tail + mm_tn(pick, last[:, q * PIECE : (q + 1) * PIECE])
    out_ref[:, :, :HALF] = out.astype(bf16).reshape(n, 8, HALF)
    out_ref[:, :, HALF:] = tail.astype(bf16).reshape(n, 8, PIECE)


def run_expert(kernel, rows, w_gate_up, w_down):
    width = rows.shape[2]
    per = 32
    return pl.pallas_call(
        kernel,
        out_shape=jax.ShapeDtypeStruct(rows.shape, bf16),
        grid=(rows.shape[0] // per,),
        in_specs=[
            pl.BlockSpec((per, 8, width), lambda i: (i, 0, 0)),
            pl.BlockSpec(w_gate_up.shape, lambda i: (0, 0, 0), pipeline_mode=pl.Buffered(1)),
            pl.BlockSpec(w_down.shape, lambda i: (0, 0, 0), pipeline_mode=pl.Buffered(1)),
        ],
        out_specs=pl.BlockSpec((per, 8, width), lambda i: (i, 0, 0)),
        compiler_params=grant(32),
    )(rows, w_gate_up, w_down)


def weighted(weight, back):
    high = weight.astype(bf16)
    low = (weight - high.astype(f32)).astype(bf16)
    both = mm_tn(jnp.concatenate([high, low], axis=1), back)
    return both[:TOK] + both[TOK:]


CG = 16


def combine_kernel(ids_ref, gates_ref, hid_ref, back_ref, out_ref, rank_scr, gate_scr):
    step = pl.program_id(0)

    @pl.when(step == 0)
    def _():
        rank_scr[...] = rank_table(ids_ref)
        gate_scr[...] = gate_table(ids_ref, gates_ref)
        out_ref[...] = hid_ref[...].astype(f32)

    ranks = rank_scr[pl.ds(step * CG, CG), :]
    gates = gate_scr[pl.ds(step * CG, CG), :]
    back = back_ref[...].reshape(2 * CG * SLOTS_A, D)
    out_ref[...] += weighted(whole_rows(ranks, CG, 2, gates), back)


def combine(ids_t, gates_t, hidden, back):
    return pl.pallas_call(
        combine_kernel,
        out_shape=pltpu.VMEM((TOK, D), f32),
        grid=(EXPERTS // CG,),
        in_specs=[
            pl.BlockSpec((TOP, TOK), lambda i: (0, 0)),
            pl.BlockSpec((TOP, TOK), lambda i: (0, 0)),
            pl.BlockSpec((TOK, D), lambda i: (0, 0)),
            pl.BlockSpec((2 * CG, 8, D), lambda i: (i, 0, 0)),
        ],
        out_specs=pl.BlockSpec((TOK, D), lambda i: (0, 0)),
        scratch_shapes=[pltpu.VMEM((EXPERTS, TOK), f32), pltpu.VMEM((EXPERTS, TOK), f32)],
        name="combine_a",
        compiler_params=grant(32),
    )(ids_t, gates_t, hidden, back)


def last_rows(ranks, values):
    hit = jnp.where(ranks == CAP - 1.0, values, 0.0)
    return jnp.broadcast_to(hit[:, None, :], (EXPERTS, 2, TOK)).reshape(2 * EXPERTS, TOK)


def combine_packed_kernel(ids_ref, gates_ref, sum_ref, back_ref, out_ref, acc_ref, tail_ref):
    ranks = rank_table(ids_ref)
    gates = gate_table(ids_ref, gates_ref)
    back = back_ref[...].reshape(2 * EXPERTS * 8, WIDTH_B)
    for j in range(PIECE // 128):
        tail_ref[j] = back[:, HALF + j * 128 : HALF + (j + 1) * 128].astype(f32)
    lower, upper = packed_rows(ranks, EXPERTS, 2, gates)[:2]
    acc_ref[:, :HALF] = sum_ref[:, :HALF] + weighted(lower, back[:, :HALF])
    acc_ref[:, HALF:] = sum_ref[:, HALF:] + weighted(upper, back[:, :HALF])
    fifth = [
        tail_ref[j, pl.ds(q, 2 * EXPERTS, stride=8), :].astype(bf16)
        for q in range(8)
        for j in range(PIECE // 128)
    ]
    acc = acc_ref[...] + weighted(last_rows(ranks, gates), jnp.concatenate(fifth, axis=1))
    out_ref[...] = acc.astype(bf16)


def combine_packed(ids_t, gates_t, base, back):
    return pl.pallas_call(
        combine_packed_kernel,
        out_shape=jax.ShapeDtypeStruct((TOK, D), bf16),
        in_specs=[pl.BlockSpec(memory_space=pltpu.VMEM)] * 4,
        out_specs=pl.BlockSpec(memory_space=pltpu.VMEM),
        scratch_shapes=[
            pltpu.VMEM((TOK, D), f32),
            pltpu.VMEM((PIECE // 128, 2 * EXPERTS * 8, 128), f32),
        ],
        name="combine_b",
        compiler_params=grant(24),
    )(ids_t, gates_t, base, back)


def shift(axis, k):
    pairs = []
    for x in range(4):
        for y in range(4):
            tx, ty = ((x + k) % 4, y) if axis == "x" else (x, (y + k) % 4)
            pairs.append((x * 4 + y, tx * 4 + ty))
    return pairs


def hop(a, axis, k):
    return lax.ppermute(a, "wide", shift(axis, k))


def gather_row(own, first):
    far = hop(own, first, 2)
    near = [hop(own, first, 1), hop(own, first, -1)]
    return jnp.concatenate([own, *near, far], axis=0)


def gather_rest(row, second):
    ahead, behind = hop(row, second, 1), hop(row, second, -1)
    half = row.shape[0] // 2
    far0, far1 = hop(ahead[:half], second, 1), hop(behind[half:], second, -1)
    return [ahead, behind, far0, far1]


def pack_prefix(latent, rope):
    packed = rope.reshape(4, 16, TOK).transpose(1, 0, 2).reshape(16, 4 * TOK)
    return jnp.concatenate([latent, packed], axis=0)


def exchange(a):
    return lax.all_to_all(a, ("req", "wide"), split_axis=0, concat_axis=0, tiled=True)


def layer(
    queries,
    suffix_latent,
    suffix_rope,
    residual,
    prefix_latent,
    prefix_rope,
    suffix_lengths,
    prefix_ids,
    w_ukv,
    w_out,
    norm_gain,
    expert_ids,
    gate_values,
    expert_gate_up,
    expert_down,
):
    scalars = jnp.concatenate([suffix_lengths[0], prefix_ids[0]])
    row0 = gather_row(pack_prefix(prefix_latent[0, 0], prefix_rope[0, 0]), "x")
    row1 = gather_row(pack_prefix(prefix_latent[0, 1], prefix_rope[0, 1]), "y")
    rest0 = gather_rest(row0, "y")
    rest1 = gather_rest(row1, "x")
    qa, qr = prepare_queries(scalars, queries, w_ukv)
    o_lat = attend(scalars, qa, qr, suffix_latent, suffix_rope, [row0, *rest0], [row1, *rest1])
    ids_t = expert_ids.T
    gates_t = gate_values.T
    hidden, normed, sent_a = project(
        scalars, o_lat, w_ukv, w_out, residual, norm_gain.reshape(1, D), ids_t
    )
    sent_a = sent_a.reshape(2 * EXPERTS, SLOTS_A, D)
    sent_b = dispatch(dispatch_packed_kernel, WIDTH_B, ids_t, normed)
    rows_a = exchange(sent_a)
    rows_b = exchange(sent_b)
    made_a = run_expert(expert_kernel, rows_a, expert_gate_up, expert_down)
    made_b = run_expert(expert_packed_kernel, rows_b, expert_gate_up, expert_down)
    back_a = exchange(made_a)
    back_b = exchange(made_b)
    part = combine(ids_t, gates_t, hidden, back_a)
    return combine_packed(ids_t, gates_t, part, back_b)


def solution(mesh):
    return jax.shard_map(
        layer,
        mesh=mesh,
        in_specs=(
            P(("req", "wide"), None),
            P(("req", "wide"), None),
            P(None, ("req", "wide")),
            P(("req", "wide"), None),
            P("req", None, "wide", None),
            P("req", None, None, "wide"),
            P(("req", "wide"), None),
            P(("req", "wide"), None),
            P(),
            P(),
            P(),
            P(("req", "wide"), None),
            P(("req", "wide"), None),
            P(("req", "wide"), None, None),
            P(("req", "wide"), None, None),
        ),
        out_specs=P(("req", "wide"), None),
        check_vma=False,
    )
```

```python
import jax
import jax.numpy as jnp
from jax import lax
from jax.experimental import pallas as pl
from jax.experimental.pallas import tpu as pltpu
from jax.sharding import PartitionSpec as P


D = 2048
HEADS = 16
NOPE = 128
ROPE = 64
LAT = 512
TOP = 6
PREF = 2
EXPERTS = 64
TOK = 128
REQS = 4
TILE = 16
CAP = 13
SLOTS_A = 8
HALF = D // 2
PIECE = D // 8
WIDTH_B = HALF + PIECE
BLK = 144
EPS = 1e-06
SCALE = 1.0 / (NOPE + ROPE) ** 0.5
LOG2E = 1.4426950408889634
NEG = -1e30
bf16 = jnp.bfloat16
f32 = jnp.float32


def request_scalars(sc_ref):
    lens = [sc_ref[r] for r in range(REQS)]
    own = [sc_ref[REQS + r] for r in range(REQS)]
    starts, total = [], 0
    for r in range(REQS):
        starts.append(total)
        total = total + lens[r]
    zero_count = sum(jnp.where(own[r] == 0, lens[r], 0) for r in range(REQS))
    bases, next0, next1 = [], 0, zero_count
    for r in range(REQS):
        is0 = own[r] == 0
        bases.append(jnp.where(is0, next0, next1))
        next0 = next0 + jnp.where(is0, lens[r], 0)
        next1 = next1 + jnp.where(is0, 0, lens[r])
    return lens, starts, bases, zero_count


def place_of(tokens, starts, bases):
    place = tokens - starts[0] + bases[0]
    for r in range(1, REQS):
        place = jnp.where(tokens >= starts[r], tokens - starts[r] + bases[r], place)
    return place


def sort_matrix(sc_ref, transposed):
    _, starts, bases, _ = request_scalars(sc_ref)
    token_dim = 0 if transposed else 1
    tokens = lax.broadcasted_iota(jnp.int32, (TOK, TOK), token_dim)
    slots = lax.broadcasted_iota(jnp.int32, (TOK, TOK), 1 - token_dim)
    return jnp.where(place_of(tokens, starts, bases) == slots, 1.0, 0.0).astype(bf16)


def grant(mib):
    return pltpu.CompilerParams(vmem_limit_bytes=mib << 20)


def in_hbm(a):
    return pltpu.with_memory_space_constraint(a, pltpu.HBM)


def mm(a, b):
    return jnp.dot(a, b, preferred_element_type=f32)


def mm_nt(a, b):
    return lax.dot_general(a, b, (((1,), (1,)), ((), ())), preferred_element_type=f32)


def mm_tn(a, b):
    return lax.dot_general(a, b, (((0,), (0,)), ((), ())), preferred_element_type=f32)


HG = 4


def query_kernel(sc_ref, q_ref, qr_ref, w_ref, qa_ref, qo_ref):
    order = sort_matrix(sc_ref, False)
    nope = mm(order, q_ref[...]).astype(bf16)
    rope = mm(order, qr_ref[...]).astype(bf16)
    for h in range(HG):
        keys = w_ref[:, h * 256 : h * 256 + 128]
        qa_ref[h] = mm_nt(nope[:, h * 128 : (h + 1) * 128], keys).astype(bf16)
        qo_ref[h] = rope[:, h * ROPE : (h + 1) * ROPE]


def prepare_queries(scalars, queries, w_ukv):
    return pl.pallas_call(
        query_kernel,
        out_shape=(
            jax.ShapeDtypeStruct((HEADS, TOK, LAT), bf16),
            jax.ShapeDtypeStruct((HEADS, TOK, ROPE), bf16),
        ),
        grid_spec=pltpu.PrefetchScalarGridSpec(
            num_scalar_prefetch=1,
            grid=(HEADS // HG,),
            in_specs=[
                pl.BlockSpec((TOK, HG * NOPE), lambda i, s: (0, i)),
                pl.BlockSpec((TOK, HG * ROPE), lambda i, s: (0, HEADS * NOPE // (HG * ROPE) + i)),
                pl.BlockSpec((LAT, HG * 2 * NOPE), lambda i, s: (0, i)),
            ],
            out_specs=[
                pl.BlockSpec((HG, TOK, LAT), lambda i, s: (i, 0, 0)),
                pl.BlockSpec((HG, TOK, ROPE), lambda i, s: (i, 0, 0)),
            ],
        ),
        name="query_prep",
        compiler_params=grant(24),
    )(scalars, queries, queries, w_ukv)


ROWS = HEADS * TILE


def block_views(refs):
    views = []
    for ref in refs:
        for b in range(ref.shape[0] // BLK):
            views.append((ref, b * BLK))
    return views


def unpack_rope(ref, at):
    return jnp.concatenate(
        [ref[at + 128 : at + 144, j * 128 : (j + 1) * 128] for j in range(4)], axis=0
    )


def attention_kernel(n_pieces, sc_ref, qa_ref, qr_ref, ll_ref, lr_ref, *rest):
    pieces = (rest[:n_pieces], rest[n_pieces : 2 * n_pieces])
    o_ref, s_scr, n_scr = rest[2 * n_pieces :]
    lens, starts, bases, zero_count = request_scalars(sc_ref)
    first = pl.program_id(0) * TILE
    c = SCALE * LOG2E

    for pre in range(PREF):
        needed = (first < zero_count) if pre == 0 else (first + TILE > zero_count)

        @pl.when(needed)
        def _(pre=pre):
            q = qa_ref[...].reshape(ROWS, LAT)
            qr = qr_ref[...].reshape(ROWS, ROPE)
            places = first + lax.broadcasted_iota(jnp.int32, (TILE, TOK), 0)
            keys_at = lax.broadcasted_iota(jnp.int32, (TILE, TOK), 1)
            bias = jnp.full((TILE, TOK), NEG, f32)
            for r in range(REQS):
                mine = (places >= bases[r]) & (places < bases[r] + lens[r])
                tok = places - bases[r] + starts[r]
                ok = mine & (keys_at >= starts[r]) & (keys_at <= tok)
                bias = jnp.where(ok, 0.0, bias)
            local_lat = ll_ref[...]
            s = mm_nt(q, local_lat) + mm(qr, lr_ref[...])
            s = (s.reshape(HEADS, TILE, TOK) + bias[None]).reshape(ROWS, TOK)
            n_scr[...] = s
            m = jnp.max(s, axis=1, keepdims=True)
            views = block_views(pieces[pre])
            chunks = [views[k : k + 4] for k in range(0, len(views), 4)]
            for k, chunk in enumerate(chunks):
                lat = jnp.concatenate([ref[at : at + 128, :] for ref, at in chunk], axis=0)
                rope = jnp.concatenate([unpack_rope(ref, at) for ref, at in chunk], axis=1)
                s = mm_nt(q, lat) + mm(qr, rope)
                s_scr[k] = s
                m = jnp.maximum(m, jnp.max(s, axis=1, keepdims=True))
            p = jnp.exp2((n_scr[...] - m) * c)
            total = jnp.sum(p, axis=1, keepdims=True)
            acc = mm(p.astype(bf16), local_lat)
            for k, chunk in enumerate(chunks):
                lat = jnp.concatenate([ref[at : at + 128, :] for ref, at in chunk], axis=0)
                p = jnp.exp2((s_scr[k] - m) * c)
                total = total + jnp.sum(p, axis=1, keepdims=True)
                acc = acc + mm(p.astype(bf16), lat)
            out = (acc / total).astype(bf16).reshape(HEADS, TILE, LAT)
            if pre == 0:
                o_ref[...] = out
            else:
                place = first + lax.broadcasted_iota(jnp.int32, (HEADS, TILE, LAT), 1)
                o_ref[...] = jnp.where(place >= zero_count, out, o_ref[...])


def attend(scalars, qa, qr, local_lat, local_rope, pieces0, pieces1):
    n_pieces = len(pieces0)
    whole = lambda a: pl.BlockSpec(a.shape, lambda i, s: (0,) * a.ndim)
    tiled = lambda width: pl.BlockSpec((HEADS, TILE, width), lambda i, s: (0, i, 0))
    pieces = [*pieces0, *pieces1]
    return pl.pallas_call(
        lambda *refs: attention_kernel(n_pieces, *refs),
        out_shape=jax.ShapeDtypeStruct((HEADS, TOK, LAT), bf16),
        grid_spec=pltpu.PrefetchScalarGridSpec(
            num_scalar_prefetch=1,
            grid=(TOK // TILE,),
            in_specs=[
                tiled(LAT),
                tiled(ROPE),
                whole(local_lat),
                whole(local_rope),
                *[pl.BlockSpec(memory_space=pltpu.VMEM) for _ in pieces],
            ],
            out_specs=tiled(LAT),
            scratch_shapes=[pltpu.VMEM((4, ROWS, 512), f32), pltpu.VMEM((ROWS, TOK), f32)],
        ),
        name="attention",
        compiler_params=grant(24),
    )(scalars, qa, qr, local_lat, local_rope, *pieces)


DG = 32


def project_kernel(
    sc_ref, o_ref, w_ref, wo_ref, res_ref, gain_ref, ids_ref,
    hid_ref, norm_ref, sent_ref, acc_ref, rank_scr, sent_scr, sems,
):
    step = pl.program_id(0)

    @pl.when(step == 0)
    def _():
        acc_ref[...] = res_ref[...].astype(f32)
        rank_scr[...] = rank_table(ids_ref)

    back = sort_matrix(sc_ref, True)
    heads = [mm(o_ref[h], w_ref[:, h * 256 + 128 : h * 256 + 256]).astype(bf16) for h in range(HG)]
    head_out = mm(back, jnp.concatenate(heads, axis=1)).astype(bf16)
    acc_ref[...] += mm(head_out, wo_ref[...])

    @pl.when(step == HEADS // HG - 1)
    def _():
        hidden = acc_ref[...].astype(bf16)
        hid_ref[...] = hidden
        h32 = hidden.astype(f32)
        inverse = lax.rsqrt(jnp.mean(h32 * h32, axis=1, keepdims=True) + EPS)
        norm_ref[...] = (h32 * inverse * gain_ref[...].astype(f32)).astype(bf16)
        copies = []
        for g in range(EXPERTS // DG):
            part = pl.ds(g * DG, DG)
            rows = whole_rows(rank_scr[g * DG : (g + 1) * DG, :], DG, 1).astype(bf16)
            sent = mm(rows, norm_ref[...]).astype(bf16)
            sent_scr[part] = sent.reshape(DG, SLOTS_A, D)
            for half in range(2):
                copy = pltpu.make_async_copy(
                    sent_scr.at[part], sent_ref.at[part, half], sems.at[g, half]
                )
                copy.start()
                copies.append(copy)
        for copy in copies:
            copy.wait()


def project(scalars, o_lat, w_ukv, w_out, residual, gain, ids_t):
    return pl.pallas_call(
        project_kernel,
        out_shape=(
            pltpu.HBM((TOK, D), bf16),
            jax.ShapeDtypeStruct((TOK, D), bf16),
            pltpu.HBM((EXPERTS, 2, SLOTS_A, D), bf16),
        ),
        grid_spec=pltpu.PrefetchScalarGridSpec(
            num_scalar_prefetch=1,
            grid=(HEADS // HG,),
            in_specs=[
                pl.BlockSpec((HG, TOK, LAT), lambda i, s: (i, 0, 0)),
                pl.BlockSpec((LAT, HG * 2 * NOPE), lambda i, s: (0, i)),
                pl.BlockSpec((HG * NOPE, D), lambda i, s: (i, 0)),
                pl.BlockSpec((TOK, D), lambda i, s: (0, 0)),
                pl.BlockSpec((1, D), lambda i, s: (0, 0)),
                pl.BlockSpec((TOP, TOK), lambda i, s: (0, 0)),
            ],
            out_specs=[
                pl.BlockSpec((TOK, D), lambda i, s: (0, 0)),
                pl.BlockSpec((TOK, D), lambda i, s: (0, 0)),
                pl.BlockSpec(memory_space=pltpu.HBM),
            ],
            scratch_shapes=[
                pltpu.VMEM((TOK, D), f32),
                pltpu.VMEM((EXPERTS, TOK), f32),
                pltpu.VMEM((EXPERTS, SLOTS_A, D), bf16),
                pltpu.SemaphoreType.DMA((EXPERTS // DG, 2)),
            ],
        ),
        name="project",
        compiler_params=grant(24),
    )(scalars, o_lat, w_ukv, w_out, residual, gain, ids_t)


def rank_table(ids_ref):
    expert = lax.broadcasted_iota(jnp.int32, (EXPERTS, TOK), 0)
    named = ids_ref[0:1, :] == expert
    for k in range(1, TOP):
        named = named | (ids_ref[k : k + 1, :] == expert)
    earlier = lax.broadcasted_iota(jnp.int32, (TOK, TOK), 0) < lax.broadcasted_iota(
        jnp.int32, (TOK, TOK), 1
    )
    rank = mm(jnp.where(named, 1.0, 0.0).astype(bf16), jnp.where(earlier, 1.0, 0.0).astype(bf16))
    return jnp.where(named, rank, -1.0)


def gate_table(ids_ref, gates_ref):
    expert = lax.broadcasted_iota(jnp.int32, (EXPERTS, TOK), 0)
    gates = jnp.zeros((EXPERTS, TOK), f32)
    for k in range(TOP):
        gates = gates + jnp.where(ids_ref[k : k + 1, :] == expert, gates_ref[k : k + 1, :], 0.0)
    return gates


def whole_rows(ranks, experts, copies, values=None):
    slot = lax.broadcasted_iota(jnp.int32, (SLOTS_A, TOK), 0).astype(f32)
    rows = []
    for e in range(experts):
        on = 1.0 if values is None else values[e : e + 1, :]
        rows += [jnp.where(ranks[e : e + 1, :] == slot, on, 0.0)] * copies
    return jnp.concatenate(rows, axis=0)


def packed_rows(ranks, experts, copies, values=None):
    row = lax.broadcasted_iota(jnp.int32, (8, TOK), 0)
    slot = (SLOTS_A + row // 2).astype(f32)
    even = row % 2 == 0
    lower, upper, last = [], [], []
    for e in range(experts):
        rank = ranks[e : e + 1, :]
        on = 1.0 if values is None else values[e : e + 1, :]
        hit = jnp.where(rank == slot, on, 0.0)
        lower += [jnp.where(even, hit, 0.0)] * copies
        upper += [jnp.where(even, 0.0, hit)] * copies
        last += [jnp.where(jnp.broadcast_to(rank, (8, TOK)) == CAP - 1.0, on, 0.0)] * copies
    return [jnp.concatenate(part, axis=0) for part in (lower, upper, last)]


def pieces_of(last):
    row = lax.broadcasted_iota(jnp.int32, last.shape, 0) % 8
    return [jnp.where(row == q, last, 0.0) for q in range(8)]


EG = 16


def dispatch_packed_kernel(ids_ref, norm_ref, out_ref, rank_scr):
    step = pl.program_id(0)

    @pl.when(step == 0)
    def _():
        rank_scr[...] = rank_table(ids_ref)

    ranks = rank_scr[pl.ds(step * EG, EG), :]
    lower, upper, last = packed_rows(ranks, EG, 1)
    sent = (
        mm(lower.astype(bf16), norm_ref[:, :HALF]) + mm(upper.astype(bf16), norm_ref[:, HALF:])
    ).astype(bf16)
    tail = jnp.zeros((EG * 8, PIECE), f32)
    for q, piece in enumerate(pieces_of(last)):
        tail = tail + mm(piece.astype(bf16), norm_ref[:, q * PIECE : (q + 1) * PIECE])
    tail = tail.astype(bf16)
    for e in range(EG):
        for copy in range(2):
            out_ref[2 * e + copy, :, :HALF] = sent[e * 8 : (e + 1) * 8]
            out_ref[2 * e + copy, :, HALF:] = tail[e * 8 : (e + 1) * 8]


def dispatch(kernel, width, ids_t, normed):
    return pl.pallas_call(
        kernel,
        out_shape=jax.ShapeDtypeStruct((2 * EXPERTS, 8, width), bf16),
        grid=(EXPERTS // EG,),
        in_specs=[
            pl.BlockSpec((TOP, TOK), lambda i: (0, 0)),
            pl.BlockSpec((TOK, D), lambda i: (0, 0)),
        ],
        out_specs=pl.BlockSpec((2 * EG, 8, width), lambda i: (i, 0, 0)),
        scratch_shapes=[pltpu.VMEM((EXPERTS, TOK), f32)],
        compiler_params=grant(32),
    )(ids_t, normed)


def expert_rows(x, wg_ref, wd_ref):
    gate_up = mm(x, wg_ref[0])
    half = gate_up.shape[1] // 2
    gate, up = gate_up[:, :half], gate_up[:, half:]
    act = (gate / (1.0 + jnp.exp(-gate)) * up).astype(bf16)
    return mm(act, wd_ref[0]).astype(bf16)


def expert_kernel(x_ref, wg_ref, wd_ref, out_ref):
    x = x_ref[...].reshape(-1, D)
    out_ref[...] = expert_rows(x, wg_ref, wd_ref).reshape(out_ref.shape)


def select(rows, columns, stride, offset):
    r = lax.broadcasted_iota(jnp.int32, (rows, columns), 0)
    c = lax.broadcasted_iota(jnp.int32, (rows, columns), 1)
    return jnp.where(c == r * stride + offset, 1.0, 0.0).astype(bf16)


def expert_packed_kernel(x_ref, wg_ref, wd_ref, out_ref):
    n = x_ref.shape[0]
    x = x_ref[...].reshape(8 * n, WIDTH_B)
    even, odd = select(4 * n, 8 * n, 2, 0), select(4 * n, 8 * n, 2, 1)
    each = [select(n, 8 * n, 8, q) for q in range(8)]
    main = jnp.concatenate([mm(even, x[:, :HALF]), mm(odd, x[:, :HALF])], axis=1)
    last = jnp.concatenate([mm(pick, x[:, HALF:]) for pick in each], axis=1)
    y = expert_rows(jnp.concatenate([main, last], axis=0).astype(bf16), wg_ref, wd_ref)
    main, last = y[: 4 * n], y[4 * n :]
    out = mm_tn(even, main[:, :HALF]) + mm_tn(odd, main[:, HALF:])
    tail = jnp.zeros((8 * n, PIECE), f32)
    for q, pick in enumerate(each):
        tail = tail + mm_tn(pick, last[:, q * PIECE : (q + 1) * PIECE])
    out_ref[:, :, :HALF] = out.astype(bf16).reshape(n, 8, HALF)
    out_ref[:, :, HALF:] = tail.astype(bf16).reshape(n, 8, PIECE)


def run_expert(kernel, rows, w_gate_up, w_down):
    width = rows.shape[2]
    per = 32
    return pl.pallas_call(
        kernel,
        out_shape=jax.ShapeDtypeStruct(rows.shape, bf16),
        grid=(rows.shape[0] // per,),
        in_specs=[
            pl.BlockSpec((per, 8, width), lambda i: (i, 0, 0)),
            pl.BlockSpec(w_gate_up.shape, lambda i: (0, 0, 0), pipeline_mode=pl.Buffered(1)),
            pl.BlockSpec(w_down.shape, lambda i: (0, 0, 0), pipeline_mode=pl.Buffered(1)),
        ],
        out_specs=pl.BlockSpec((per, 8, width), lambda i: (i, 0, 0)),
        compiler_params=grant(32),
    )(rows, w_gate_up, w_down)


def weighted(weight, back):
    high = weight.astype(bf16)
    low = (weight - high.astype(f32)).astype(bf16)
    both = mm_tn(jnp.concatenate([high, low], axis=1), back)
    return both[:TOK] + both[TOK:]


CG = 16


def combine_kernel(ids_ref, gates_ref, hid_ref, back_ref, out_ref, rank_scr, gate_scr):
    step = pl.program_id(0)

    @pl.when(step == 0)
    def _():
        rank_scr[...] = rank_table(ids_ref)
        gate_scr[...] = gate_table(ids_ref, gates_ref)
        out_ref[...] = hid_ref[...].astype(f32)

    ranks = rank_scr[pl.ds(step * CG, CG), :]
    gates = gate_scr[pl.ds(step * CG, CG), :]
    back = back_ref[...].reshape(2 * CG * SLOTS_A, D)
    out_ref[...] += weighted(whole_rows(ranks, CG, 2, gates), back)


def combine(ids_t, gates_t, hidden, back):
    return pl.pallas_call(
        combine_kernel,
        out_shape=pltpu.HBM((TOK, D), f32),
        grid=(EXPERTS // CG,),
        in_specs=[
            pl.BlockSpec((TOP, TOK), lambda i: (0, 0)),
            pl.BlockSpec((TOP, TOK), lambda i: (0, 0)),
            pl.BlockSpec((TOK, D), lambda i: (0, 0)),
            pl.BlockSpec((2 * CG, 8, D), lambda i: (i, 0, 0)),
        ],
        out_specs=pl.BlockSpec((TOK, D), lambda i: (0, 0)),
        scratch_shapes=[pltpu.VMEM((EXPERTS, TOK), f32), pltpu.VMEM((EXPERTS, TOK), f32)],
        name="combine_a",
        compiler_params=grant(32),
    )(ids_t, gates_t, hidden, back)


def last_rows(ranks, values):
    hit = jnp.where(ranks == CAP - 1.0, values, 0.0)
    return jnp.broadcast_to(hit[:, None, :], (EXPERTS, 2, TOK)).reshape(2 * EXPERTS, TOK)


def combine_packed_kernel(
    ids_ref, gates_ref, sum_hbm, back_ref, out_ref, acc_ref, tail_ref, sum_ref, sem
):
    fetch = pltpu.make_async_copy(sum_hbm, sum_ref, sem)
    fetch.start()
    ranks = rank_table(ids_ref)
    gates = gate_table(ids_ref, gates_ref)
    back = back_ref[...].reshape(2 * EXPERTS * 8, WIDTH_B)
    for j in range(PIECE // 128):
        tail_ref[j] = back[:, HALF + j * 128 : HALF + (j + 1) * 128].astype(f32)
    lower, upper = packed_rows(ranks, EXPERTS, 2, gates)[:2]
    acc_ref[:, :HALF] = weighted(lower, back[:, :HALF])
    acc_ref[:, HALF:] = weighted(upper, back[:, :HALF])
    fifth = [
        tail_ref[j, pl.ds(q, 2 * EXPERTS, stride=8), :].astype(bf16)
        for q in range(8)
        for j in range(PIECE // 128)
    ]
    acc = acc_ref[...] + weighted(last_rows(ranks, gates), jnp.concatenate(fifth, axis=1))
    fetch.wait()
    out_ref[...] = (acc + sum_ref[...]).astype(bf16)


def combine_packed(ids_t, gates_t, base, back):
    return pl.pallas_call(
        combine_packed_kernel,
        out_shape=jax.ShapeDtypeStruct((TOK, D), bf16),
        in_specs=[
            pl.BlockSpec(memory_space=pltpu.VMEM),
            pl.BlockSpec(memory_space=pltpu.VMEM),
            pl.BlockSpec(memory_space=pltpu.HBM),
            pl.BlockSpec(memory_space=pltpu.VMEM),
        ],
        out_specs=pl.BlockSpec(memory_space=pltpu.VMEM),
        scratch_shapes=[
            pltpu.VMEM((TOK, D), f32),
            pltpu.VMEM((PIECE // 128, 2 * EXPERTS * 8, 128), f32),
            pltpu.VMEM((TOK, D), f32),
            pltpu.SemaphoreType.DMA,
        ],
        name="combine_b",
        compiler_params=grant(24),
    )(ids_t, gates_t, in_hbm(base), back)


def shift(axis, k):
    pairs = []
    for x in range(4):
        for y in range(4):
            tx, ty = ((x + k) % 4, y) if axis == "x" else (x, (y + k) % 4)
            pairs.append((x * 4 + y, tx * 4 + ty))
    return pairs


def hop(a, axis, k):
    return lax.ppermute(a, "wide", shift(axis, k))


def gather_row(own, first):
    far = hop(own, first, 2)
    near = [hop(own, first, 1), hop(own, first, -1)]
    return jnp.concatenate([own, *near, far], axis=0)


def gather_rest(row, second):
    ahead, behind = hop(row, second, 1), hop(row, second, -1)
    half = row.shape[0] // 2
    far0, far1 = hop(ahead[:half], second, 1), hop(behind[half:], second, -1)
    return [ahead, behind, far0, far1]


def pack_kernel(lat_ref, rope_ref, out0_ref, out1_ref, sems):
    copies = []
    for pre, out_ref in enumerate((out0_ref, out1_ref)):
        pairs = [(lat_ref.at[0, pre], out_ref.at[pl.ds(0, TOK)])]
        for j in range(4):
            source = rope_ref.at[0, pre, pl.ds(j * 16, 16)]
            pairs.append((source, out_ref.at[pl.ds(TOK, 16), pl.ds(j * TOK, TOK)]))
        for k, (source, target) in enumerate(pairs):
            copy = pltpu.make_async_copy(source, target, sems.at[pre, k])
            copy.start()
            copies.append(copy)
    for copy in copies:
        copy.wait()


def pack_prefixes(latent, rope):
    return pl.pallas_call(
        pack_kernel,
        out_shape=(pltpu.VMEM((BLK, LAT), bf16),) * PREF,
        in_specs=[pl.BlockSpec(memory_space=pltpu.HBM)] * 2,
        out_specs=[pl.BlockSpec(memory_space=pltpu.VMEM)] * 2,
        scratch_shapes=[pltpu.SemaphoreType.DMA((PREF, 5))],
        name="pack",
        compiler_params=grant(8),
    )(in_hbm(latent), in_hbm(rope))


def exchange(a):
    return lax.all_to_all(a, ("req", "wide"), split_axis=0, concat_axis=0, tiled=True)


def layer(
    queries,
    suffix_latent,
    suffix_rope,
    residual,
    prefix_latent,
    prefix_rope,
    suffix_lengths,
    prefix_ids,
    w_ukv,
    w_out,
    norm_gain,
    expert_ids,
    gate_values,
    expert_gate_up,
    expert_down,
):
    scalars = jnp.concatenate([suffix_lengths[0], prefix_ids[0]])
    shard0, shard1 = pack_prefixes(prefix_latent, prefix_rope)
    row0 = gather_row(shard0, "x")
    row1 = gather_row(shard1, "y")
    rest0 = gather_rest(row0, "y")
    rest1 = gather_rest(row1, "x")
    qa, qr = prepare_queries(scalars, queries, w_ukv)
    o_lat = attend(scalars, qa, qr, suffix_latent, suffix_rope, [row0, *rest0], [row1, *rest1])
    ids_t = expert_ids.T
    gates_t = gate_values.T
    hidden, normed, sent_a = project(
        scalars, o_lat, w_ukv, w_out, residual, norm_gain.reshape(1, D), ids_t
    )
    sent_a = sent_a.reshape(2 * EXPERTS, SLOTS_A, D)
    sent_b = dispatch(dispatch_packed_kernel, WIDTH_B, ids_t, normed)
    rows_a = exchange(sent_a)
    rows_b = exchange(sent_b)
    made_a = run_expert(expert_kernel, rows_a, expert_gate_up, expert_down)
    made_b = run_expert(expert_packed_kernel, rows_b, expert_gate_up, expert_down)
    back_a = exchange(made_a)
    back_b = exchange(made_b)
    part = combine(ids_t, gates_t, hidden, back_a)
    return combine_packed(ids_t, gates_t, part, back_b)


def solution(mesh):
    return jax.shard_map(
        layer,
        mesh=mesh,
        in_specs=(
            P(("req", "wide"), None),
            P(("req", "wide"), None),
            P(None, ("req", "wide")),
            P(("req", "wide"), None),
            P("req", None, "wide", None),
            P("req", None, None, "wide"),
            P(("req", "wide"), None),
            P(("req", "wide"), None),
            P(),
            P(),
            P(),
            P(("req", "wide"), None),
            P(("req", "wide"), None),
            P(("req", "wide"), None, None),
            P(("req", "wide"), None, None),
        ),
        out_specs=P(("req", "wide"), None),
        check_vma=False,
    )
```

```python
import jax
import jax.numpy as jnp
from jax import lax
from jax.experimental import pallas as pl
from jax.experimental.pallas import tpu as pltpu
from jax.sharding import PartitionSpec as P


D = 2048
HEADS = 16
NOPE = 128
ROPE = 64
LAT = 512
TOP = 6
PREF = 2
EXPERTS = 64
TOK = 128
REQS = 4
TILE = 16
CAP = 13
SLOTS_A = 8
HALF = D // 2
PIECE = D // 8
WIDTH_B = HALF + PIECE
BLK = 144
EPS = 1e-06
SCALE = 1.0 / (NOPE + ROPE) ** 0.5
LOG2E = 1.4426950408889634
NEG = -1e30
bf16 = jnp.bfloat16
f32 = jnp.float32


def request_scalars(sc_ref):
    lens = [sc_ref[r] for r in range(REQS)]
    own = [sc_ref[REQS + r] for r in range(REQS)]
    starts, total = [], 0
    for r in range(REQS):
        starts.append(total)
        total = total + lens[r]
    zero_count = sum(jnp.where(own[r] == 0, lens[r], 0) for r in range(REQS))
    bases, next0, next1 = [], 0, zero_count
    for r in range(REQS):
        is0 = own[r] == 0
        bases.append(jnp.where(is0, next0, next1))
        next0 = next0 + jnp.where(is0, lens[r], 0)
        next1 = next1 + jnp.where(is0, 0, lens[r])
    return lens, starts, bases, zero_count


def place_of(tokens, starts, bases):
    place = tokens - starts[0] + bases[0]
    for r in range(1, REQS):
        place = jnp.where(tokens >= starts[r], tokens - starts[r] + bases[r], place)
    return place


def sort_matrix(sc_ref, transposed):
    _, starts, bases, _ = request_scalars(sc_ref)
    token_dim = 0 if transposed else 1
    tokens = lax.broadcasted_iota(jnp.int32, (TOK, TOK), token_dim)
    slots = lax.broadcasted_iota(jnp.int32, (TOK, TOK), 1 - token_dim)
    return jnp.where(place_of(tokens, starts, bases) == slots, 1.0, 0.0).astype(bf16)


def grant(mib):
    return pltpu.CompilerParams(vmem_limit_bytes=mib << 20)


def in_hbm(a):
    return pltpu.with_memory_space_constraint(a, pltpu.HBM)


def mm(a, b):
    return jnp.dot(a, b, preferred_element_type=f32)


def mm_nt(a, b):
    return lax.dot_general(a, b, (((1,), (1,)), ((), ())), preferred_element_type=f32)


def mm_tn(a, b):
    return lax.dot_general(a, b, (((0,), (0,)), ((), ())), preferred_element_type=f32)


HG = 4


def query_kernel(sc_ref, q_ref, qr_ref, w_ref, qa_ref, qo_ref):
    order = sort_matrix(sc_ref, False)
    nope = mm(order, q_ref[...]).astype(bf16)
    rope = mm(order, qr_ref[...]).astype(bf16)
    for h in range(HG):
        keys = w_ref[:, h * 256 : h * 256 + 128]
        qa_ref[h] = mm_nt(nope[:, h * 128 : (h + 1) * 128], keys).astype(bf16)
        qo_ref[h] = rope[:, h * ROPE : (h + 1) * ROPE]


def prepare_queries(scalars, queries, w_ukv):
    return pl.pallas_call(
        query_kernel,
        out_shape=(
            jax.ShapeDtypeStruct((HEADS, TOK, LAT), bf16),
            jax.ShapeDtypeStruct((HEADS, TOK, ROPE), bf16),
        ),
        grid_spec=pltpu.PrefetchScalarGridSpec(
            num_scalar_prefetch=1,
            grid=(HEADS // HG,),
            in_specs=[
                pl.BlockSpec((TOK, HG * NOPE), lambda i, s: (0, i)),
                pl.BlockSpec((TOK, HG * ROPE), lambda i, s: (0, HEADS * NOPE // (HG * ROPE) + i)),
                pl.BlockSpec((LAT, HG * 2 * NOPE), lambda i, s: (0, i)),
            ],
            out_specs=[
                pl.BlockSpec((HG, TOK, LAT), lambda i, s: (i, 0, 0)),
                pl.BlockSpec((HG, TOK, ROPE), lambda i, s: (i, 0, 0)),
            ],
        ),
        name="query_prep",
        compiler_params=grant(24),
    )(scalars, queries, queries, w_ukv)


ROWS = HEADS * TILE


def block_views(refs):
    views = []
    for ref in refs:
        for b in range(ref.shape[0] // BLK):
            views.append((ref, b * BLK))
    return views


def unpack_rope(ref, at):
    return jnp.concatenate(
        [ref[at + 128 : at + 144, j * 128 : (j + 1) * 128] for j in range(4)], axis=0
    )


def attention_kernel(n_pieces, sc_ref, qa_ref, qr_ref, ll_ref, lr_ref, *rest):
    pieces = (rest[:n_pieces], rest[n_pieces : 2 * n_pieces])
    o_ref, s_scr, n_scr = rest[2 * n_pieces :]
    lens, starts, bases, zero_count = request_scalars(sc_ref)
    first = pl.program_id(0) * TILE
    c = SCALE * LOG2E

    for pre in range(PREF):
        needed = (first < zero_count) if pre == 0 else (first + TILE > zero_count)

        @pl.when(needed)
        def _(pre=pre):
            q = qa_ref[...].reshape(ROWS, LAT)
            qr = qr_ref[...].reshape(ROWS, ROPE)
            places = first + lax.broadcasted_iota(jnp.int32, (TILE, TOK), 0)
            keys_at = lax.broadcasted_iota(jnp.int32, (TILE, TOK), 1)
            bias = jnp.full((TILE, TOK), NEG, f32)
            for r in range(REQS):
                mine = (places >= bases[r]) & (places < bases[r] + lens[r])
                tok = places - bases[r] + starts[r]
                ok = mine & (keys_at >= starts[r]) & (keys_at <= tok)
                bias = jnp.where(ok, 0.0, bias)
            local_lat = ll_ref[...]
            s = mm_nt(q, local_lat) + mm(qr, lr_ref[...])
            s = (s.reshape(HEADS, TILE, TOK) + bias[None]).reshape(ROWS, TOK)
            n_scr[...] = s
            m = jnp.max(s, axis=1, keepdims=True)
            views = block_views(pieces[pre])
            chunks = [views[k : k + 4] for k in range(0, len(views), 4)]
            for k, chunk in enumerate(chunks):
                lat = jnp.concatenate([ref[at : at + 128, :] for ref, at in chunk], axis=0)
                rope = jnp.concatenate([unpack_rope(ref, at) for ref, at in chunk], axis=1)
                s = mm_nt(q, lat) + mm(qr, rope)
                s_scr[k] = s
                m = jnp.maximum(m, jnp.max(s, axis=1, keepdims=True))
            p = jnp.exp2((n_scr[...] - m) * c)
            total = jnp.sum(p, axis=1, keepdims=True)
            acc = mm(p.astype(bf16), local_lat)
            for k, chunk in enumerate(chunks):
                lat = jnp.concatenate([ref[at : at + 128, :] for ref, at in chunk], axis=0)
                p = jnp.exp2((s_scr[k] - m) * c)
                total = total + jnp.sum(p, axis=1, keepdims=True)
                acc = acc + mm(p.astype(bf16), lat)
            out = (acc / total).astype(bf16).reshape(HEADS, TILE, LAT)
            if pre == 0:
                o_ref[...] = out
            else:
                place = first + lax.broadcasted_iota(jnp.int32, (HEADS, TILE, LAT), 1)
                o_ref[...] = jnp.where(place >= zero_count, out, o_ref[...])


def attend(scalars, qa, qr, local_lat, local_rope, pieces0, pieces1):
    n_pieces = len(pieces0)
    whole = lambda a: pl.BlockSpec(a.shape, lambda i, s: (0,) * a.ndim)
    tiled = lambda width: pl.BlockSpec((HEADS, TILE, width), lambda i, s: (0, i, 0))
    pieces = [*pieces0, *pieces1]
    return pl.pallas_call(
        lambda *refs: attention_kernel(n_pieces, *refs),
        out_shape=jax.ShapeDtypeStruct((HEADS, TOK, LAT), bf16),
        grid_spec=pltpu.PrefetchScalarGridSpec(
            num_scalar_prefetch=1,
            grid=(TOK // TILE,),
            in_specs=[
                tiled(LAT),
                tiled(ROPE),
                whole(local_lat),
                whole(local_rope),
                *[pl.BlockSpec(memory_space=pltpu.VMEM) for _ in pieces],
            ],
            out_specs=tiled(LAT),
            scratch_shapes=[pltpu.VMEM((4, ROWS, 512), f32), pltpu.VMEM((ROWS, TOK), f32)],
        ),
        name="attention",
        compiler_params=grant(24),
    )(scalars, qa, qr, local_lat, local_rope, *pieces)


DG = 32


def project_kernel(
    sc_ref, o_ref, w_ref, wo_ref, res_ref, gain_ref, ids_ref,
    hid_ref, norm_ref, sent_ref, acc_ref, rank_scr, sent_scr, sems,
):
    step = pl.program_id(0)

    @pl.when(step == 0)
    def _():
        acc_ref[...] = res_ref[...].astype(f32)
        rank_scr[...] = rank_table(ids_ref)

    back = sort_matrix(sc_ref, True)
    heads = [mm(o_ref[h], w_ref[:, h * 256 + 128 : h * 256 + 256]).astype(bf16) for h in range(HG)]
    head_out = mm(back, jnp.concatenate(heads, axis=1)).astype(bf16)
    acc_ref[...] += mm(head_out, wo_ref[...])

    @pl.when(step == HEADS // HG - 1)
    def _():
        hidden = acc_ref[...].astype(bf16)
        hid_ref[...] = hidden
        h32 = hidden.astype(f32)
        inverse = lax.rsqrt(jnp.mean(h32 * h32, axis=1, keepdims=True) + EPS)
        norm_ref[...] = (h32 * inverse * gain_ref[...].astype(f32)).astype(bf16)
        copies = []
        for g in range(EXPERTS // DG):
            part = pl.ds(g * DG, DG)
            rows = whole_rows(rank_scr[g * DG : (g + 1) * DG, :], DG, 1).astype(bf16)
            sent = mm(rows, norm_ref[...]).astype(bf16)
            sent_scr[part] = sent.reshape(DG, SLOTS_A, D)
            for half in range(2):
                copy = pltpu.make_async_copy(
                    sent_scr.at[part], sent_ref.at[part, half], sems.at[g, half]
                )
                copy.start()
                copies.append(copy)
        for copy in copies:
            copy.wait()


def project(scalars, o_lat, w_ukv, w_out, residual, gain, ids_t):
    return pl.pallas_call(
        project_kernel,
        out_shape=(
            pltpu.HBM((TOK, D), bf16),
            jax.ShapeDtypeStruct((TOK, D), bf16),
            pltpu.HBM((EXPERTS, 2, SLOTS_A, D), bf16),
        ),
        grid_spec=pltpu.PrefetchScalarGridSpec(
            num_scalar_prefetch=1,
            grid=(HEADS // HG,),
            in_specs=[
                pl.BlockSpec((HG, TOK, LAT), lambda i, s: (i, 0, 0)),
                pl.BlockSpec((LAT, HG * 2 * NOPE), lambda i, s: (0, i)),
                pl.BlockSpec((HG * NOPE, D), lambda i, s: (i, 0)),
                pl.BlockSpec((TOK, D), lambda i, s: (0, 0)),
                pl.BlockSpec((1, D), lambda i, s: (0, 0)),
                pl.BlockSpec((TOP, TOK), lambda i, s: (0, 0)),
            ],
            out_specs=[
                pl.BlockSpec((TOK, D), lambda i, s: (0, 0)),
                pl.BlockSpec((TOK, D), lambda i, s: (0, 0)),
                pl.BlockSpec(memory_space=pltpu.HBM),
            ],
            scratch_shapes=[
                pltpu.VMEM((TOK, D), f32),
                pltpu.VMEM((EXPERTS, TOK), f32),
                pltpu.VMEM((EXPERTS, SLOTS_A, D), bf16),
                pltpu.SemaphoreType.DMA((EXPERTS // DG, 2)),
            ],
        ),
        name="project",
        compiler_params=grant(24),
    )(scalars, o_lat, w_ukv, w_out, residual, gain, ids_t)


def rank_table(ids_ref):
    expert = lax.broadcasted_iota(jnp.int32, (EXPERTS, TOK), 0)
    named = ids_ref[0:1, :] == expert
    for k in range(1, TOP):
        named = named | (ids_ref[k : k + 1, :] == expert)
    earlier = lax.broadcasted_iota(jnp.int32, (TOK, TOK), 0) < lax.broadcasted_iota(
        jnp.int32, (TOK, TOK), 1
    )
    rank = mm(jnp.where(named, 1.0, 0.0).astype(bf16), jnp.where(earlier, 1.0, 0.0).astype(bf16))
    return jnp.where(named, rank, -1.0)


def gate_table(ids_ref, gates_ref):
    expert = lax.broadcasted_iota(jnp.int32, (EXPERTS, TOK), 0)
    gates = jnp.zeros((EXPERTS, TOK), f32)
    for k in range(TOP):
        gates = gates + jnp.where(ids_ref[k : k + 1, :] == expert, gates_ref[k : k + 1, :], 0.0)
    return gates


def whole_rows(ranks, experts, copies, values=None):
    slot = lax.broadcasted_iota(jnp.int32, (SLOTS_A, TOK), 0).astype(f32)
    rows = []
    for e in range(experts):
        on = 1.0 if values is None else values[e : e + 1, :]
        rows += [jnp.where(ranks[e : e + 1, :] == slot, on, 0.0)] * copies
    return jnp.concatenate(rows, axis=0)


def packed_rows(ranks, experts, copies, values=None):
    row = lax.broadcasted_iota(jnp.int32, (8, TOK), 0)
    slot = (SLOTS_A + row // 2).astype(f32)
    even = row % 2 == 0
    lower, upper, last = [], [], []
    for e in range(experts):
        rank = ranks[e : e + 1, :]
        on = 1.0 if values is None else values[e : e + 1, :]
        hit = jnp.where(rank == slot, on, 0.0)
        lower += [jnp.where(even, hit, 0.0)] * copies
        upper += [jnp.where(even, 0.0, hit)] * copies
        last += [jnp.where(jnp.broadcast_to(rank, (8, TOK)) == CAP - 1.0, on, 0.0)] * copies
    return [jnp.concatenate(part, axis=0) for part in (lower, upper, last)]


def pieces_of(last):
    row = lax.broadcasted_iota(jnp.int32, last.shape, 0) % 8
    return [jnp.where(row == q, last, 0.0) for q in range(8)]


EG = 16


def dispatch_packed_kernel(ids_ref, norm_ref, out_ref, rank_scr):
    step = pl.program_id(0)

    @pl.when(step == 0)
    def _():
        rank_scr[...] = rank_table(ids_ref)

    ranks = rank_scr[pl.ds(step * EG, EG), :]
    lower, upper, last = packed_rows(ranks, EG, 1)
    sent = (
        mm(lower.astype(bf16), norm_ref[:, :HALF]) + mm(upper.astype(bf16), norm_ref[:, HALF:])
    ).astype(bf16)
    tail = jnp.zeros((EG * 8, PIECE), f32)
    for q, piece in enumerate(pieces_of(last)):
        tail = tail + mm(piece.astype(bf16), norm_ref[:, q * PIECE : (q + 1) * PIECE])
    tail = tail.astype(bf16)
    for e in range(EG):
        for copy in range(2):
            out_ref[2 * e + copy, :, :HALF] = sent[e * 8 : (e + 1) * 8]
            out_ref[2 * e + copy, :, HALF:] = tail[e * 8 : (e + 1) * 8]


def dispatch(kernel, width, ids_t, normed):
    return pl.pallas_call(
        kernel,
        out_shape=jax.ShapeDtypeStruct((2 * EXPERTS, 8, width), bf16),
        grid=(EXPERTS // EG,),
        in_specs=[
            pl.BlockSpec((TOP, TOK), lambda i: (0, 0)),
            pl.BlockSpec((TOK, D), lambda i: (0, 0)),
        ],
        out_specs=pl.BlockSpec((2 * EG, 8, width), lambda i: (i, 0, 0)),
        scratch_shapes=[pltpu.VMEM((EXPERTS, TOK), f32)],
        compiler_params=grant(32),
    )(ids_t, normed)


def expert_rows(x, wg_ref, wd_ref):
    gate_up = mm(x, wg_ref[0])
    half = gate_up.shape[1] // 2
    gate, up = gate_up[:, :half], gate_up[:, half:]
    act = (gate / (1.0 + jnp.exp(-gate)) * up).astype(bf16)
    return mm(act, wd_ref[0]).astype(bf16)


def expert_kernel(x_ref, wg_ref, wd_ref, out_ref):
    x = x_ref[...].reshape(-1, D)
    out_ref[...] = expert_rows(x, wg_ref, wd_ref).reshape(out_ref.shape)


def select(rows, columns, stride, offset):
    r = lax.broadcasted_iota(jnp.int32, (rows, columns), 0)
    c = lax.broadcasted_iota(jnp.int32, (rows, columns), 1)
    return jnp.where(c == r * stride + offset, 1.0, 0.0).astype(bf16)


def expert_packed_kernel(x_ref, wg_ref, wd_ref, out_ref):
    n = x_ref.shape[0]
    x = x_ref[...].reshape(8 * n, WIDTH_B)
    even, odd = select(4 * n, 8 * n, 2, 0), select(4 * n, 8 * n, 2, 1)
    each = [select(n, 8 * n, 8, q) for q in range(8)]
    main = jnp.concatenate([mm(even, x[:, :HALF]), mm(odd, x[:, :HALF])], axis=1)
    last = jnp.concatenate([mm(pick, x[:, HALF:]) for pick in each], axis=1)
    y = expert_rows(jnp.concatenate([main, last], axis=0).astype(bf16), wg_ref, wd_ref)
    main, last = y[: 4 * n], y[4 * n :]
    out = mm_tn(even, main[:, :HALF]) + mm_tn(odd, main[:, HALF:])
    tail = jnp.zeros((8 * n, PIECE), f32)
    for q, pick in enumerate(each):
        tail = tail + mm_tn(pick, last[:, q * PIECE : (q + 1) * PIECE])
    out_ref[:, :, :HALF] = out.astype(bf16).reshape(n, 8, HALF)
    out_ref[:, :, HALF:] = tail.astype(bf16).reshape(n, 8, PIECE)


def run_expert(kernel, rows, w_gate_up, w_down):
    width = rows.shape[2]
    per = 32
    return pl.pallas_call(
        kernel,
        out_shape=jax.ShapeDtypeStruct(rows.shape, bf16),
        grid=(rows.shape[0] // per,),
        in_specs=[
            pl.BlockSpec((per, 8, width), lambda i: (i, 0, 0)),
            pl.BlockSpec(w_gate_up.shape, lambda i: (0, 0, 0), pipeline_mode=pl.Buffered(1)),
            pl.BlockSpec(w_down.shape, lambda i: (0, 0, 0), pipeline_mode=pl.Buffered(1)),
        ],
        out_specs=pl.BlockSpec((per, 8, width), lambda i: (i, 0, 0)),
        compiler_params=grant(32),
    )(rows, w_gate_up, w_down)


def weighted(weight, back):
    high = weight.astype(bf16)
    low = (weight - high.astype(f32)).astype(bf16)
    both = mm_tn(jnp.concatenate([high, low], axis=1), back)
    return both[:TOK] + both[TOK:]


CG = 16


def combine_kernel(ids_ref, gates_ref, hid_ref, back_ref, out_ref, rank_scr, gate_scr):
    step = pl.program_id(0)

    @pl.when(step == 0)
    def _():
        rank_scr[...] = rank_table(ids_ref)
        gate_scr[...] = gate_table(ids_ref, gates_ref)
        out_ref[...] = hid_ref[...].astype(f32)

    ranks = rank_scr[pl.ds(step * CG, CG), :]
    gates = gate_scr[pl.ds(step * CG, CG), :]
    back = back_ref[...].reshape(2 * CG * SLOTS_A, D)
    out_ref[...] += weighted(whole_rows(ranks, CG, 2, gates), back)


def combine(ids_t, gates_t, hidden, back):
    return pl.pallas_call(
        combine_kernel,
        out_shape=pltpu.HBM((TOK, D), f32),
        grid=(EXPERTS // CG,),
        in_specs=[
            pl.BlockSpec((TOP, TOK), lambda i: (0, 0)),
            pl.BlockSpec((TOP, TOK), lambda i: (0, 0)),
            pl.BlockSpec((TOK, D), lambda i: (0, 0)),
            pl.BlockSpec((2 * CG, 8, D), lambda i: (i, 0, 0)),
        ],
        out_specs=pl.BlockSpec((TOK, D), lambda i: (0, 0)),
        scratch_shapes=[pltpu.VMEM((EXPERTS, TOK), f32), pltpu.VMEM((EXPERTS, TOK), f32)],
        name="combine_a",
        compiler_params=grant(32),
    )(ids_t, gates_t, hidden, back)


def last_rows(ranks, values):
    hit = jnp.where(ranks == CAP - 1.0, values, 0.0)
    return jnp.broadcast_to(hit[:, None, :], (EXPERTS, 2, TOK)).reshape(2 * EXPERTS, TOK)


def combine_packed_kernel(
    ids_ref, gates_ref, sum_hbm, back_ref, out_ref, acc_ref, tail_ref, sum_ref, sem
):
    fetch = pltpu.make_async_copy(sum_hbm, sum_ref, sem)
    fetch.start()
    ranks = rank_table(ids_ref)
    gates = gate_table(ids_ref, gates_ref)
    back = back_ref[...].reshape(2 * EXPERTS * 8, WIDTH_B)
    for j in range(PIECE // 128):
        tail_ref[j] = back[:, HALF + j * 128 : HALF + (j + 1) * 128].astype(f32)
    lower, upper = packed_rows(ranks, EXPERTS, 2, gates)[:2]
    acc_ref[:, :HALF] = weighted(lower, back[:, :HALF])
    acc_ref[:, HALF:] = weighted(upper, back[:, :HALF])
    fifth = [
        tail_ref[j, pl.ds(q, 2 * EXPERTS, stride=8), :].astype(bf16)
        for q in range(8)
        for j in range(PIECE // 128)
    ]
    acc = acc_ref[...] + weighted(last_rows(ranks, gates), jnp.concatenate(fifth, axis=1))
    fetch.wait()
    out_ref[...] = (acc + sum_ref[...]).astype(bf16)


def combine_packed(ids_t, gates_t, base, back):
    return pl.pallas_call(
        combine_packed_kernel,
        out_shape=jax.ShapeDtypeStruct((TOK, D), bf16),
        in_specs=[
            pl.BlockSpec(memory_space=pltpu.VMEM),
            pl.BlockSpec(memory_space=pltpu.VMEM),
            pl.BlockSpec(memory_space=pltpu.HBM),
            pl.BlockSpec(memory_space=pltpu.VMEM),
        ],
        out_specs=pl.BlockSpec(memory_space=pltpu.VMEM),
        scratch_shapes=[
            pltpu.VMEM((TOK, D), f32),
            pltpu.VMEM((PIECE // 128, 2 * EXPERTS * 8, 128), f32),
            pltpu.VMEM((TOK, D), f32),
            pltpu.SemaphoreType.DMA,
        ],
        name="combine_b",
        compiler_params=grant(24),
    )(ids_t, gates_t, in_hbm(base), back)


def shift(axis, k):
    pairs = []
    for x in range(4):
        for y in range(4):
            tx, ty = ((x + k) % 4, y) if axis == "x" else (x, (y + k) % 4)
            pairs.append((x * 4 + y, tx * 4 + ty))
    return pairs


def hop(a, axis, k):
    return lax.ppermute(a, "wide", shift(axis, k))


def gather_row(own, first):
    far = hop(own, first, 2)
    near = [hop(own, first, 1), hop(own, first, -1)]
    return jnp.concatenate([own, *near, far], axis=0)


def gather_rest(row, second):
    ahead, behind = hop(row, second, 1), hop(row, second, -1)
    far = hop(row, second, 2)
    return [ahead, behind, far]


def pack_kernel(lat_ref, rope_ref, out0_ref, out1_ref, sems):
    copies = []
    for pre, out_ref in enumerate((out0_ref, out1_ref)):
        pairs = [(lat_ref.at[0, pre], out_ref.at[pl.ds(0, TOK)])]
        for j in range(4):
            source = rope_ref.at[0, pre, pl.ds(j * 16, 16)]
            pairs.append((source, out_ref.at[pl.ds(TOK, 16), pl.ds(j * TOK, TOK)]))
        for k, (source, target) in enumerate(pairs):
            copy = pltpu.make_async_copy(source, target, sems.at[pre, k])
            copy.start()
            copies.append(copy)
    for copy in copies:
        copy.wait()


def pack_prefixes(latent, rope):
    return pl.pallas_call(
        pack_kernel,
        out_shape=(pltpu.VMEM((BLK, LAT), bf16),) * PREF,
        in_specs=[pl.BlockSpec(memory_space=pltpu.HBM)] * 2,
        out_specs=[pl.BlockSpec(memory_space=pltpu.VMEM)] * 2,
        scratch_shapes=[pltpu.SemaphoreType.DMA((PREF, 5))],
        name="pack",
        compiler_params=grant(8),
    )(in_hbm(latent), in_hbm(rope))


def exchange(a):
    return lax.all_to_all(a, ("req", "wide"), split_axis=0, concat_axis=0, tiled=True)


def layer(
    queries,
    suffix_latent,
    suffix_rope,
    residual,
    prefix_latent,
    prefix_rope,
    suffix_lengths,
    prefix_ids,
    w_ukv,
    w_out,
    norm_gain,
    expert_ids,
    gate_values,
    expert_gate_up,
    expert_down,
):
    scalars = jnp.concatenate([suffix_lengths[0], prefix_ids[0]])
    shard0, shard1 = pack_prefixes(prefix_latent, prefix_rope)
    row0 = gather_row(shard0, "x")
    row1 = gather_row(shard1, "y")
    rest0 = gather_rest(row0, "y")
    rest1 = gather_rest(row1, "x")
    qa, qr = prepare_queries(scalars, queries, w_ukv)
    o_lat = attend(scalars, qa, qr, suffix_latent, suffix_rope, [row0, *rest0], [row1, *rest1])
    ids_t = expert_ids.T
    gates_t = gate_values.T
    hidden, normed, sent_a = project(
        scalars, o_lat, w_ukv, w_out, residual, norm_gain.reshape(1, D), ids_t
    )
    sent_a = sent_a.reshape(2 * EXPERTS, SLOTS_A, D)
    sent_b = dispatch(dispatch_packed_kernel, WIDTH_B, ids_t, normed)
    rows_a = exchange(sent_a)
    rows_b = exchange(sent_b)
    made_a = run_expert(expert_kernel, rows_a, expert_gate_up, expert_down)
    made_b = run_expert(expert_packed_kernel, rows_b, expert_gate_up, expert_down)
    back_a = exchange(made_a)
    back_b = exchange(made_b)
    part = combine(ids_t, gates_t, hidden, back_a)
    return combine_packed(ids_t, gates_t, part, back_b)


def solution(mesh):
    return jax.shard_map(
        layer,
        mesh=mesh,
        in_specs=(
            P(("req", "wide"), None),
            P(("req", "wide"), None),
            P(None, ("req", "wide")),
            P(("req", "wide"), None),
            P("req", None, "wide", None),
            P("req", None, None, "wide"),
            P(("req", "wide"), None),
            P(("req", "wide"), None),
            P(),
            P(),
            P(),
            P(("req", "wide"), None),
            P(("req", "wide"), None),
            P(("req", "wide"), None, None),
            P(("req", "wide"), None, None),
        ),
        out_specs=P(("req", "wide"), None),
        check_vma=False,
    )
```
